32 devices in a mesh: expert: 16 (over z, y, x), dp: 2 (over core).
Axes of the slice: x: 2, y: 2, z: 4, core: 2. Of those that a mesh axis runs over, the one named last changes fastest.
Arguments:
- block_input: float32 [16384, 768], P(('expert', 'dp')), may hold values from -6 to 6
- cotangent: float32 [16384, 768], P(('expert', 'dp')), may hold values from -6 to 6
- segment_ids: int32 [32, 512], P(('expert', 'dp')), may hold values from 0 to 7, never falling along the last dimension, each value on 1 to 256 neighbouring positions
- routes: int32 [16384, 2], P(('expert', 'dp')), may hold values from 0 to 15, as said below
- slot_ids: int32 [16384, 2], P(('expert', 'dp')), may hold values from 0 to 127, as said below
- attention_in: bfloat16 [768, 2304], P('dp'), may hold values from -0.21875 to 0.21875
- attention_out: bfloat16 [768, 768], P('dp'), may hold values from -1.25 to 1.25
- router_weight: bfloat16 [768, 16], P('dp'), may hold values from -0.21875 to 0.21875
- first_gain: bfloat16 [768], P('dp'), may hold values from 0.099609375 to 1.8984375
- second_gain: bfloat16 [768], P('dp'), may hold values from 0.099609375 to 1.8984375
- bias_table: bfloat16 [32, 12], P('dp'), may hold values from -4 to 302
- expert_up: bfloat16 [16, 768, 3072], P('expert'), may hold values from -0.21875 to 0.21875
- expert_down: bfloat16 [16, 3072, 768], P('expert'), may hold values from -0.109375 to 0.109375
Outputs:
- block_output: float32 [16384, 768], P(('expert', 'dp'))
- input_grad: float32 [16384, 768], P(('expert', 'dp'))
- gradient_in: float32 [768, 2304], P('dp')
- gradient_out: float32 [768, 768], P('dp')
- gradient_router: float32 [768, 16], P('dp')
- gradient_first: float32 [768], P('dp')
- gradient_second: float32 [768], P('dp')
- gradient_bias: float32 [32, 12], P('dp')
- gradient_up: float32 [16, 768, 3072], P('expert', None, 'dp')
- gradient_down: float32 [16, 3072, 768], P('expert', 'dp')
The draws below stay inside these ranges and needn't reach their ends.
Inputs may be any that keep to these rules, and one draw needn't show every extreme that they name: `routes`: the two experts of a row differ. Among the rows of one sequence no expert is named more than 128 times, and one expert, the same in every sequence, is named exactly 128 times. `slot_ids`: within one sequence, the slots of the rows naming one expert are distinct and are 0 up to the number of those rows - 1.
All inputs are finite; a program needn't handle non-finite values.
Results may differ from the reference program's by a relative error of at most 0.014.
Values may be sent and summed in bfloat16 or wider, within the bound.
A program may use at most 320 MiB of HBM per device.

```python
import math
import jax
import jax.numpy as jnp
import numpy as np
from jax import lax

D = 768
H = 12
HD = 64
F = 3072
NB = 32
SEQ = 512
EXPERTS = 16
SEQS = 32
TOKENS = 16384
CAP = 128


def plan_routes(key):
    base_key = jax.random.fold_in(key, 11)
    popular = jax.random.randint(jax.random.fold_in(base_key, 1), (), 0, EXPERTS)
    tickets = EXPERTS * CAP
    wanted = 2 * SEQ - CAP
    ticket_ids = jnp.arange(tickets, dtype=jnp.int32)
    ticket_expert = ticket_ids // CAP
    ticket_slot = ticket_ids % CAP

    def one_sequence(seq_key):
        key_weight, key_noise, key_shuffle, key_reverse = jax.random.split(seq_key, 4)
        weights = jax.random.randint(key_weight, (EXPERTS,), 1, 9)
        ticket_weight = weights[ticket_expert]
        jitter = jax.random.randint(key_noise, (tickets,), 0, 8) % ticket_weight
        scores = ticket_slot * ticket_weight + jitter
        scores = jnp.where(ticket_expert == popular, 8192, scores)
        ranked = jnp.argsort(scores * 16384 + ticket_ids)
        rank_of = jnp.zeros((tickets,), jnp.int32).at[ranked].set(ticket_ids)
        keyed_order = jnp.where(rank_of < wanted, 0, 1) * tickets + ticket_ids
        chosen = jnp.argsort(keyed_order)[:wanted]
        chosen_expert = chosen // CAP
        chosen_slot = chosen % CAP
        leading = jnp.arange(CAP, dtype=jnp.int32)
        first_expert = jnp.concatenate([jnp.full((CAP,), popular, jnp.int32), chosen_expert[:SEQ - CAP]])
        first_slot = jnp.concatenate([leading, chosen_slot[:SEQ - CAP]])
        second_expert = chosen_expert[SEQ - CAP:]
        second_slot = chosen_slot[SEQ - CAP:]
        pair_expert = jnp.stack([first_expert, second_expert], axis=1)
        pair_slot = jnp.stack([first_slot, second_slot], axis=1)
        reverse_pair = jax.random.randint(key_reverse, (SEQ,), 0, 2)
        pair_expert = jnp.where(reverse_pair[:, None] == 1, pair_expert[:, ::-1], pair_expert)
        pair_slot = jnp.where(reverse_pair[:, None] == 1, pair_slot[:, ::-1], pair_slot)
        shuffle = jax.random.permutation(key_shuffle, SEQ)
        return (pair_expert[shuffle], pair_slot[shuffle])
    seq_keys = jax.random.split(jax.random.fold_in(base_key, 2), SEQS)
    experts_drawn, slots_drawn = jax.vmap(one_sequence)(seq_keys)
    return (experts_drawn.reshape(TOKENS, 2).astype(jnp.int32), slots_drawn.reshape(TOKENS, 2).astype(jnp.int32))


def draw_routes(key, part):
    return plan_routes(key)[0]


def draw_slot_ids(key, part):
    return plan_routes(key)[1]


def draw_bias_table(key, part):
    return jnp.clip(jax.random.normal(jax.random.fold_in(key, 4), (NB, H), jnp.float32), -4.0, 4.0).astype(jnp.bfloat16)


def steps_of(key, extent, cuts, smallest, high):
    loudness, own = 1.0, jax.random.fold_in(key, 6)
    for position, shards_of in cuts:
        draws = jnp.exp(jax.random.uniform(jax.random.fold_in(own, position), (shards_of,), jnp.float32, smallest / len(cuts), high / len(cuts)))
        loudness = loudness * jnp.repeat(draws, extent[position] // shards_of).reshape([-1 if axis == position else 1 for axis in range(len(extent))])
    return loudness


def profile(amount, total, limit, skew):
    loads = [(1 << 20) // math.isqrt(standing ** skew) + 1 for standing in range(2, amount + 1)]
    rest, given = total - limit - (amount - 1), [1] * (amount - 1)
    while rest > 0:
        candidates = [i for i in range(amount - 1) if given[i] < limit]
        pool, budget = sum([loads[i] for i in candidates]), rest
        for i in candidates:
            extra = min(limit - given[i], max(1, budget * loads[i] // pool), rest)
            given[i] = given[i] + extra
            rest = rest - extra
    return np.array([limit] + given)


def uneven(stream_key, number_of, total, bound, lean):
    if number_of == 2:
        one = jax.random.randint(stream_key, (), max(1, total - bound), min(bound, total - 1) + 1)
        return jnp.stack([one, total - one])
    sizes = jnp.asarray(profile(number_of, total, bound, lean), jnp.int32)
    couples = (number_of - 1) // 2
    giver, receiver = sizes[1:1 + 2 * couples:2], sizes[2:2 + 2 * couples:2]
    margin = jnp.minimum(giver - 1, bound - receiver)
    shifted = jax.random.randint(jax.random.fold_in(stream_key, 1), (couples,), 0, 1 << 20) % (margin + 1)
    sizes = sizes.at[1:1 + 2 * couples:2].set(giver - shifted).at[2:2 + 2 * couples:2].set(receiver + shifted)
    return sizes[jax.random.permutation(jax.random.fold_in(stream_key, 2), number_of)]


def scatter_about(stream_key, shape, scale, reach, cuts=(), kind=jnp.bfloat16):
    result = jax.random.normal(stream_key, shape, jnp.float32) * scale
    if len(cuts) > 0:
        result = steps_of(stream_key, shape, cuts, -0.22, 0.18) * result
    return jnp.clip(result, min=-reach, max=reach).astype(kind)


def setup_inputs(seed: int = 0) -> dict:
    key_of = jax.random.split(jax.random.key(seed), 14)
    return {
        "block_input": scatter_about(key_of[0], (TOKENS, D), 1.0, 6.0, ((0, 32),), jnp.float32),
        "cotangent": scatter_about(key_of[1], (TOKENS, D), 1.0, 6.0, ((0, 32),), jnp.float32),
        "segment_ids": jax.vmap(lambda own: jnp.searchsorted(jnp.cumsum(uneven(own, max(4, SEQ // 64), SEQ, SEQ // 2, 2)), jnp.arange(SEQ), side="right"))(jax.random.split(key_of[2], SEQS)).reshape((SEQS, SEQ)).astype(jnp.int32),
        "routes": draw_routes(jax.random.fold_in(key_of[13], 71), 0),
        "slot_ids": draw_slot_ids(jax.random.fold_in(key_of[13], 71), 0),
        "attention_in": scatter_about(key_of[5], (D, 3 * D), D ** -0.5, 0.21875, ((0, 2),)),
        "attention_out": scatter_about(key_of[6], (D, D), (D // 32) ** -0.5, 1.25, ((0, 2),)),
        "router_weight": scatter_about(key_of[7], (D, EXPERTS), D ** -0.5, 0.21875, ((0, 2),)),
        "first_gain": jnp.clip(1.0 + 0.18 * jax.random.normal(key_of[8], (D,), jnp.float32), 0.099609375, 1.8984375).astype(jnp.bfloat16),
        "second_gain": jnp.clip(1.0 + 0.18 * jax.random.normal(key_of[9], (D,), jnp.float32), 0.099609375, 1.8984375).astype(jnp.bfloat16),
        "bias_table": draw_bias_table(jax.random.fold_in(key_of[13], 71), 0),
        "expert_up": scatter_about(key_of[11], (EXPERTS, D, F), D ** -0.5, 0.21875, ((0, 16),)),
        "expert_down": scatter_about(key_of[12], (EXPERTS, F, D), F ** -0.5, 0.109375, ((0, 16),)),
    }


EPS = 1e-06

def reach_marks(buckets, reach_len):
    half_count = buckets // 2
    step_ids = np.arange(1, half_count)
    thresholds = np.floor(half_count * (reach_len / half_count) ** (step_ids / half_count))
    thresholds = np.maximum(thresholds, half_count + step_ids)
    return thresholds.astype(np.int32)

def bucket_of(distance, buckets, reach_len):
    half_count = buckets // 2
    thresholds = jnp.asarray(reach_marks(buckets, reach_len), dtype=jnp.int32)
    counted = lax.optimization_barrier(jnp.sum((distance[..., None] >= thresholds).astype(jnp.int32), axis=-1))
    return jnp.minimum(distance, half_count) + counted

def normal_cdf(argument):
    return 0.5 * (1.0 + jax.scipy.special.erf(argument * (1.0 / math.sqrt(2.0))))

def gelu_slope(argument):
    return normal_cdf(argument) + argument * (jnp.exp(-0.5 * argument * argument) * (1.0 / math.sqrt(2.0 * math.pi)))

def widen(narrow):
    return lax.optimization_barrier(narrow).astype(jnp.float32)

def attend(seq_input, seq_segments, attention_in, first_gain, bias_values):
    rms_one = lax.rsqrt(lax.optimization_barrier(jnp.mean(seq_input * seq_input, axis=1, keepdims=True)) + EPS)
    normal_one = seq_input * rms_one
    normed_one = (normal_one * first_gain.astype(jnp.float32)).astype(jnp.bfloat16)
    triple = jnp.dot(normed_one, attention_in, preferred_element_type=jnp.float32).astype(jnp.bfloat16)
    wide_triple = widen(triple)
    queries = wide_triple[:, :D].reshape(SEQ, H, HD)
    keys_all = wide_triple[:, D:2 * D].reshape(SEQ, H, HD)
    values_all = wide_triple[:, 2 * D:].reshape(SEQ, H, HD)
    positions = jnp.arange(SEQ, dtype=jnp.int32)
    distance = positions[:, None] - positions[None, :]
    allowed = (distance >= 0) & (seq_segments[:, None] == seq_segments[None, :])
    bucket_ids = bucket_of(jnp.maximum(distance, 0), NB, SEQ)
    bias_full = jnp.transpose(jnp.take(bias_values, bucket_ids, axis=0), (2, 0, 1))
    scores = jnp.einsum('ihd,jhd->hij', queries, keys_all) * (1.0 / math.sqrt(HD)) + bias_full
    scores = jnp.where(allowed[None], scores, -jnp.inf)
    row_top = lax.optimization_barrier(jnp.max(scores, axis=2, keepdims=True))
    log_total = row_top + jnp.log(lax.optimization_barrier(jnp.sum(jnp.exp(scores - row_top), axis=2, keepdims=True)))
    prob_full = jnp.exp(scores - log_total)
    prob_half = prob_full.astype(jnp.bfloat16)
    context = jnp.einsum('hij,jhd->ihd', widen(prob_half), values_all).astype(jnp.bfloat16).reshape(SEQ, D)
    return (rms_one, normal_one, normed_one, queries, keys_all, values_all, bucket_ids, prob_full, prob_half, context)

def reference(block_input, cotangent, segment_ids, routes, slot_ids, attention_in, attention_out, router_weight, first_gain, second_gain, bias_table, expert_up, expert_down):
    bias_values = bias_table.astype(jnp.float32)
    inputs_seq = block_input.reshape(SEQS, SEQ, D)

    def forward_seq(packed):
        seq_input, seq_segments = packed
        pieces = attend(seq_input, seq_segments, attention_in, first_gain, bias_values)
        return seq_input + jnp.dot(pieces[9], attention_out, preferred_element_type=jnp.float32)
    hidden_state = lax.map(forward_seq, (inputs_seq, segment_ids)).reshape(TOKENS, D)
    rms_two = lax.rsqrt(lax.optimization_barrier(jnp.mean(hidden_state * hidden_state, axis=1, keepdims=True)) + EPS)
    normal_two = hidden_state * rms_two
    normed_two = (normal_two * second_gain.astype(jnp.float32)).astype(jnp.bfloat16)
    logits = jnp.dot(normed_two, router_weight, preferred_element_type=jnp.float32)
    expert_ids = jnp.arange(EXPERTS, dtype=jnp.int32)
    pick_first = (routes[:, 0:1] == expert_ids[None, :]).astype(jnp.float32)
    pick_second = (routes[:, 1:2] == expert_ids[None, :]).astype(jnp.float32)
    logit_first = lax.optimization_barrier(jnp.sum(logits * pick_first, axis=1))
    logit_second = lax.optimization_barrier(jnp.sum(logits * pick_second, axis=1))
    gate_first = jax.nn.sigmoid(logit_first - logit_second)
    gate_second = jax.nn.sigmoid(logit_second - logit_first)
    gate_pair = jnp.stack([gate_first, gate_second], axis=1)
    token_ids = jnp.arange(TOKENS, dtype=jnp.int32)
    seq_of = token_ids // SEQ
    slot_place = routes * (SEQS * CAP) + seq_of[:, None] * CAP + slot_ids
    assign_ids = jnp.arange(2 * TOKENS, dtype=jnp.int32)
    slot_owner = jnp.full((EXPERTS * SEQS * CAP,), 2 * TOKENS, jnp.int32).at[slot_place.reshape(-1)].set(assign_ids)
    slot_owner = slot_owner.reshape(EXPERTS, SEQS * CAP)
    normed_pad = jnp.concatenate([normed_two, jnp.zeros((1, D), jnp.bfloat16)], axis=0)
    gate_pad = jnp.concatenate([gate_pair.reshape(-1), jnp.zeros((1,), jnp.float32)], axis=0)
    cot_pad = jnp.concatenate([cotangent, jnp.zeros((1, D), jnp.float32)], axis=0)

    def expert_step(carry, packed):
        mixture, gate_grad, normed_grad = carry
        assigned, up_matrix, down_matrix = packed
        slot_token = assigned // 2
        rows_in = jnp.take(normed_pad, slot_token, axis=0)
        expert_pre = jnp.dot(rows_in, up_matrix, preferred_element_type=jnp.float32)
        activation = (expert_pre * normal_cdf(expert_pre)).astype(jnp.bfloat16)
        out_rows = jnp.dot(activation, down_matrix, preferred_element_type=jnp.float32).astype(jnp.bfloat16)
        out_wide = out_rows.astype(jnp.float32)
        slot_gate = jnp.take(gate_pad, assigned)
        cot_rows = jnp.take(cot_pad, slot_token, axis=0)
        mixture = mixture.at[slot_token].add(slot_gate[:, None] * out_wide, mode='drop')
        gate_grad = gate_grad.at[assigned].add(lax.optimization_barrier(jnp.sum(cot_rows * out_wide, axis=1)), mode='drop')
        out_cot = (slot_gate[:, None] * cot_rows).astype(jnp.bfloat16)
        act_grad = jnp.dot(out_cot, down_matrix.T, preferred_element_type=jnp.float32)
        pre_grad = (act_grad * gelu_slope(expert_pre)).astype(jnp.bfloat16)
        grad_down = jnp.dot(activation.T, out_cot, preferred_element_type=jnp.float32)
        grad_up = jnp.dot(rows_in.T, pre_grad, preferred_element_type=jnp.float32)
        back_rows = jnp.dot(pre_grad, up_matrix.T, preferred_element_type=jnp.float32).astype(jnp.bfloat16)
        normed_grad = normed_grad.at[slot_token].add(back_rows.astype(jnp.float32), mode='drop')
        return ((mixture, gate_grad, normed_grad), (grad_up, grad_down))
    start_carry = (jnp.zeros((TOKENS, D), jnp.float32), jnp.zeros((2 * TOKENS,), jnp.float32), jnp.zeros((TOKENS, D), jnp.float32))
    (mixture, gate_grad, normed_grad), (gradient_up, gradient_down) = lax.scan(expert_step, start_carry, (slot_owner, expert_up, expert_down))
    gate_grad = gate_grad.reshape(TOKENS, 2)
    block_output = hidden_state + mixture
    logit_delta = gate_first * gate_second * (gate_grad[:, 0] - gate_grad[:, 1])
    logit_grad = (pick_first * logit_delta[:, None] - pick_second * logit_delta[:, None]).astype(jnp.bfloat16)
    normed_grad = normed_grad + jnp.dot(logit_grad, router_weight.T, preferred_element_type=jnp.float32)
    gradient_router = jnp.dot(normed_two.T, logit_grad, preferred_element_type=jnp.float32)
    gradient_second = lax.optimization_barrier(jnp.sum(normed_grad * normal_two, axis=0))
    scaled_two = normed_grad * second_gain.astype(jnp.float32)
    hidden_grad = cotangent + (rms_two * scaled_two - hidden_state * (rms_two * rms_two * rms_two) * lax.optimization_barrier(jnp.mean(scaled_two * hidden_state, axis=1, keepdims=True)))
    bucket_range = jnp.arange(NB, dtype=jnp.int32)
    score_scale = 1.0 / math.sqrt(HD)

    def backward_seq(carry, packed):
        grad_in, grad_out, grad_first, grad_bias = carry
        seq_input, seq_segments, seq_hidden_grad = packed
        rms_one, normal_one, normed_one, queries, keys_all, values_all, bucket_ids, prob_full, prob_half, context = attend(seq_input, seq_segments, attention_in, first_gain, bias_values)
        residual_cot = seq_hidden_grad.astype(jnp.bfloat16)
        grad_out = grad_out + jnp.dot(context.T, residual_cot, preferred_element_type=jnp.float32)
        context_grad = jnp.dot(residual_cot, attention_out.T, preferred_element_type=jnp.float32).astype(jnp.bfloat16)
        context_wide = widen(context_grad).reshape(SEQ, H, HD)
        prob_grad = jnp.einsum('ihd,jhd->hij', context_wide, values_all)
        row_dot = lax.optimization_barrier(jnp.sum(prob_full * prob_grad, axis=2, keepdims=True))
        score_grad = prob_full * (prob_grad - row_dot)
        bucket_hot = (bucket_ids[..., None] == bucket_range).astype(jnp.float32)
        grad_bias = grad_bias + jnp.einsum('hij,ijb->bh', score_grad, bucket_hot, precision=lax.Precision.HIGHEST)
        score_wide = widen(score_grad.astype(jnp.bfloat16))
        query_grad = jnp.einsum('hij,jhd->ihd', score_wide, keys_all) * score_scale
        key_grad = jnp.einsum('hij,ihd->jhd', score_wide, queries) * score_scale
        value_grad = jnp.einsum('hij,ihd->jhd', widen(prob_half), context_wide)
        triple_grad = jnp.concatenate([query_grad.reshape(SEQ, D), key_grad.reshape(SEQ, D), value_grad.reshape(SEQ, D)], axis=1).astype(jnp.bfloat16)
        grad_in = grad_in + jnp.dot(normed_one.T, triple_grad, preferred_element_type=jnp.float32)
        normed_one_grad = jnp.dot(triple_grad, attention_in.T, preferred_element_type=jnp.float32)
        grad_first = grad_first + lax.optimization_barrier(jnp.sum(normed_one_grad * normal_one, axis=0))
        scaled_one = normed_one_grad * first_gain.astype(jnp.float32)
        seq_grad = seq_hidden_grad + (rms_one * scaled_one - seq_input * (rms_one * rms_one * rms_one) * lax.optimization_barrier(jnp.mean(scaled_one * seq_input, axis=1, keepdims=True)))
        return ((grad_in, grad_out, grad_first, grad_bias), seq_grad)
    start_grads = (jnp.zeros((D, 3 * D), jnp.float32), jnp.zeros((D, D), jnp.float32), jnp.zeros((D,), jnp.float32), jnp.zeros((NB, H), jnp.float32))
    (gradient_in, gradient_out, gradient_first, gradient_bias), input_grad = lax.scan(backward_seq, start_grads, (inputs_seq, segment_ids, hidden_grad.reshape(SEQS, SEQ, D)))
    input_grad = input_grad.reshape(TOKENS, D)
    return (block_output, input_grad, gradient_in, gradient_out, gradient_router, gradient_first, gradient_second, gradient_bias, gradient_up, gradient_down)
```

```python
import functools
import math

import jax
import jax.numpy as jnp
import numpy as np
from jax import lax
from jax.experimental import pallas as pl
from jax.experimental.pallas import tpu as pltpu
from jax.sharding import PartitionSpec as P

EPS = 1e-06
F32 = jnp.float32
BF16 = jnp.bfloat16
BLOCK = 128
MASKED = -1e30


def reach_marks(buckets, reach_len):
    half_count = buckets // 2
    step_ids = np.arange(1, half_count)
    thresholds = np.floor(half_count * (reach_len / half_count) ** (step_ids / half_count))
    thresholds = np.maximum(thresholds, half_count + step_ids)
    return [int(mark) for mark in thresholds.astype(np.int32)]


def normal_cdf(argument):
    return 0.5 * (1.0 + jax.scipy.special.erf(argument * (1.0 / math.sqrt(2.0))))


def gelu_slope(argument):
    return normal_cdf(argument) + argument * (
        jnp.exp(-0.5 * argument * argument) * (1.0 / math.sqrt(2.0 * math.pi))
    )


def dot(left, right, left_dim=1, right_dim=0):
    return lax.dot_general(
        left, right, (((left_dim,), (right_dim,)), ((), ())), preferred_element_type=F32
    )


def bucket_hot(buckets, length, width):
    column = lax.broadcasted_iota(jnp.int32, (1, width), 1)
    distance = jnp.maximum(length // 2 + BLOCK - 1 - column, 0)
    bucket = jnp.minimum(distance, buckets // 2)
    for mark in reach_marks(buckets, length):
        bucket = bucket + jnp.where(distance >= mark, 1, 0)
    rows = lax.broadcasted_iota(jnp.int32, (buckets, width), 0)
    return jnp.where(rows == bucket, 1.0, 0.0)


def spans(length):
    reach = length // 2
    for block in range(length // BLOCK):
        low = max(0, block * BLOCK - reach)
        high = (block + 1) * BLOCK
        yield block, low, high, reach + BLOCK - (high - low)


def halves(pair):
    lane = lax.broadcasted_iota(jnp.int32, (1, pair.shape[1]), 1)
    first = lane < pair.shape[1] // 2
    zero = jnp.zeros_like(pair)
    return jnp.where(first, pair, zero), jnp.where(first, zero, pair)


def forward_kernel(
    x_ref, segment_ref, route_ref, in_ref, out_ref, router_ref, gain_ref, bias_ref,
    hidden_ref, normed_ref, triple_ref, context_ref, prob_ref, gate_ref,
    table_ref, mask_ref, one_ref,
):
    length, width = x_ref.shape
    heads, buckets = bias_ref.shape
    pair = 2 * (width // heads)
    pairs = heads // 2
    reach = length // 2
    span = reach + BLOCK
    scale = 1.0 / math.sqrt(width // heads)

    x = x_ref[...]
    rms = lax.rsqrt(jnp.mean(x * x, axis=1, keepdims=True) + EPS)
    one_ref[...] = (x * rms * gain_ref[0:1, :].astype(F32)).astype(BF16)

    chunk = 3 * pair

    def project(step, carry):
        columns = pl.ds(pl.multiple_of(step * chunk, BLOCK), chunk)
        triple_ref[:, columns] = dot(one_ref[...], in_ref[:, columns]).astype(BF16)
        return carry

    lax.fori_loop(0, 3 * width // chunk, project, 0)

    wide = span + BLOCK
    by_column = dot(bias_ref[...], bucket_hot(buckets, length, wide).astype(BF16))
    for head in range(heads):
        spread = jnp.broadcast_to(by_column[head : head + 1, :], (BLOCK, wide))
        rolled = pltpu.roll(spread, wide - BLOCK + 1, 1, stride=1, stride_axis=0)
        table_ref[head // 2, (head % 2) * BLOCK : (head % 2 + 1) * BLOCK, :] = rolled[:, :span]

    segment_row = segment_ref[...].astype(F32)
    segment_column = jnp.transpose(jnp.broadcast_to(segment_row, (BLOCK, length)))
    for block, low, high, skip in spans(length):
        rows = block * BLOCK + lax.broadcasted_iota(jnp.int32, (BLOCK, high - low), 0)
        columns = low + lax.broadcasted_iota(jnp.int32, (BLOCK, high - low), 1)
        own = segment_column[block * BLOCK : (block + 1) * BLOCK, 0:1]
        allowed = (rows >= columns) & (own == segment_row[:, low:high])
        mask_ref[block, :, skip:] = jnp.where(allowed, 0.0, MASKED)

    def attend(step, carry):
        base = pl.multiple_of(step * pair, pair)
        query_columns = pl.ds(base, pair)
        key_columns = pl.ds(pl.multiple_of(width + base, pair), pair)
        value_columns = pl.ds(pl.multiple_of(2 * width + base, pair), pair)
        for block, low, high, skip in spans(length):
            rows = slice(block * BLOCK, (block + 1) * BLOCK)
            query = triple_ref[rows, query_columns] * jnp.asarray(scale, BF16)
            stacked = jnp.concatenate(halves(query), axis=0)
            scores = dot(stacked, triple_ref[low:high, key_columns], 1, 1)
            mask = mask_ref[block, :, skip:]
            scores = scores + table_ref[step, :, skip:] + jnp.concatenate([mask, mask], axis=0)
            top = jnp.max(scores, axis=1, keepdims=True)
            weight = jnp.exp(scores - top)
            prob = weight * (1.0 / jnp.sum(weight, axis=1, keepdims=True))
            half = prob.astype(BF16)
            prob_ref[step, block, :, skip:] = half
            first, second = halves(triple_ref[low:high, value_columns])
            context = dot(half[:BLOCK], first) + dot(half[BLOCK:], second)
            context_ref[rows, query_columns] = context.astype(BF16)
        return carry

    lax.fori_loop(0, pairs, attend, 0)

    hidden = x_ref[...] + dot(context_ref[...], out_ref[...])
    hidden_ref[...] = hidden
    rms = lax.rsqrt(jnp.mean(hidden * hidden, axis=1, keepdims=True) + EPS)
    normed = (hidden * rms * gain_ref[1:2, :].astype(F32)).astype(BF16)
    normed_ref[...] = normed
    logits = dot(router_ref[...], normed, 1, 1)
    expert_ids = lax.broadcasted_iota(jnp.int32, logits.shape, 0)
    first = jnp.sum(jnp.where(expert_ids == route_ref[0:1, :], logits, 0.0), axis=0, keepdims=True)
    second = jnp.sum(jnp.where(expert_ids == route_ref[1:2, :], logits, 0.0), axis=0, keepdims=True)
    gate_ref[0:1, :] = 1.0 / (1.0 + jnp.exp(second - first))
    gate_ref[1:2, :] = 1.0 / (1.0 + jnp.exp(first - second))


def backward_kernel(
    x_ref, hidden_grad_ref, triple_ref, context_ref, prob_ref, in_ref, out_ref, gain_ref,
    input_grad_ref, in_grad_ref, out_grad_ref, gain_grad_ref, bias_grad_ref,
    context_grad_ref, triple_grad_ref, turned_ref, key_ref, value_ref, diagonal_ref, sums_ref,
):
    length, width = x_ref.shape
    buckets, heads = bias_grad_ref.shape
    pair = 2 * (width // heads)
    pairs = heads // 2
    reach = length // 2
    span = reach + BLOCK
    scale = 1.0 / math.sqrt(width // heads)

    residual = hidden_grad_ref[...].astype(BF16)
    context_grad_ref[...] = dot(residual, out_ref[...], 1, 1).astype(BF16)
    out_grad_ref[...] = dot(jnp.transpose(context_ref[...]), residual)
    diagonal_ref[...] = jnp.zeros_like(diagonal_ref)

    def attend(step, carry):
        base = pl.multiple_of(step * pair, pair)
        query_columns = pl.ds(base, pair)
        key_columns = pl.ds(pl.multiple_of(width + base, pair), pair)
        value_columns = pl.ds(pl.multiple_of(2 * width + base, pair), pair)
        key_ref[...] = jnp.zeros_like(key_ref)
        value_ref[...] = jnp.zeros_like(value_ref)
        for block, low, high, skip in spans(length):
            rows = slice(block * BLOCK, (block + 1) * BLOCK)
            query = triple_ref[rows, query_columns] * jnp.asarray(scale, BF16)
            query = jnp.concatenate(halves(query), axis=0)
            grad = jnp.concatenate(halves(context_grad_ref[rows, query_columns]), axis=0)
            half = prob_ref[step, block, :, skip:]
            prob = half.astype(F32)
            prob_grad = dot(grad, triple_ref[low:high, value_columns], 1, 1)
            row_dot = jnp.sum(prob * prob_grad, axis=1, keepdims=True)
            score_grad = prob * (prob_grad - row_dot)
            diagonal_ref[step, :, skip:] += score_grad
            score_half = score_grad.astype(BF16)
            first, second = halves(triple_ref[low:high, key_columns])
            query_grad = dot(score_half[:BLOCK], first) + dot(score_half[BLOCK:], second)
            triple_grad_ref[rows, query_columns] = (query_grad * scale).astype(BF16)
            key_ref[low:high, :] += dot(score_half, query, 0, 0)
            value_ref[low:high, :] += dot(half, grad, 0, 0)
        triple_grad_ref[:, key_columns] = key_ref[...].astype(BF16)
        triple_grad_ref[:, value_columns] = value_ref[...].astype(BF16)
        return carry

    lax.fori_loop(0, pairs, attend, 0)

    x = x_ref[...]
    rms = lax.rsqrt(jnp.mean(x * x, axis=1, keepdims=True) + EPS)
    gain = gain_ref[0:1, :].astype(F32)
    turned_ref[...] = jnp.transpose((x * rms * gain).astype(BF16))
    chunk = 3 * pair

    def weigh(step, carry):
        columns = pl.ds(pl.multiple_of(step * chunk, BLOCK), chunk)
        in_grad_ref[:, columns] = dot(turned_ref[...], triple_grad_ref[:, columns])
        return carry

    lax.fori_loop(0, 3 * width // chunk, weigh, 0)

    gain_grad_ref[...] = jnp.zeros_like(gain_grad_ref)

    def finish(step, carry):
        rows = pl.ds(pl.multiple_of(step * BLOCK, BLOCK), BLOCK)
        normed_grad = dot(triple_grad_ref[rows, :], in_ref[...], 1, 1)
        part = x_ref[rows, :]
        scaling = lax.rsqrt(jnp.mean(part * part, axis=1, keepdims=True) + EPS)
        gain_grad_ref[...] += jnp.sum(normed_grad * (part * scaling), axis=0, keepdims=True)
        scaled = normed_grad * gain
        inner = jnp.mean(scaled * part, axis=1, keepdims=True)
        input_grad_ref[rows, :] = hidden_grad_ref[rows, :] + (
            scaling * scaled - part * (scaling * scaling * scaling) * inner
        )
        return carry

    lax.fori_loop(0, length // BLOCK, finish, 0)

    wide = span + BLOCK
    row_ids = lax.broadcasted_iota(jnp.int32, (BLOCK, wide), 0)
    for head in range(heads):
        sheet = diagonal_ref[head // 2, (head % 2) * BLOCK : (head % 2 + 1) * BLOCK, :]
        sheet = jnp.concatenate([sheet, jnp.zeros((BLOCK, BLOCK), F32)], axis=1)
        sheet = pltpu.roll(sheet, BLOCK - 1, 1)
        step = 1
        while step < BLOCK:
            sheet = jnp.where((row_ids & step) != 0, pltpu.roll(sheet, wide - step, 1), sheet)
            step *= 2
        sums_ref[head : head + 1, :] = jnp.sum(sheet, axis=0, keepdims=True)
    hot = bucket_hot(buckets, length, wide).astype(BF16)
    rest = sums_ref[...]
    total = jnp.zeros((buckets, heads), F32)
    for _ in range(3):
        piece = rest.astype(BF16)
        total = total + dot(hot, piece, 1, 1)
        rest = rest - piece.astype(F32)
    bias_grad_ref[...] = total


def whole(count):
    return [pl.BlockSpec(memory_space=pltpu.VMEM)] * count


def params(**extra):
    return pltpu.CompilerParams(vmem_limit_bytes=60 * 2**20, **extra)


def forward(x, segments, route_rows, full_in, full_out, router_rows, gains, bias_rows):
    length, width = x.shape
    heads = bias_rows.shape[0]
    blocks, span = length // BLOCK, length // 2 + BLOCK
    shape = jax.ShapeDtypeStruct
    return pl.pallas_call(
        forward_kernel,
        out_shape=(
            shape((length, width), F32),
            shape((length, width), BF16),
            shape((length, 3 * width), BF16),
            shape((length, width), BF16),
            shape((heads // 2, blocks, 2 * BLOCK, span), BF16),
            shape((2, length), F32),
        ),
        in_specs=whole(8),
        out_specs=tuple(whole(6)),
        scratch_shapes=[
            pltpu.VMEM((heads // 2, 2 * BLOCK, span), F32),
            pltpu.VMEM((blocks, BLOCK, span), F32),
            pltpu.VMEM((length, width), BF16),
        ],
        compiler_params=params(),
        cost_estimate=pl.CostEstimate(
            flops=12 * 10**9, bytes_accessed=2 * 10**7, transcendentals=2 * 10**6
        ),
        name="attention_forward",
    )(x, segments, route_rows, full_in, full_out, router_rows, gains, bias_rows)


def backward(x, hidden_grad, triple, context, probs, full_in, full_out, gains, buckets):
    length, width = x.shape
    pairs, blocks, _, span = probs.shape
    shape = jax.ShapeDtypeStruct
    return pl.pallas_call(
        backward_kernel,
        out_shape=(
            shape((length, width), F32),
            shape((width, 3 * width), F32),
            shape((width, width), F32),
            shape((1, width), F32),
            shape((buckets, 2 * pairs), F32),
        ),
        in_specs=whole(8),
        out_specs=tuple(whole(5)),
        scratch_shapes=[
            pltpu.VMEM((length, width), BF16),
            pltpu.VMEM((length, 3 * width), BF16),
            pltpu.VMEM((width, length), BF16),
            pltpu.VMEM((length, 2 * (width // (2 * pairs))), F32),
            pltpu.VMEM((length, 2 * (width // (2 * pairs))), F32),
            pltpu.VMEM((pairs, 2 * BLOCK, span), F32),
            pltpu.VMEM((2 * pairs, span + BLOCK), F32),
        ],
        compiler_params=params(),
        cost_estimate=pl.CostEstimate(
            flops=25 * 10**9, bytes_accessed=3 * 10**7, transcendentals=2 * 10**6
        ),
        name="attention_backward",
    )(x, hidden_grad, triple, context, probs, full_in, full_out, gains)


def shards(
    block_input,
    cotangent,
    segment_ids,
    routes,
    slot_ids,
    attention_in,
    attention_out,
    router_weight,
    first_gain,
    second_gain,
    bias_table,
    expert_up,
    expert_down,
):
    length, width = block_input.shape
    owners = lax.axis_size("expert")
    capacity = 4 * length // owners
    experts = router_weight.shape[1]
    slots = experts * capacity

    place = routes * capacity + slot_ids
    slot_range = jnp.arange(slots, dtype=jnp.int32)[None, :]
    match_first = place[:, 0:1] == slot_range
    match_second = place[:, 1:2] == slot_range
    hot_first = match_first.astype(BF16)
    hot_second = match_second.astype(BF16)
    hot_both = (match_first | match_second).astype(BF16)

    def exchange(rows):
        return lax.all_to_all(
            rows.reshape(owners, -1, rows.shape[-1]), "expert", split_axis=0, concat_axis=0, tiled=True
        )

    cot_rows = exchange(dot(hot_both, cotangent.astype(BF16), 0, 0).astype(BF16))
    full_in, full_out, full_router, gains, bias_small = (
        lax.all_gather(attention_in, "dp", axis=0, tiled=True),
        lax.all_gather(attention_out, "dp", axis=0, tiled=True),
        lax.all_gather(router_weight, "dp", axis=0, tiled=True),
        lax.all_gather(jnp.stack([first_gain, second_gain]), "dp", axis=1, tiled=True),
        lax.all_gather(bias_table, "dp", axis=0, tiled=True),
    )
    buckets = bias_small.shape[0]
    hidden_state, normed_two, triple, context, probs, gates = forward(
        block_input, segment_ids, routes.T, full_in, full_out, full_router.T, gains, bias_small.T
    )
    gate_first, gate_second = gates[0], gates[1]
    rms_two = lax.rsqrt(jnp.mean(hidden_state * hidden_state, axis=1, keepdims=True) + EPS)
    normal_two = hidden_state * rms_two
    expert_ids = jnp.arange(experts, dtype=jnp.int32)
    pick_first = (routes[:, 0:1] == expert_ids[None, :]).astype(F32)
    pick_second = (routes[:, 1:2] == expert_ids[None, :]).astype(F32)
    slot_gates = jnp.sum(
        jnp.where(match_first, gate_first[:, None], 0.0)
        + jnp.where(match_second, gate_second[:, None], 0.0),
        axis=0,
    )
    slot_gates = exchange(slot_gates.reshape(owners, 1, -1))
    up_matrix = expert_up[0]
    down_matrix = expert_down[0]
    flat_rows = exchange(dot(hot_both, normed_two, 0, 0).astype(BF16)).reshape(-1, width)
    expert_pre = dot(flat_rows, up_matrix)
    activation = (expert_pre * normal_cdf(expert_pre)).astype(BF16)
    produced = dot(activation, down_matrix).astype(BF16)
    returned = exchange(produced).reshape(slots, width)
    picked_first = dot(hot_first, returned)
    picked_second = dot(hot_second, returned)
    block_output = hidden_state + (
        gate_first[:, None] * picked_first + gate_second[:, None] * picked_second
    )
    gate_grad_first = jnp.sum(cotangent * picked_first, axis=1)
    gate_grad_second = jnp.sum(cotangent * picked_second, axis=1)
    logit_delta = gate_first * gate_second * (gate_grad_first - gate_grad_second)
    logit_grad = ((pick_first - pick_second) * logit_delta[:, None]).astype(BF16)
    flat_grad = (slot_gates.reshape(-1)[:, None] * cot_rows.reshape(-1, width).astype(F32)).astype(
        BF16
    )
    act_grad = dot(flat_grad, down_matrix, 1, 1)
    pre_grad = (act_grad * gelu_slope(expert_pre)).astype(BF16)
    grad_down = dot(activation, flat_grad, 0, 0)
    grad_up = dot(flat_rows, pre_grad, 0, 0)
    back_rows = dot(pre_grad, up_matrix, 1, 1).astype(BF16)
    home_rows = exchange(back_rows).reshape(slots, width)
    normed_grad = dot(hot_both, home_rows) + dot(logit_grad, full_router, 1, 1)
    router_grad = dot(normed_two, logit_grad, 0, 0)
    second_grad = jnp.sum(normed_grad * normal_two, axis=0)
    scaled_two = normed_grad * gains[1:2].astype(F32)
    hidden_grad = cotangent + (
        rms_two * scaled_two
        - hidden_state
        * (rms_two * rms_two * rms_two)
        * jnp.mean(scaled_two * hidden_state, axis=1, keepdims=True)
    )
    input_grad, triple_weight, proj_grad, first_grad, bias_grad = backward(
        block_input, hidden_grad, triple, context, probs, full_in, full_out, gains, buckets
    )
    member = lax.axis_index("dp")
    pair_size = lax.axis_size("dp")
    big = jnp.concatenate([triple_weight, proj_grad], axis=1)
    big = lax.psum(lax.psum_scatter(big, "dp", scatter_dimension=0, tiled=True), "expert")
    small = lax.psum((router_grad, first_grad[0], second_grad, bias_grad), ("expert", "dp"))
    small = [
        lax.dynamic_slice_in_dim(
            gradient, member * (gradient.shape[0] // pair_size), gradient.shape[0] // pair_size, 0
        )
        for gradient in small
    ]
    up_share, down_share = (
        lax.psum_scatter(
            grad_up[None].astype(BF16), "dp", scatter_dimension=2, tiled=True
        ).astype(F32),
        lax.psum_scatter(
            grad_down[None].astype(BF16), "dp", scatter_dimension=1, tiled=True
        ).astype(F32),
    )
    return (
        block_output,
        input_grad,
        big[:, : 3 * width],
        big[:, 3 * width :],
        small[0],
        small[1],
        small[2],
        small[3],
        up_share,
        down_share,
    )


def solution(mesh):
    rows = P(("expert", "dp"), None)
    return jax.shard_map(
        shards,
        mesh=mesh,
        in_specs=(
            rows,
            rows,
            rows,
            rows,
            rows,
            P("dp", None),
            P("dp", None),
            P("dp", None),
            P("dp"),
            P("dp"),
            P("dp", None),
            P("expert", None, None),
            P("expert", None, None),
        ),
        out_specs=(
            rows,
            rows,
            P("dp", None),
            P("dp", None),
            P("dp", None),
            P("dp"),
            P("dp"),
            P("dp", None),
            P("expert", None, "dp"),
            P("expert", "dp", None),
        ),
        check_vma=False,
    )
```

```python
import functools
import math

import jax
import jax.numpy as jnp
import numpy as np
from jax import lax
from jax.experimental import pallas as pl
from jax.experimental.pallas import tpu as pltpu
from jax.sharding import PartitionSpec as P

EPS = 1e-06
F32 = jnp.float32
BF16 = jnp.bfloat16
BLOCK = 128
MASKED = -1e30


def reach_marks(buckets, reach_len):
    half_count = buckets // 2
    step_ids = np.arange(1, half_count)
    thresholds = np.floor(half_count * (reach_len / half_count) ** (step_ids / half_count))
    thresholds = np.maximum(thresholds, half_count + step_ids)
    return [int(mark) for mark in thresholds.astype(np.int32)]


def normal_cdf(argument):
    return 0.5 * (1.0 + jax.scipy.special.erf(argument * (1.0 / math.sqrt(2.0))))


def gelu_slope(argument):
    return normal_cdf(argument) + argument * (
        jnp.exp(-0.5 * argument * argument) * (1.0 / math.sqrt(2.0 * math.pi))
    )


def dot(left, right, left_dim=1, right_dim=0):
    return lax.dot_general(
        left, right, (((left_dim,), (right_dim,)), ((), ())), preferred_element_type=F32
    )


def bucket_hot(buckets, length, width):
    column = lax.broadcasted_iota(jnp.int32, (1, width), 1)
    distance = jnp.maximum(length // 2 + BLOCK - 1 - column, 0)
    bucket = jnp.minimum(distance, buckets // 2)
    for mark in reach_marks(buckets, length):
        bucket = bucket + jnp.where(distance >= mark, 1, 0)
    rows = lax.broadcasted_iota(jnp.int32, (buckets, width), 0)
    return jnp.where(rows == bucket, 1.0, 0.0)


def spans(length):
    reach = length // 2
    for block in range(length // BLOCK):
        low = max(0, block * BLOCK - reach)
        high = (block + 1) * BLOCK
        yield block, low, high, reach + BLOCK - (high - low)


def halves(pair):
    lane = lax.broadcasted_iota(jnp.int32, (1, pair.shape[1]), 1)
    first = lane < pair.shape[1] // 2
    zero = jnp.zeros_like(pair)
    return jnp.where(first, pair, zero), jnp.where(first, zero, pair)


def hot_rows(place_ref, first, count):
    ids = first + lax.broadcasted_iota(jnp.int32, (count, place_ref.shape[1]), 0)
    return ids == place_ref[0:1, :], ids == place_ref[1:2, :]


def bf16_of(flags):
    return jnp.where(flags, 1.0, 0.0).astype(BF16)


def pieces_of(row):
    parts = []
    for _ in range(3):
        piece = row.astype(BF16).astype(F32)
        parts.append(piece)
        row = row - piece
    parts.append(jnp.zeros((5, row.shape[1]), F32))
    return jnp.concatenate(parts, axis=0).astype(BF16)


def forward_kernel(
    owners, experts, buckets,
    x_ref, cot_ref, segment_ref, route_ref, place_ref, in_half_ref, out_half_ref, small_part_ref,
    hidden_ref, normed_ref, triple_ref, context_ref, prob_ref, gate_ref,
    x_rows_ref, gate_rows_ref, cot_rows_ref, in_ref, out_ref, small_ref,
    table_ref, mask_ref, one_ref, half_ref, cot_send_ref, small_got_ref,
    weight_send, weight_recv, cot_send, cot_recv,
):
    me, core = lax.axis_index("expert"), lax.axis_index("dp")
    length, width = x_ref.shape
    heads = 2 * prob_ref.shape[0]
    pair = 2 * (width // heads)
    pairs = heads // 2
    reach = length // 2
    span = reach + BLOCK
    scale = 1.0 / math.sqrt(width // heads)
    slots = x_rows_ref.shape[0]
    capacity = slots // owners
    share = in_half_ref.shape[0]

    def block(index):
        return pl.ds(pl.multiple_of(index * capacity, capacity), capacity)

    mine = pl.ds(pl.multiple_of(core * share, share), share)
    greet(me, core, owners)
    weights = [
        remote(in_half_ref, in_ref.at[mine], weight_send.at[0], weight_recv.at[0], (me, 1 - core)),
        remote(out_half_ref, out_ref.at[mine], weight_send.at[1], weight_recv.at[1], (me, 1 - core)),
        remote(small_part_ref, small_got_ref, weight_send.at[2], weight_recv.at[2], (me, 1 - core)),
    ]
    for copy in weights:
        copy.start()
    in_ref[mine, :] = in_half_ref[...]
    out_ref[mine, :] = out_half_ref[...]
    half_ref[...] = cot_ref[...].astype(BF16)

    def cot_copy(step):
        peer = partner(me, step, owners, 1)
        return remote(
            cot_send_ref.at[block(step)], cot_rows_ref.at[block(step)], cot_send.at[step], cot_recv.at[step], (peer, core)
        )

    def dispatch(step, carry):
        peer = partner(me, step, owners, 1)
        first, second = hot_rows(place_ref, peer * capacity, capacity)
        cot_send_ref[block(step), :] = dot(bf16_of(first | second), half_ref[...]).astype(BF16)

        @pl.when(step >= 2)
        def _():
            cot_copy(step - 1).start()

        return carry

    lax.fori_loop(0, owners, dispatch, 0)
    cot_copy(owners - 1).start()
    cot_rows_ref[block(0), :] = cot_send_ref[block(0), :]

    x = x_ref[...]
    rms = lax.rsqrt(jnp.mean(x * x, axis=1, keepdims=True) + EPS)
    for copy in weights:
        copy.wait_recv()
    small_ref[...] = small_part_ref[...] + small_got_ref[...]
    one_ref[...] = (x * rms * small_ref[experts : experts + 1, :].astype(F32)).astype(BF16)

    chunk = 3 * pair

    def project(step, carry):
        columns = pl.ds(pl.multiple_of(step * chunk, BLOCK), chunk)
        triple_ref[:, columns] = dot(one_ref[...], in_ref[:, columns]).astype(BF16)
        return carry

    lax.fori_loop(0, 3 * width // chunk, project, 0)

    wide = span + BLOCK
    bias = small_ref[experts + 2 : experts + 2 + heads, 0:buckets]
    by_column = dot(bias, bucket_hot(buckets, length, wide).astype(BF16))
    for head in range(heads):
        spread = jnp.broadcast_to(by_column[head : head + 1, :], (BLOCK, wide))
        rolled = pltpu.roll(spread, wide - BLOCK + 1, 1, stride=1, stride_axis=0)
        table_ref[head // 2, (head % 2) * BLOCK : (head % 2 + 1) * BLOCK, :] = rolled[:, :span]

    segment_row = segment_ref[...].astype(F32)
    segment_column = jnp.transpose(jnp.broadcast_to(segment_row, (BLOCK, length)))
    for index, low, high, skip in spans(length):
        rows = index * BLOCK + lax.broadcasted_iota(jnp.int32, (BLOCK, high - low), 0)
        columns = low + lax.broadcasted_iota(jnp.int32, (BLOCK, high - low), 1)
        own = segment_column[index * BLOCK : (index + 1) * BLOCK, 0:1]
        allowed = (rows >= columns) & (own == segment_row[:, low:high])
        mask_ref[index, :, skip:] = jnp.where(allowed, 0.0, MASKED)

    def attend(step, carry):
        base = pl.multiple_of(step * pair, pair)
        query_columns = pl.ds(base, pair)
        key_columns = pl.ds(pl.multiple_of(width + base, pair), pair)
        value_columns = pl.ds(pl.multiple_of(2 * width + base, pair), pair)
        for index, low, high, skip in spans(length):
            rows = slice(index * BLOCK, (index + 1) * BLOCK)
            query = triple_ref[rows, query_columns] * jnp.asarray(scale, BF16)
            stacked = jnp.concatenate(halves(query), axis=0)
            scores = dot(stacked, triple_ref[low:high, key_columns], 1, 1)
            mask = mask_ref[index, :, skip:]
            scores = scores + table_ref[step, :, skip:] + jnp.concatenate([mask, mask], axis=0)
            top = jnp.max(scores, axis=1, keepdims=True)
            weight = jnp.exp(scores - top)
            prob = weight * (1.0 / jnp.sum(weight, axis=1, keepdims=True))
            half = prob.astype(BF16)
            prob_ref[step, index, :, skip:] = half
            first, second = halves(triple_ref[low:high, value_columns])
            context = dot(half[:BLOCK], first) + dot(half[BLOCK:], second)
            context_ref[rows, query_columns] = context.astype(BF16)
        return carry

    lax.fori_loop(0, pairs, attend, 0)

    hidden = x_ref[...] + dot(context_ref[...], out_ref[...])
    hidden_ref[...] = hidden
    rms = lax.rsqrt(jnp.mean(hidden * hidden, axis=1, keepdims=True) + EPS)
    normed = (hidden * rms * small_ref[experts + 1 : experts + 2, :].astype(F32)).astype(BF16)
    normed_ref[...] = normed
    logits = dot(small_ref[0:experts, :], normed, 1, 1)
    expert_ids = lax.broadcasted_iota(jnp.int32, logits.shape, 0)
    first = jnp.sum(jnp.where(expert_ids == route_ref[0:1, :], logits, 0.0), axis=0, keepdims=True)
    second = jnp.sum(jnp.where(expert_ids == route_ref[1:2, :], logits, 0.0), axis=0, keepdims=True)
    gate_first = 1.0 / (1.0 + jnp.exp(second - first))
    gate_second = 1.0 / (1.0 + jnp.exp(first - second))
    gate_ref[0:1, :] = gate_first
    gate_ref[1:2, :] = gate_second
    first_pieces, second_pieces = pieces_of(gate_first), pieces_of(gate_second)

    def outgoing(step, carry):
        first, second = hot_rows(place_ref, step * capacity, capacity)
        x_rows_ref[block(step), :] = dot(bf16_of(first | second), normed_ref[...]).astype(BF16)
        gates = dot(first_pieces, bf16_of(first), 1, 1) + dot(second_pieces, bf16_of(second), 1, 1)
        gate_rows_ref[step] = jnp.sum(gates, axis=0, keepdims=True)
        return carry

    lax.fori_loop(0, owners, outgoing, 0)

    def finish(step, carry):
        cot_copy(step).wait()
        return carry

    lax.fori_loop(1, owners, finish, 0)
    for copy in weights:
        copy.wait_send()


def backward_kernel(
    owners, experts, buckets, digits,
    x_ref, cot_ref, hidden_ref, normed_ref, triple_ref, context_ref, prob_ref, gate_ref, route_ref, place_ref,
    home_ref, dot_ref, in_ref, out_ref, small_ref, y_hbm,
    block_ref, input_grad_ref, in_share_ref, out_share_ref, small_sum_ref,
    context_grad_ref, triple_grad_ref, turned_ref, key_ref, value_ref, diagonal_ref, sums_ref,
    grads_ref, small_mine_ref, small_got_ref, came_ref, work_ref, got_ref, final_ref,
    y_send, y_recv, own_sem, core_send, core_recv, ring_send, ring_recv, small_send, small_recv,
):
    me, core = lax.axis_index("expert"), lax.axis_index("dp")
    hidden_grad_ref = block_ref
    length, width = x_ref.shape
    pairs = prob_ref.shape[0]
    heads = 2 * pairs
    pair = 2 * (width // heads)
    reach = length // 2
    span = reach + BLOCK
    scale = 1.0 / math.sqrt(width // heads)
    slots = home_ref.shape[0]
    capacity = slots // owners

    def block(index):
        return pl.ds(pl.multiple_of(index * capacity, capacity), capacity)

    own_y = pltpu.make_async_copy(y_hbm.at[block(0)], came_ref.at[block(me)], own_sem)
    own_y.start()
    greet(me, core, owners)

    def y_copy(step, sign):
        peer = partner(me, step, owners, -1)
        target = me if sign < 0 else partner(me, step, owners, 1)
        return remote(
            y_hbm.at[block(step)], came_ref.at[block(target)], y_send.at[step], y_recv.at[step], (peer, core)
        )

    def start_y(step, carry):
        y_copy(step, -1).start()
        return carry

    lax.fori_loop(1, owners, start_y, 0)

    def column(row):
        return jnp.transpose(jnp.broadcast_to(row, (BLOCK, length)))

    place_first = column(place_ref[0:1, :].astype(F32))
    place_second = column(place_ref[1:2, :].astype(F32))
    lane = lax.broadcasted_iota(jnp.int32, (length, BLOCK), 1).astype(F32)
    wide_k = 2 * BLOCK

    def hot_columns(group):
        first = (group * BLOCK).astype(F32) if hasattr(group, "astype") else float(group * BLOCK)
        return place_first - first == lane, place_second - first == lane

    def gather_rows(rows_ref, base_ref):
        def add(group, carry):
            left = hot_columns(2 * group)
            right = hot_columns(2 * group + 1)
            hot = jnp.concatenate([bf16_of(left[0] | left[1]), bf16_of(right[0] | right[1])], axis=1)
            rows = pl.ds(pl.multiple_of(group * wide_k, wide_k), wide_k)
            base_ref[...] += dot(hot, rows_ref[rows, :])
            return carry

        lax.fori_loop(0, slots // wide_k, add, 0)

    per_row = BLOCK // capacity

    def dot_row(group):
        if per_row == 1:
            return dot_ref[group]
        return jnp.concatenate([dot_ref[group * per_row + b] for b in range(per_row)], axis=1)

    def pick(group, carry):
        first, second = hot_columns(group)
        row = dot_row(group)
        return carry + jnp.where(first, row, 0.0) - jnp.where(second, row, 0.0)

    picked = lax.fori_loop(0, slots // BLOCK, pick, jnp.zeros((length, BLOCK), F32))
    difference = jnp.sum(picked, axis=1, keepdims=True)
    gates = column(gate_ref[0:1, :]) * column(gate_ref[1:2, :])
    ids = lax.broadcasted_iota(jnp.int32, (length, BLOCK), 1)
    pick_first = jnp.where(column(route_ref[0:1, :].astype(F32)).astype(jnp.int32) == ids, 1.0, 0.0)
    pick_second = jnp.where(column(route_ref[1:2, :].astype(F32)).astype(jnp.int32) == ids, 1.0, 0.0)
    logit_grad = ((pick_first - pick_second) * gates * difference).astype(BF16)

    small_mine_ref[...] = jnp.zeros_like(small_mine_ref)
    hidden_grad_ref[...] = dot(logit_grad[:, 0:experts], small_ref[0:experts, :])
    gather_rows(home_ref, hidden_grad_ref)
    small_mine_ref[0:experts, :] = dot(logit_grad, normed_ref[...], 0, 0)[0:experts, :]

    def settle(step, carry):
        rows = pl.ds(pl.multiple_of(step * BLOCK, BLOCK), BLOCK)
        normed_grad = hidden_grad_ref[rows, :]
        hidden = hidden_ref[rows, :]
        rms = lax.rsqrt(jnp.mean(hidden * hidden, axis=1, keepdims=True) + EPS)
        scaled = normed_grad * small_ref[experts + 1 : experts + 2, :].astype(F32)
        inner = jnp.mean(scaled * hidden, axis=1, keepdims=True)
        hidden_grad_ref[rows, :] = cot_ref[rows, :] + (rms * scaled - hidden * (rms * rms * rms) * inner)
        return carry + jnp.sum(normed_grad * (hidden * rms), axis=0, keepdims=True)

    small_mine_ref[experts + 1 : experts + 2, :] = lax.fori_loop(
        0, length // BLOCK, settle, jnp.zeros((1, width), F32)
    )

    residual = hidden_grad_ref[...].astype(BF16)
    context_grad_ref[...] = dot(residual, out_ref[...], 1, 1).astype(BF16)
    grads_ref[:, 3 * width :] = dot(jnp.transpose(context_ref[...]), residual)
    diagonal_ref[...] = jnp.zeros_like(diagonal_ref)

    def attend(step, carry):
        base = pl.multiple_of(step * pair, pair)
        query_columns = pl.ds(base, pair)
        key_columns = pl.ds(pl.multiple_of(width + base, pair), pair)
        value_columns = pl.ds(pl.multiple_of(2 * width + base, pair), pair)
        key_ref[...] = jnp.zeros_like(key_ref)
        value_ref[...] = jnp.zeros_like(value_ref)
        for index, low, high, skip in spans(length):
            rows = slice(index * BLOCK, (index + 1) * BLOCK)
            query = triple_ref[rows, query_columns] * jnp.asarray(scale, BF16)
            query = jnp.concatenate(halves(query), axis=0)
            grad = jnp.concatenate(halves(context_grad_ref[rows, query_columns]), axis=0)
            half = prob_ref[step, index, :, skip:]
            prob = half.astype(F32)
            prob_grad = dot(grad, triple_ref[low:high, value_columns], 1, 1)
            norm = 1.0 / jnp.sum(prob, axis=1, keepdims=True)
            row_dot = norm * jnp.sum(prob * prob_grad, axis=1, keepdims=True)
            score_grad = (prob * norm) * (prob_grad - row_dot)
            diagonal_ref[step, :, skip:] += score_grad
            score_half = score_grad.astype(BF16)
            first, second = halves(triple_ref[low:high, key_columns])
            query_grad = dot(score_half[:BLOCK], first) + dot(score_half[BLOCK:], second)
            triple_grad_ref[rows, query_columns] = (query_grad * scale).astype(BF16)
            key_ref[low:high, :] += dot(score_half, query, 0, 0)
            value_ref[low:high, :] += dot(half, grad, 0, 0)
        triple_grad_ref[:, key_columns] = key_ref[...].astype(BF16)
        triple_grad_ref[:, value_columns] = value_ref[...].astype(BF16)
        return carry

    lax.fori_loop(0, pairs, attend, 0)

    x = x_ref[...]
    rms = lax.rsqrt(jnp.mean(x * x, axis=1, keepdims=True) + EPS)
    gain = small_ref[experts : experts + 1, :].astype(F32)
    turned_ref[...] = jnp.transpose((x * rms * gain).astype(BF16))
    chunk = 3 * pair

    def weigh(step, carry):
        columns = pl.ds(pl.multiple_of(step * chunk, BLOCK), chunk)
        grads_ref[:, columns] = dot(turned_ref[...], triple_grad_ref[:, columns])
        return carry

    lax.fori_loop(0, 3 * width // chunk, weigh, 0)

    def finish(step, carry):
        rows = pl.ds(pl.multiple_of(step * BLOCK, BLOCK), BLOCK)
        normed_grad = dot(triple_grad_ref[rows, :], in_ref[...], 1, 1)
        part = x_ref[rows, :]
        scaling = lax.rsqrt(jnp.mean(part * part, axis=1, keepdims=True) + EPS)
        scaled = normed_grad * gain
        inner = jnp.mean(scaled * part, axis=1, keepdims=True)
        input_grad_ref[rows, :] = hidden_grad_ref[rows, :] + (
            scaling * scaled - part * (scaling * scaling * scaling) * inner
        )
        return carry + jnp.sum(normed_grad * (part * scaling), axis=0, keepdims=True)

    small_mine_ref[experts : experts + 1, :] = lax.fori_loop(
        0, length // BLOCK, finish, jnp.zeros((1, width), F32)
    )

    wide = span + BLOCK
    row_ids = lax.broadcasted_iota(jnp.int32, (BLOCK, wide), 0)
    for head in range(heads):
        sheet = diagonal_ref[head // 2, (head % 2) * BLOCK : (head % 2 + 1) * BLOCK, :]
        sheet = jnp.concatenate([sheet, jnp.zeros((BLOCK, BLOCK), F32)], axis=1)
        sheet = pltpu.roll(sheet, BLOCK - 1, 1)
        step = 1
        while step < BLOCK:
            sheet = jnp.where((row_ids & step) != 0, pltpu.roll(sheet, wide - step, 1), sheet)
            step *= 2
        sums_ref[head : head + 1, :] = jnp.sum(sheet, axis=0, keepdims=True)
    hot = bucket_hot(buckets, length, wide).astype(BF16)
    rest = sums_ref[...]
    total = jnp.zeros((heads, buckets), F32)
    for _ in range(3):
        piece = rest.astype(BF16)
        total = total + dot(piece, hot, 1, 1)
        rest = rest - piece.astype(F32)
    small_mine_ref[experts + 2 : experts + 2 + heads, 0:buckets] = total

    reduce_grads(
        me, core, digits, grads_ref, in_share_ref, out_share_ref, small_mine_ref, small_got_ref, small_sum_ref,
        work_ref, got_ref, final_ref, core_send, core_recv, ring_send, ring_recv, small_send, small_recv,
    )

    def finish_y(step, carry):
        y_copy(step, -1).wait_send()
        y_copy(step, 1).wait_recv()
        return carry

    own_y.wait()
    lax.fori_loop(1, owners, finish_y, 0)
    block_ref[...] = hidden_ref[...]
    gather_rows(came_ref, block_ref)


COLORS = 4


def reduce_grads(
    me, core, digits, grads_ref, in_share_ref, out_share_ref, small_mine_ref, small_got_ref, small_sum_ref,
    work_ref, got_ref, final_ref, core_send, core_recv, ring_send, ring_recv, small_send, small_recv,
):
    colors, many, rows, columns = work_ref.shape
    share, wide = in_share_ref.shape[0], grads_ref.shape[1]
    width = out_share_ref.shape[1]
    part_rows = share // colors
    down = part_rows // rows
    strides = []
    stride = 1
    for size in digits:
        strides.append(stride)
        stride *= size
    place = [lax.rem(lax.div(me, strides[axis]), digits[axis]) for axis in range(len(digits))]
    orders = [[0, 1, 2], [1, 0, 2]]

    def pieces(side, use):
        for across in range(wide // columns):
            sheet = grads_ref[
                pl.ds(pl.multiple_of(side * share, share), share), across * columns : (across + 1) * columns
            ]
            for color in range(colors):
                for step in range(down):
                    low = color * part_rows + step * rows
                    use(color, across * down + step, sheet[low : low + rows, :])

    def put_give(color, index, value):
        work_ref[color, index] = value.astype(BF16)

    pieces(1 - core, put_give)
    other = (me, 1 - core)
    swap = [
        remote(work_ref, got_ref.at[0], core_send.at[0], core_recv.at[0], other),
        remote(small_mine_ref, small_got_ref.at[0], core_send.at[1], core_recv.at[1], other),
    ]
    for copy in swap:
        copy.start()
    for copy in swap:
        copy.wait()

    def put_work(color, index, value):
        work_ref[color, index] = (value + got_ref[0, color, index].astype(F32)).astype(BF16)

    pieces(core, put_work)
    small_sum_ref[...] = small_mine_ref[...] + small_got_ref[0]

    def peer_of(axis, ahead):
        digit = lax.rem(place[axis] + ahead, digits[axis])
        return digit, (me + (digit - place[axis]) * strides[axis], core)

    levels = []
    for color in range(colors):
        order = orders[color % 2]
        base, extent, landing, seen = jnp.int32(0), many, 0, []
        for axis in order:
            part = extent // digits[axis]
            seen.append((axis, base, part, landing))
            base = base + place[axis] * part
            extent = part
            landing += part * (digits[axis] - 1)
        levels.append(seen)

    def sem_of(color, level, ahead, way):
        return ((color * 3 + level) * 4 + ahead) * 2 + way

    def scatter(color, level):
        axis, base, part, landing = levels[color][level]
        copies = []
        for ahead in range(1, digits[axis]):
            digit, device = peer_of(axis, ahead)
            index = sem_of(color, level, ahead, 0)
            copies.append(
                remote(
                    work_ref.at[color, pl.ds(base + digit * part, part)],
                    got_ref.at[1, color, pl.ds(landing + (ahead - 1) * part, part)],
                    ring_send.at[index], ring_recv.at[index], device,
                )
            )
        return copies

    def scattered(color, level):
        axis, base, part, landing = levels[color][level]
        mine = base + place[axis] * part
        target = final_ref if level == len(digits) - 1 else work_ref

        def add(step, carry):
            value = work_ref[color, mine + step].astype(F32)
            for ahead in range(1, digits[axis]):
                value = value + got_ref[1, color, landing + (ahead - 1) * part + step].astype(F32)
            target[color, mine + step] = value.astype(BF16)
            return carry

        lax.fori_loop(0, part, add, 0)

    def gather(color, level):
        axis, base, part, _ = levels[color][level]
        mine = base + place[axis] * part
        copies = []
        for ahead in range(1, digits[axis]):
            _, device = peer_of(axis, ahead)
            index = sem_of(color, level, ahead, 1)
            copies.append(
                remote(
                    final_ref.at[color, pl.ds(mine, part)], final_ref.at[color, pl.ds(mine, part)],
                    ring_send.at[index], ring_recv.at[index], device,
                )
            )
        return copies

    def small_copies(axis):
        copies = []
        for ahead in range(1, digits[axis]):
            _, device = peer_of(axis, ahead)
            index = sum(digits[:axis]) - axis + ahead
            copies.append(
                remote(small_sum_ref, small_got_ref.at[index], small_send.at[index], small_recv.at[index], device)
            )
        return copies

    depth = len(digits)
    flights = [None] * colors
    small_flight = None
    ticks = 2 * depth + 1
    lags = [0 if color < 2 else 1 for color in range(colors)]
    for tick in range(ticks + max(lags)):
        for color in range(colors):
            step = tick - lags[color]
            if step < 0 or step >= ticks:
                continue
            if flights[color] is not None:
                for copy in flights[color]:
                    copy.wait()
                flights[color] = None
                if step <= depth:
                    scattered(color, step - 1)
            if step < depth:
                flights[color] = scatter(color, step)
            elif step < 2 * depth:
                flights[color] = gather(color, 2 * depth - 1 - step)
            for copy in flights[color] or ():
                copy.start()
        if tick <= depth:
            if small_flight is not None:
                for copy in small_flight:
                    copy.wait()
                value = small_sum_ref[...]
                for ahead in range(1, digits[tick - 1]):
                    value = value + small_got_ref[sum(digits[: tick - 1]) - (tick - 1) + ahead]
                small_sum_ref[...] = value
                small_flight = None
            if tick < depth:
                small_flight = small_copies(tick)
                for copy in small_flight:
                    copy.start()

    for color in range(colors):
        for index in range(many):
            across, step = index // down, index % down
            low = color * part_rows + step * rows
            value = final_ref[color, index].astype(F32)
            if across * columns < 3 * width:
                in_share_ref[low : low + rows, across * columns : (across + 1) * columns] = value
            else:
                left = across * columns - 3 * width
                out_share_ref[low : low + rows, left : left + columns] = value


MESH = pl.DeviceIdType.MESH
GROUP = 4


def partner(me, step, owners, sign):
    groups = owners // GROUP
    outer = lax.rem(lax.div(me, GROUP) + sign * lax.div(step, GROUP) + groups, groups)
    inner = lax.rem(lax.rem(me, GROUP) + sign * lax.rem(step, GROUP) + GROUP, GROUP)
    return outer * GROUP + inner


def greet(me, core, owners):
    barrier = pltpu.get_barrier_semaphore()

    def signal(step, carry):
        pl.semaphore_signal(
            barrier, inc=1, device_id=(partner(me, step, owners, 1), core), device_id_type=MESH
        )
        return carry

    lax.fori_loop(1, owners, signal, 0)
    pl.semaphore_signal(barrier, inc=1, device_id=(me, 1 - core), device_id_type=MESH)
    pl.semaphore_wait(barrier, owners)


def remote(source, target, send, receive, device):
    return pltpu.make_async_remote_copy(
        src_ref=source, dst_ref=target, send_sem=send, recv_sem=receive,
        device_id=device, device_id_type=MESH,
    )


def whole(count):
    return [pl.BlockSpec(memory_space=pltpu.VMEM)] * count


def params(**extra):
    return pltpu.CompilerParams(vmem_limit_bytes=60 * 2**20, **extra)


def forward(x, cot, segments, route_rows, place_rows, in_half, out_half, small_part, owners, experts, buckets, heads):
    length, width = x.shape
    slots = 4 * length
    blocks, span = length // BLOCK, length // 2 + BLOCK
    shape, vmem, dma = jax.ShapeDtypeStruct, pltpu.VMEM, pltpu.SemaphoreType.DMA
    return pl.pallas_call(
        functools.partial(forward_kernel, owners, experts, buckets),
        out_shape=(
            shape((length, width), F32),
            shape((length, width), BF16),
            shape((length, 3 * width), BF16),
            shape((length, width), BF16),
            shape((heads // 2, blocks, 2 * BLOCK, span), BF16),
            shape((2, length), F32),
            shape((slots, width), BF16),
            shape((owners, 1, slots // owners), F32),
            shape((slots, width), BF16),
            shape((2 * in_half.shape[0], 3 * width), BF16),
            shape((2 * out_half.shape[0], width), BF16),
            shape(small_part.shape, BF16),
        ),
        in_specs=whole(8),
        out_specs=tuple(whole(12)),
        scratch_shapes=[
            vmem((heads // 2, 2 * BLOCK, span), F32),
            vmem((blocks, BLOCK, span), F32),
            vmem((length, width), BF16),
            vmem((length, width), BF16),
            vmem((slots, width), BF16),
            vmem(small_part.shape, BF16),
            dma((3,)),
            dma((3,)),
            dma((owners,)),
            dma((owners,)),
        ],
        compiler_params=params(collective_id=0, has_side_effects=True),
        cost_estimate=pl.CostEstimate(
            flops=12 * 10**9, bytes_accessed=2 * 10**7, transcendentals=2 * 10**6
        ),
        name="attention_forward",
    )(x, cot, segments, route_rows, place_rows, in_half, out_half, small_part)


def backward(operands, y_rows, owners, experts, buckets, digits):
    x, probs, small = operands[0], operands[6], operands[14]
    length, width = x.shape
    pairs, blocks, _, span = probs.shape
    slots = operands[10].shape[0]
    share = width // 2
    columns = width // 2
    piece_rows = share // COLORS * 8 // owners
    shape, vmem, dma = jax.ShapeDtypeStruct, pltpu.VMEM, pltpu.SemaphoreType.DMA
    pieces = (COLORS, owners, piece_rows, columns)
    return pl.pallas_call(
        functools.partial(backward_kernel, owners, experts, buckets, digits),
        out_shape=(
            shape((length, width), F32),
            shape((length, width), F32),
            shape((share, 3 * width), F32),
            shape((share, width), F32),
            shape(small.shape, F32),
        ),
        in_specs=whole(15) + [pl.BlockSpec(memory_space=pl.ANY)],
        out_specs=tuple(whole(5)),
        scratch_shapes=[
            vmem((length, width), BF16),
            vmem((length, 3 * width), BF16),
            vmem((width, length), BF16),
            vmem((length, 2 * (width // (2 * pairs))), F32),
            vmem((length, 2 * (width // (2 * pairs))), F32),
            vmem((pairs, 2 * BLOCK, span), F32),
            vmem((2 * pairs, span + BLOCK), F32),
            vmem((width, 4 * width), F32),
            vmem(small.shape, F32),
            vmem((sum(digits) - len(digits) + 1,) + small.shape, F32),
            vmem((slots, width), BF16),
            vmem(pieces, BF16),
            vmem((2,) + pieces, BF16),
            vmem(pieces, BF16),
            dma((owners,)),
            dma((owners,)),
            dma,
            dma((2,)),
            dma((2,)),
            dma((COLORS * 24,)),
            dma((COLORS * 24,)),
            dma((12,)),
            dma((12,)),
        ],
        compiler_params=pltpu.CompilerParams(
            vmem_limit_bytes=67043328, collective_id=2, has_side_effects=True
        ),
        cost_estimate=pl.CostEstimate(
            flops=25 * 10**9, bytes_accessed=3 * 10**7, transcendentals=2 * 10**6
        ),
        name="attention_backward",
    )(*operands, y_rows)


def expert_kernel(
    owners,
    x_ref, gate_ref, cot_ref, up_hbm, down_hbm,
    y_ref, home_ref, dot_ref, up_grad_ref, down_grad_ref,
    up, down, rows, cots, act, pre, out_sum, back_sum, back_rows, y_rows, gates, dots,
    up_ring, down_ring, up_got, down_got, up_out, down_out,
    weight_sem, cot_sem, own_sem, y_sem,
    x_send, x_recv, gate_send, gate_recv, back_send, back_recv, dot_send, dot_recv,
    ring_send, up_recv, down_recv, out_sem,
):
    me, core = lax.axis_index("expert"), lax.axis_index("dp")
    slots, width = rows.shape
    hidden = up.shape[1]
    capacity = slots // owners
    chunk = min(slots, 512)
    per = chunk // capacity
    tile = 256

    def block(index):
        return pl.ds(pl.multiple_of(index * capacity, capacity), capacity)

    load_up = pltpu.make_async_copy(up_hbm, up, weight_sem.at[0])
    load_down = pltpu.make_async_copy(down_hbm, down, weight_sem.at[1])
    load_cots = pltpu.make_async_copy(cot_ref, cots, cot_sem)
    load_up.start()
    load_down.start()
    load_cots.start()
    own_rows = pltpu.make_async_copy(x_ref.at[block(me)], rows.at[block(0)], own_sem.at[0])
    own_rows.start()
    greet(me, core, owners)

    def send_rows(step):
        peer = partner(me, step, owners, 1)
        return (
            remote(x_ref.at[block(peer)], rows.at[block(step)], x_send.at[step], x_recv.at[step], (peer, core)),
            remote(gate_ref.at[peer], gates.at[step], gate_send.at[step], gate_recv.at[step], (peer, core)),
        )

    def start_rows(step, carry):
        for copy in send_rows(step):
            copy.start()
        return carry

    lax.fori_loop(1, owners, start_rows, 0)
    gates[0] = gate_ref[me]

    def send_back(step):
        peer = partner(me, step, owners, -1)
        return (
            remote(back_rows.at[block(step)], home_ref.at[block(me)], back_send.at[step], back_recv.at[step], (peer, core)),
            remote(dots.at[step], dot_ref.at[me], dot_send.at[step], dot_recv.at[step], (peer, core)),
        )

    def get_back(step):
        peer = partner(me, step, owners, 1)
        return (
            remote(back_rows.at[block(step)], home_ref.at[block(peer)], back_send.at[step], back_recv.at[step], (peer, core)),
            remote(dots.at[step], dot_ref.at[peer], dot_send.at[step], dot_recv.at[step], (peer, core)),
        )

    home_own = pltpu.make_async_copy(back_rows.at[block(0)], home_ref.at[block(me)], own_sem.at[1])
    y_copies = []
    for index in range(slots // chunk):
        first = index * per
        part = slice(index * chunk, (index + 1) * chunk)
        if index == 0:
            own_rows.wait()
            load_cots.wait()
            load_up.wait()
            load_down.wait()

        def arrive(step, carry):
            for copy in send_rows(step):
                copy.wait_recv()
            return carry

        lax.fori_loop(max(first, 1), first + per, arrive, 0)
        column = jnp.concatenate(
            [
                jnp.transpose(jnp.broadcast_to(gates[first + b], (BLOCK, capacity)))[:, 0:1]
                for b in range(per)
            ],
            axis=0,
        )
        out_sum[...] = jnp.zeros_like(out_sum)
        back_sum[...] = jnp.zeros_like(back_sum)

        def through(step, carry):
            columns = pl.ds(pl.multiple_of(step * tile, tile), tile)
            before = dot(rows[part, :], up[:, columns])
            act_grad = dot(cots[part, :], down[columns, :], 1, 1)
            chance = normal_cdf(before)
            value = before * chance
            slope = chance + before * (
                jnp.exp(-0.5 * before * before) * (1.0 / math.sqrt(2.0 * math.pi))
            )
            out_sum[...] += dot(value.astype(BF16), down[columns, :])
            act[part, columns] = (value * column).astype(BF16)
            pre_grad = (act_grad * slope * column).astype(BF16)
            pre[part, columns] = pre_grad
            back_sum[...] += dot(pre_grad, up[:, columns], 1, 1)
            return carry

        lax.fori_loop(0, hidden // tile, through, 0)
        back_rows[part, :] = back_sum[...].astype(BF16)
        produced = out_sum[...]
        inner = jnp.sum(produced * cots[part, :].astype(F32), axis=1, keepdims=True)
        spread = jnp.broadcast_to(inner, (chunk, BLOCK))
        for b in range(per):
            turned = jnp.transpose(spread[b * capacity : (b + 1) * capacity, :])
            dots[first + b] = turned[0:1, :]
        if index >= 2:
            y_copies[index - 2].wait()
        y_rows[index % 2] = (produced * column).astype(BF16)
        y_copy = pltpu.make_async_copy(y_rows.at[index % 2], y_ref.at[part], y_sem.at[index % 2])
        y_copy.start()
        y_copies.append(y_copy)

        def start_back(step, carry):
            for copy in send_back(step):
                copy.start()
            return carry

        lax.fori_loop(max(first, 1), first + per, start_back, 0)
        if index == 0:
            home_own.start()
            dot_ref[me] = dots[0]
    for y_copy in y_copies[-2:]:
        y_copy.wait()

    half = hidden // 2
    count = half // tile

    def columns_of(side, step):
        return pl.ds(pl.multiple_of(side * half + step * tile, tile), tile)

    def up_tile(side, step):
        return dot(rows[...], pre[:, columns_of(side, step)], 0, 0)

    def down_tile(side, step):
        return dot(act[:, columns_of(side, step)], cots[...], 0, 0)

    def up_copy(step):
        slot = lax.rem(step, 2)
        return remote(
            up_ring.at[slot], up_got.at[:, columns_of(0, step)], ring_send.at[slot], up_recv.at[step], (me, 1 - core)
        )

    def down_copy(step):
        slot = lax.rem(step, 2)
        return remote(
            down_ring.at[slot], down_got.at[columns_of(0, step), :], ring_send.at[2 + slot], down_recv.at[step], (me, 1 - core)
        )

    def give(step, carry):
        slot = lax.rem(step, 2)

        @pl.when(step >= 2)
        def _():
            up_copy(step - 2).wait_send()
            down_copy(step - 2).wait_send()

        up_ring[slot] = up_tile(1 - core, step).astype(BF16)
        up_copy(step).start()
        down_ring[slot] = down_tile(1 - core, step).astype(BF16)
        down_copy(step).start()
        return carry

    lax.fori_loop(0, count, give, 0)

    def up_write(step):
        slot = lax.rem(step, 2)
        return pltpu.make_async_copy(up_out.at[slot], up_grad_ref.at[:, columns_of(0, step)], out_sem.at[slot])

    def down_write(step):
        slot = lax.rem(step, 2)
        return pltpu.make_async_copy(down_out.at[slot], down_grad_ref.at[columns_of(0, step), :], out_sem.at[2 + slot])

    def take(step, carry):
        slot = lax.rem(step, 2)

        @pl.when(step >= 2)
        def _():
            up_write(step - 2).wait()
            down_write(step - 2).wait()

        mine = up_tile(core, step)
        up_copy(step).wait_recv()
        up_out[slot] = mine + up_got[:, columns_of(0, step)].astype(F32)
        up_write(step).start()
        mine = down_tile(core, step)
        down_copy(step).wait_recv()
        down_out[slot] = mine + down_got[columns_of(0, step), :].astype(F32)
        down_write(step).start()
        return carry

    lax.fori_loop(0, count, take, 0)

    for step in range(max(count - 2, 0), count):
        up_copy(step).wait_send()
        down_copy(step).wait_send()
        up_write(step).wait()
        down_write(step).wait()
    home_own.wait()

    def finish(step, carry):
        for copy in send_rows(step):
            copy.wait_send()
        for copy in send_back(step):
            copy.wait_send()
        for copy in get_back(step):
            copy.wait_recv()
        return carry

    lax.fori_loop(1, owners, finish, 0)


def experts_of(x_rows, gate_rows, cot_rows, up_matrix, down_matrix, owners):
    slots, width = x_rows.shape
    hidden = up_matrix.shape[1]
    capacity = slots // owners
    chunk, tile, half = min(slots, 512), 256, hidden // 2
    count = half // tile
    shape, vmem, dma = jax.ShapeDtypeStruct, pltpu.VMEM, pltpu.SemaphoreType.DMA
    anywhere = pl.BlockSpec(memory_space=pl.ANY)
    near = pl.BlockSpec(memory_space=pltpu.VMEM)
    return pl.pallas_call(
        functools.partial(expert_kernel, owners),
        out_shape=(
            shape((slots, width), BF16),
            shape((slots, width), BF16),
            shape((owners, 1, capacity), F32),
            shape((width, half), F32),
            shape((half, width), F32),
        ),
        in_specs=[anywhere, near, anywhere, anywhere, anywhere],
        out_specs=(anywhere, anywhere, near, anywhere, anywhere),
        scratch_shapes=[
            vmem((width, hidden), BF16),
            vmem((hidden, width), BF16),
            vmem((slots, width), BF16),
            vmem((slots, width), BF16),
            vmem((slots, hidden), BF16),
            vmem((slots, hidden), BF16),
            vmem((chunk, width), F32),
            vmem((chunk, width), F32),
            vmem((slots, width), BF16),
            vmem((2, chunk, width), BF16),
            vmem((owners, 1, capacity), F32),
            vmem((owners, 1, capacity), F32),
            vmem((2, width, tile), BF16),
            vmem((2, tile, width), BF16),
            vmem((width, half), BF16),
            vmem((half, width), BF16),
            vmem((2, width, tile), F32),
            vmem((2, tile, width), F32),
            dma((2,)),
            dma,
            dma((2,)),
            dma((2,)),
        ]
        + [dma((owners,))] * 8
        + [dma((4,)), dma((count,)), dma((count,)), dma((4,))],
        compiler_params=pltpu.CompilerParams(
            vmem_limit_bytes=67043328, collective_id=1, has_side_effects=True
        ),
        cost_estimate=pl.CostEstimate(
            flops=58 * 10**9, bytes_accessed=4 * 10**7, transcendentals=2 * 10**7
        ),
        name="experts",
    )(x_rows, gate_rows, cot_rows, up_matrix, down_matrix)


def shards(
    block_input,
    cotangent,
    segment_ids,
    routes,
    slot_ids,
    attention_in,
    attention_out,
    router_weight,
    first_gain,
    second_gain,
    bias_table,
    expert_up,
    expert_down,
):
    length, width = block_input.shape
    owners = lax.axis_size("expert")
    capacity = 4 * length // owners
    experts = router_weight.shape[1]
    heads = bias_table.shape[1]
    member = lax.axis_index("dp")
    pair_size = lax.axis_size("dp")
    buckets = pair_size * bias_table.shape[0]
    share = width // pair_size
    inner = owners // 4
    side = math.isqrt(inner)
    digits = (side, inner // side, 4)

    rows = -(-(experts + 2 + heads) // 16) * 16
    wide_part = jnp.concatenate([router_weight.T, first_gain[None], second_gain[None]], axis=0)
    small_part = jnp.zeros((rows, width), BF16)
    small_part = lax.dynamic_update_slice(small_part, wide_part, (0, member * share))
    small_part = lax.dynamic_update_slice(
        small_part, bias_table.T, (experts + 2, member * bias_table.shape[0])
    )
    route_rows = routes.T
    place_rows = route_rows * capacity + slot_ids.T
    (
        hidden_state, normed_two, triple, context, probs, gates,
        x_rows, gate_rows, cot_rows, full_in, full_out, small,
    ) = forward(
        block_input, cotangent, segment_ids, route_rows, place_rows, attention_in, attention_out, small_part,
        owners, experts, buckets, heads,
    )
    y_rows, home_rows, gate_dots, up_share, down_share = experts_of(
        x_rows, gate_rows, cot_rows, expert_up[0], expert_down[0], owners
    )
    block_output, input_grad, in_share, out_share, small_sum = backward(
        (
            block_input, cotangent, hidden_state, normed_two, triple, context, probs, gates, route_rows, place_rows,
            home_rows, gate_dots, full_in, full_out, small,
        ),
        y_rows, owners, experts, buckets, digits,
    )
    mine = lax.dynamic_slice_in_dim(small_sum[: experts + 2], member * share, share, 1)
    bias_grad = lax.dynamic_slice(
        small_sum, (experts + 2, member * bias_table.shape[0]), (heads, bias_table.shape[0])
    )
    return (
        block_output,
        input_grad,
        in_share,
        out_share,
        mine[:experts].T,
        mine[experts],
        mine[experts + 1],
        bias_grad.T,
        up_share[None],
        down_share[None],
    )


def solution(mesh):
    rows = P(("expert", "dp"), None)
    return jax.shard_map(
        shards,
        mesh=mesh,
        in_specs=(
            rows,
            rows,
            rows,
            rows,
            rows,
            P("dp", None),
            P("dp", None),
            P("dp", None),
            P("dp"),
            P("dp"),
            P("dp", None),
            P("expert", None, None),
            P("expert", None, None),
        ),
        out_specs=(
            rows,
            rows,
            P("dp", None),
            P("dp", None),
            P("dp", None),
            P("dp"),
            P("dp"),
            P("dp", None),
            P("expert", None, "dp"),
            P("expert", "dp", None),
        ),
        check_vma=False,
    )
```

```python
import functools
import math

import jax
import jax.numpy as jnp
import numpy as np
from jax import lax
from jax.experimental import pallas as pl
from jax.experimental.pallas import tpu as pltpu
from jax.sharding import PartitionSpec as P

EPS = 1e-06
F32 = jnp.float32
BF16 = jnp.bfloat16
BLOCK = 128
MASKED = -1e30


def reach_marks(buckets, reach_len):
    half_count = buckets // 2
    step_ids = np.arange(1, half_count)
    thresholds = np.floor(half_count * (reach_len / half_count) ** (step_ids / half_count))
    thresholds = np.maximum(thresholds, half_count + step_ids)
    return [int(mark) for mark in thresholds.astype(np.int32)]


def normal_cdf(argument):
    return 0.5 * (1.0 + jax.scipy.special.erf(argument * (1.0 / math.sqrt(2.0))))


def gelu_slope(argument):
    return normal_cdf(argument) + argument * (
        jnp.exp(-0.5 * argument * argument) * (1.0 / math.sqrt(2.0 * math.pi))
    )


def dot(left, right, left_dim=1, right_dim=0):
    return lax.dot_general(
        left, right, (((left_dim,), (right_dim,)), ((), ())), preferred_element_type=F32
    )


def bucket_hot(buckets, length, width):
    column = lax.broadcasted_iota(jnp.int32, (1, width), 1)
    distance = jnp.maximum(length // 2 + BLOCK - 1 - column, 0)
    bucket = jnp.minimum(distance, buckets // 2)
    for mark in reach_marks(buckets, length):
        bucket = bucket + jnp.where(distance >= mark, 1, 0)
    rows = lax.broadcasted_iota(jnp.int32, (buckets, width), 0)
    return jnp.where(rows == bucket, 1.0, 0.0)


def spans(length):
    reach = length // 2
    for block in range(length // BLOCK):
        low = max(0, block * BLOCK - reach)
        high = (block + 1) * BLOCK
        yield block, low, high, reach + BLOCK - (high - low)


def halves(pair):
    lane = lax.broadcasted_iota(jnp.int32, (1, pair.shape[1]), 1)
    first = lane < pair.shape[1] // 2
    zero = jnp.zeros_like(pair)
    return jnp.where(first, pair, zero), jnp.where(first, zero, pair)


def hot_rows(place_ref, first, count):
    ids = first + lax.broadcasted_iota(jnp.int32, (count, place_ref.shape[1]), 0)
    return ids == place_ref[0:1, :], ids == place_ref[1:2, :]


def bf16_of(flags):
    return jnp.where(flags, 1.0, 0.0).astype(BF16)


def pieces_of(row):
    parts = []
    for _ in range(3):
        piece = row.astype(BF16).astype(F32)
        parts.append(piece)
        row = row - piece
    parts.append(jnp.zeros((5, row.shape[1]), F32))
    return jnp.concatenate(parts, axis=0).astype(BF16)


def forward_kernel(
    owners, experts, buckets,
    x_ref, cot_ref, segment_ref, route_ref, place_ref, in_half_ref, out_half_ref, small_part_ref,
    hidden_hbm, normed_hbm, triple_hbm, context_hbm, prob_hbm, gate_ref,
    x_rows_hbm, gate_rows_ref, cot_rows_ref, in_hbm, out_hbm, small_ref,
    hidden_ref, normed_ref, triple_ref, context_ref, prob_ref, x_rows_ref, in_ref, out_ref, store_sem,
    table_ref, mask_ref, one_ref, half_ref, cot_send_ref, small_got_ref,
    weight_send, weight_recv, cot_send, cot_recv,
):
    me, core = lax.axis_index("expert"), lax.axis_index("dp")
    length, width = x_ref.shape
    heads = 2 * prob_ref.shape[0]
    pair = 2 * (width // heads)
    pairs = heads // 2
    reach = length // 2
    span = reach + BLOCK
    scale = 1.0 / math.sqrt(width // heads)
    slots = x_rows_ref.shape[0]
    capacity = slots // owners
    share = in_half_ref.shape[0]

    def block(index):
        return pl.ds(pl.multiple_of(index * capacity, capacity), capacity)

    stores = []

    def store(source, target):
        copy = pltpu.make_async_copy(source, target, store_sem.at[len(stores)])
        copy.start()
        stores.append(copy)

    mine = pl.ds(pl.multiple_of(core * share, share), share)
    half_ref[...] = cot_ref[...].astype(BF16)
    greet(me, core, owners)
    weights = [
        remote(in_half_ref, in_ref.at[mine], weight_send.at[0], weight_recv.at[0], (me, 1 - core)),
        remote(out_half_ref, out_ref.at[mine], weight_send.at[1], weight_recv.at[1], (me, 1 - core)),
        remote(small_part_ref, small_got_ref, weight_send.at[2], weight_recv.at[2], (me, 1 - core)),
    ]
    for copy in weights:
        copy.start()
    in_ref[mine, :] = in_half_ref[...]
    out_ref[mine, :] = out_half_ref[...]

    def cot_copy(step):
        peer = partner(me, step, owners, 1)
        return remote(
            cot_send_ref.at[block(step)], cot_rows_ref.at[block(step)], cot_send.at[step], cot_recv.at[step], (peer, core)
        )

    def dispatch(step, carry):
        peer = partner(me, step, owners, 1)
        first, second = hot_rows(place_ref, peer * capacity, capacity)
        cot_send_ref[block(step), :] = dot(bf16_of(first | second), half_ref[...]).astype(BF16)

        @pl.when(step >= 2)
        def _():
            cot_copy(step - 1).start()

        return carry

    lax.fori_loop(0, owners, dispatch, 0)
    cot_copy(owners - 1).start()
    store(cot_send_ref.at[block(0)], cot_rows_ref.at[block(0)])

    x = x_ref[...]
    rms = lax.rsqrt(jnp.mean(x * x, axis=1, keepdims=True) + EPS)
    for copy in weights:
        copy.wait_recv()
    small_ref[...] = small_part_ref[...] + small_got_ref[...]
    store(in_ref, in_hbm)
    store(out_ref, out_hbm)
    one_ref[...] = (x * rms * small_ref[experts : experts + 1, :].astype(F32)).astype(BF16)

    chunk = 3 * pair

    def project(step, carry):
        columns = pl.ds(pl.multiple_of(step * chunk, BLOCK), chunk)
        triple_ref[:, columns] = dot(one_ref[...], in_ref[:, columns]).astype(BF16)
        return carry

    lax.fori_loop(0, 3 * width // chunk, project, 0)

    store(triple_ref, triple_hbm)
    wide = span + BLOCK
    bias = small_ref[experts + 2 : experts + 2 + heads, 0:buckets]
    by_column = dot(bias, bucket_hot(buckets, length, wide).astype(BF16))
    for head in range(heads):
        spread = jnp.broadcast_to(by_column[head : head + 1, :], (BLOCK, wide))
        rolled = pltpu.roll(spread, wide - BLOCK + 1, 1, stride=1, stride_axis=0)
        table_ref[head // 2, (head % 2) * BLOCK : (head % 2 + 1) * BLOCK, :] = rolled[:, :span]

    segment_row = segment_ref[...].astype(F32)
    segment_column = jnp.transpose(jnp.broadcast_to(segment_row, (BLOCK, length)))
    for index, low, high, skip in spans(length):
        rows = index * BLOCK + lax.broadcasted_iota(jnp.int32, (BLOCK, high - low), 0)
        columns = low + lax.broadcasted_iota(jnp.int32, (BLOCK, high - low), 1)
        own = segment_column[index * BLOCK : (index + 1) * BLOCK, 0:1]
        allowed = (rows >= columns) & (own == segment_row[:, low:high])
        mask_ref[index, :, skip:] = jnp.where(allowed, 0.0, MASKED)

    def attend(step, carry):
        base = pl.multiple_of(step * pair, pair)
        query_columns = pl.ds(base, pair)
        key_columns = pl.ds(pl.multiple_of(width + base, pair), pair)
        value_columns = pl.ds(pl.multiple_of(2 * width + base, pair), pair)
        for index, low, high, skip in spans(length):
            rows = slice(index * BLOCK, (index + 1) * BLOCK)
            query = triple_ref[rows, query_columns] * jnp.asarray(scale, BF16)
            stacked = jnp.concatenate(halves(query), axis=0)
            scores = dot(stacked, triple_ref[low:high, key_columns], 1, 1)
            mask = mask_ref[index, :, skip:]
            scores = scores + table_ref[step, :, skip:] + jnp.concatenate([mask, mask], axis=0)
            top = jnp.max(scores, axis=1, keepdims=True)
            weight = jnp.exp(scores - top)
            prob = weight * (1.0 / jnp.sum(weight, axis=1, keepdims=True))
            half = prob.astype(BF16)
            prob_ref[step, index, :, skip:] = half
            first, second = halves(triple_ref[low:high, value_columns])
            context = dot(half[:BLOCK], first) + dot(half[BLOCK:], second)
            context_ref[rows, query_columns] = context.astype(BF16)
        return carry

    lax.fori_loop(0, pairs, attend, 0)
    store(prob_ref, prob_hbm)
    store(context_ref, context_hbm)

    hidden = x_ref[...] + dot(context_ref[...], out_ref[...])
    hidden_ref[...] = hidden
    store(hidden_ref, hidden_hbm)
    rms = lax.rsqrt(jnp.mean(hidden * hidden, axis=1, keepdims=True) + EPS)
    normed = (hidden * rms * small_ref[experts + 1 : experts + 2, :].astype(F32)).astype(BF16)
    normed_ref[...] = normed
    store(normed_ref, normed_hbm)
    logits = dot(small_ref[0:experts, :], normed, 1, 1)
    expert_ids = lax.broadcasted_iota(jnp.int32, logits.shape, 0)
    first = jnp.sum(jnp.where(expert_ids == route_ref[0:1, :], logits, 0.0), axis=0, keepdims=True)
    second = jnp.sum(jnp.where(expert_ids == route_ref[1:2, :], logits, 0.0), axis=0, keepdims=True)
    gate_first = 1.0 / (1.0 + jnp.exp(second - first))
    gate_second = 1.0 / (1.0 + jnp.exp(first - second))
    gate_ref[0:1, :] = gate_first
    gate_ref[1:2, :] = gate_second
    first_pieces, second_pieces = pieces_of(gate_first), pieces_of(gate_second)

    def outgoing(step, carry):
        first, second = hot_rows(place_ref, step * capacity, capacity)
        x_rows_ref[block(step), :] = dot(bf16_of(first | second), normed_ref[...]).astype(BF16)
        gates = dot(first_pieces, bf16_of(first), 1, 1) + dot(second_pieces, bf16_of(second), 1, 1)
        gate_rows_ref[step] = jnp.sum(gates, axis=0, keepdims=True)
        return carry

    lax.fori_loop(0, owners, outgoing, 0)
    store(x_rows_ref, x_rows_hbm)

    def finish(step, carry):
        cot_copy(step).wait()
        return carry

    lax.fori_loop(1, owners, finish, 0)
    for copy in weights:
        copy.wait_send()
    for copy in stores:
        copy.wait()


def backward_kernel(
    owners, experts, buckets, digits,
    x_hbm, cot_hbm, hidden_hbm, normed_hbm, triple_hbm, context_hbm, prob_hbm, gate_ref, route_ref, place_ref,
    home_hbm, dot_ref, in_hbm, out_hbm, small_ref, y_hbm,
    block_ref, input_grad_ref, in_share_ref, out_share_ref, small_sum_ref,
    home_ref, cot_ref, hidden_ref, normed_ref, context_ref, out_ref, x_ref, triple_ref, prob_ref, in_ref, load_sem,
    context_grad_ref, triple_grad_ref, turned_ref, key_ref, value_ref, diagonal_ref, sums_ref,
    grads_ref, small_mine_ref, small_got_ref, came_ref, work_ref, got_ref, final_ref,
    y_send, y_recv, own_sem, core_send, core_recv, ring_send, ring_recv, small_send, small_recv,
):
    me, core = lax.axis_index("expert"), lax.axis_index("dp")
    hidden_grad_ref = block_ref
    length, width = x_ref.shape
    pairs = prob_ref.shape[0]
    heads = 2 * pairs
    pair = 2 * (width // heads)
    reach = length // 2
    span = reach + BLOCK
    scale = 1.0 / math.sqrt(width // heads)
    slots = home_ref.shape[0]
    capacity = slots // owners

    def block(index):
        return pl.ds(pl.multiple_of(index * capacity, capacity), capacity)

    loads = [
        pltpu.make_async_copy(source, target, load_sem.at[index])
        for index, (source, target) in enumerate(
            (
                (home_hbm, home_ref),
                (cot_hbm, cot_ref),
                (hidden_hbm, hidden_ref),
                (normed_hbm, normed_ref),
                (context_hbm, context_ref),
                (out_hbm, out_ref),
                (x_hbm, x_ref),
                (triple_hbm, triple_ref),
                (prob_hbm, prob_ref),
                (in_hbm, in_ref),
            )
        )
    ]
    for copy in loads:
        copy.start()
    own_y = pltpu.make_async_copy(y_hbm.at[block(0)], came_ref.at[block(me)], own_sem)
    own_y.start()
    greet(me, core, owners)

    def y_copy(step, sign):
        peer = partner(me, step, owners, -1)
        target = me if sign < 0 else partner(me, step, owners, 1)
        return remote(
            y_hbm.at[block(step)], came_ref.at[block(target)], y_send.at[step], y_recv.at[step], (peer, core)
        )

    def start_y(step, carry):
        y_copy(step, -1).start()
        return carry

    lax.fori_loop(1, owners, start_y, 0)

    def column(row):
        return jnp.transpose(jnp.broadcast_to(row, (BLOCK, length)))

    place_first = column(place_ref[0:1, :].astype(F32))
    place_second = column(place_ref[1:2, :].astype(F32))
    lane = lax.broadcasted_iota(jnp.int32, (length, BLOCK), 1).astype(F32)
    wide_k = 2 * BLOCK

    def hot_columns(group):
        first = (group * BLOCK).astype(F32) if hasattr(group, "astype") else float(group * BLOCK)
        return place_first - first == lane, place_second - first == lane

    def gather_rows(rows_ref, base_ref):
        def add(group, carry):
            left = hot_columns(2 * group)
            right = hot_columns(2 * group + 1)
            hot = jnp.concatenate([bf16_of(left[0] | left[1]), bf16_of(right[0] | right[1])], axis=1)
            rows = pl.ds(pl.multiple_of(group * wide_k, wide_k), wide_k)
            base_ref[...] += dot(hot, rows_ref[rows, :])
            return carry

        lax.fori_loop(0, slots // wide_k, add, 0)

    per_row = BLOCK // capacity

    def dot_row(group):
        if per_row == 1:
            return dot_ref[group]
        return jnp.concatenate([dot_ref[group * per_row + b] for b in range(per_row)], axis=1)

    def pick(group, carry):
        first, second = hot_columns(group)
        row = dot_row(group)
        return carry + jnp.where(first, row, 0.0) - jnp.where(second, row, 0.0)

    picked = lax.fori_loop(0, slots // BLOCK, pick, jnp.zeros((length, BLOCK), F32))
    difference = jnp.sum(picked, axis=1, keepdims=True)
    gates = column(gate_ref[0:1, :]) * column(gate_ref[1:2, :])
    ids = lax.broadcasted_iota(jnp.int32, (length, BLOCK), 1)
    pick_first = jnp.where(column(route_ref[0:1, :].astype(F32)).astype(jnp.int32) == ids, 1.0, 0.0)
    pick_second = jnp.where(column(route_ref[1:2, :].astype(F32)).astype(jnp.int32) == ids, 1.0, 0.0)
    logit_grad = ((pick_first - pick_second) * gates * difference).astype(BF16)

    small_mine_ref[...] = jnp.zeros_like(small_mine_ref)
    for copy in loads[:6]:
        copy.wait()
    hidden_grad_ref[...] = dot(logit_grad[:, 0:experts], small_ref[0:experts, :])
    gather_rows(home_ref, hidden_grad_ref)
    small_mine_ref[0:experts, :] = dot(logit_grad, normed_ref[...], 0, 0)[0:experts, :]

    def settle(step, carry):
        rows = pl.ds(pl.multiple_of(step * BLOCK, BLOCK), BLOCK)
        normed_grad = hidden_grad_ref[rows, :]
        hidden = hidden_ref[rows, :]
        rms = lax.rsqrt(jnp.mean(hidden * hidden, axis=1, keepdims=True) + EPS)
        scaled = normed_grad * small_ref[experts + 1 : experts + 2, :].astype(F32)
        inner = jnp.mean(scaled * hidden, axis=1, keepdims=True)
        hidden_grad_ref[rows, :] = cot_ref[rows, :] + (rms * scaled - hidden * (rms * rms * rms) * inner)
        return carry + jnp.sum(normed_grad * (hidden * rms), axis=0, keepdims=True)

    small_mine_ref[experts + 1 : experts + 2, :] = lax.fori_loop(
        0, length // BLOCK, settle, jnp.zeros((1, width), F32)
    )

    residual = hidden_grad_ref[...].astype(BF16)
    grads_ref[:, 3 * width :] = dot(jnp.transpose(context_ref[...]), residual)
    advance, advance_small = reducer(
        me, core, digits, grads_ref, in_share_ref, out_share_ref, small_mine_ref, small_got_ref, small_sum_ref,
        work_ref, got_ref, final_ref, core_send, core_recv, ring_send, ring_recv, small_send, small_recv,
    )
    advance(3)
    context_grad_ref[...] = dot(residual, out_ref[...], 1, 1).astype(BF16)
    diagonal_ref[...] = jnp.zeros_like(diagonal_ref)
    for copy in loads[6:]:
        copy.wait()
    x = x_ref[...]
    rms = lax.rsqrt(jnp.mean(x * x, axis=1, keepdims=True) + EPS)
    gain = small_ref[experts : experts + 1, :].astype(F32)
    turned_ref[...] = jnp.transpose((x * rms * gain).astype(BF16))

    def attend(step, carry):
        base = pl.multiple_of(step * pair, pair)
        query_columns = pl.ds(base, pair)
        key_columns = pl.ds(pl.multiple_of(width + base, pair), pair)
        value_columns = pl.ds(pl.multiple_of(2 * width + base, pair), pair)
        key_ref[...] = jnp.zeros_like(key_ref)
        value_ref[...] = jnp.zeros_like(value_ref)
        for index, low, high, skip in spans(length):
            rows = slice(index * BLOCK, (index + 1) * BLOCK)
            query = triple_ref[rows, query_columns] * jnp.asarray(scale, BF16)
            query = jnp.concatenate(halves(query), axis=0)
            grad = jnp.concatenate(halves(context_grad_ref[rows, query_columns]), axis=0)
            half = prob_ref[step, index, :, skip:]
            prob = half.astype(F32)
            prob_grad = dot(grad, triple_ref[low:high, value_columns], 1, 1)
            norm = 1.0 / jnp.sum(prob, axis=1, keepdims=True)
            row_dot = norm * jnp.sum(prob * prob_grad, axis=1, keepdims=True)
            score_grad = (prob * norm) * (prob_grad - row_dot)
            diagonal_ref[step, :, skip:] += score_grad
            score_half = score_grad.astype(BF16)
            first, second = halves(triple_ref[low:high, key_columns])
            query_grad = dot(score_half[:BLOCK], first) + dot(score_half[BLOCK:], second)
            triple_grad_ref[rows, query_columns] = (query_grad * scale).astype(BF16)
            key_ref[low:high, :] += dot(score_half, query, 0, 0)
            value_ref[low:high, :] += dot(half, grad, 0, 0)
        triple_grad_ref[:, key_columns] = key_ref[...].astype(BF16)
        triple_grad_ref[:, value_columns] = value_ref[...].astype(BF16)
        return carry

    groups = COLORS - 1
    part = width // groups
    for group in range(groups):
        lax.fori_loop(group * pairs // groups, (group + 1) * pairs // groups, attend, 0)
        for color in [3, *range(group)]:
            advance(color)

        def weigh(section, carry):
            source = pl.ds(pl.multiple_of(section * width + group * part, BLOCK), part)
            target = pl.ds(pl.multiple_of(group * width + section * part, BLOCK), part)
            grads_ref[:, target] = dot(turned_ref[...], triple_grad_ref[:, source])
            return carry

        lax.fori_loop(0, 3, weigh, 0)
        advance(group)

    def finish(step, carry):
        rows = pl.ds(pl.multiple_of(step * BLOCK, BLOCK), BLOCK)
        normed_grad = dot(triple_grad_ref[rows, :], in_ref[...], 1, 1)
        part = x_ref[rows, :]
        scaling = lax.rsqrt(jnp.mean(part * part, axis=1, keepdims=True) + EPS)
        scaled = normed_grad * gain
        inner = jnp.mean(scaled * part, axis=1, keepdims=True)
        input_grad_ref[rows, :] = hidden_grad_ref[rows, :] + (
            scaling * scaled - part * (scaling * scaling * scaling) * inner
        )
        return carry + jnp.sum(normed_grad * (part * scaling), axis=0, keepdims=True)

    small_mine_ref[experts : experts + 1, :] = lax.fori_loop(
        0, length // BLOCK, finish, jnp.zeros((1, width), F32)
    )

    for color in (2, 1, 0, 3):
        advance(color)
    wide = span + BLOCK
    row_ids = lax.broadcasted_iota(jnp.int32, (BLOCK, wide), 0)
    for head in range(heads):
        sheet = diagonal_ref[head // 2, (head % 2) * BLOCK : (head % 2 + 1) * BLOCK, :]
        sheet = jnp.concatenate([sheet, jnp.zeros((BLOCK, BLOCK), F32)], axis=1)
        sheet = pltpu.roll(sheet, BLOCK - 1, 1)
        step = 1
        while step < BLOCK:
            sheet = jnp.where((row_ids & step) != 0, pltpu.roll(sheet, wide - step, 1), sheet)
            step *= 2
        sums_ref[head : head + 1, :] = jnp.sum(sheet, axis=0, keepdims=True)
    hot = bucket_hot(buckets, length, wide).astype(BF16)
    rest = sums_ref[...]
    total = jnp.zeros((heads, buckets), F32)
    for _ in range(3):
        piece = rest.astype(BF16)
        total = total + dot(piece, hot, 1, 1)
        rest = rest - piece.astype(F32)
    small_mine_ref[experts + 2 : experts + 2 + heads, 0:buckets] = total

    def finish_y(step, carry):
        y_copy(step, -1).wait_send()
        y_copy(step, 1).wait_recv()
        return carry

    for turn in range(2 * len(digits) + 2):
        for color in (2, 1, 0, 3):
            advance(color)
        advance_small()
        if turn == 3:
            own_y.wait()
            lax.fori_loop(1, owners, finish_y, 0)
            block_ref[...] = hidden_ref[...]
            gather_rows(came_ref, block_ref)


COLORS = 4


def reducer(
    me, core, digits, grads_ref, in_share_ref, out_share_ref, small_mine_ref, small_got_ref, small_sum_ref,
    work_ref, got_ref, final_ref, core_send, core_recv, ring_send, ring_recv, small_send, small_recv,
):
    _, many, rows, columns = work_ref.shape
    share, width = out_share_ref.shape
    groups = COLORS - 1
    section = width // groups
    down = share // rows
    strides = []
    stride = 1
    for size in digits:
        strides.append(stride)
        stride *= size
    place = [lax.rem(lax.div(me, strides[axis]), digits[axis]) for axis in range(len(digits))]
    orders = [[0, 1, 2], [1, 0, 2]]
    other = (me, 1 - core)

    def sheets(color, side):
        for across in range(width // columns):
            sheet = grads_ref[
                pl.ds(pl.multiple_of(side * share, share), share),
                color * width + across * columns : color * width + (across + 1) * columns,
            ]
            for step in range(down):
                yield across * down + step, sheet[step * rows : (step + 1) * rows, :]

    def swap(color):
        for index, value in sheets(color, 1 - core):
            work_ref[color, index] = value.astype(BF16)
        return [remote(work_ref.at[color], got_ref.at[0, color], core_send.at[color], core_recv.at[color], other)]

    def swapped(color):
        for index, value in sheets(color, core):
            work_ref[color, index] = (value + got_ref[0, color, index].astype(F32)).astype(BF16)

    def settled(color):
        for index in range(many):
            across, step = index // down, index % down
            low = step * rows
            value = final_ref[color, index].astype(F32)
            if color == groups:
                out_share_ref[low : low + rows, across * columns : (across + 1) * columns] = value
                continue
            for left in range(0, columns, BLOCK):
                start = across * columns + left
                target = start // section * width + color * section + start % section
                in_share_ref[low : low + rows, target : target + BLOCK] = value[:, left : left + BLOCK]

    def peer_of(axis, ahead):
        digit = lax.rem(place[axis] + ahead, digits[axis])
        return digit, (me + (digit - place[axis]) * strides[axis], core)

    levels = []
    for color in range(COLORS):
        order = orders[color % 2]
        base, extent, landing, seen = jnp.int32(0), many, 0, []
        for axis in order:
            part = extent // digits[axis]
            seen.append((axis, base, part, landing))
            base = base + place[axis] * part
            extent = part
            landing += part * (digits[axis] - 1)
        levels.append(seen)

    def sem_of(color, level, ahead, way):
        return ((color * 3 + level) * 4 + ahead) * 2 + way

    def scatter(color, level):
        axis, base, part, landing = levels[color][level]
        copies = []
        for ahead in range(1, digits[axis]):
            digit, device = peer_of(axis, ahead)
            index = sem_of(color, level, ahead, 0)
            copies.append(
                remote(
                    work_ref.at[color, pl.ds(base + digit * part, part)],
                    got_ref.at[1, color, pl.ds(landing + (ahead - 1) * part, part)],
                    ring_send.at[index], ring_recv.at[index], device,
                )
            )
        return copies

    def scattered(color, level):
        axis, base, part, landing = levels[color][level]
        mine = base + place[axis] * part
        target = final_ref if level == len(digits) - 1 else work_ref

        def add(step, carry):
            value = work_ref[color, mine + step].astype(F32)
            for ahead in range(1, digits[axis]):
                value = value + got_ref[1, color, landing + (ahead - 1) * part + step].astype(F32)
            target[color, mine + step] = value.astype(BF16)
            return carry

        lax.fori_loop(0, part, add, 0)

    def gather(color, level):
        axis, base, part, _ = levels[color][level]
        mine = base + place[axis] * part
        copies = []
        for ahead in range(1, digits[axis]):
            _, device = peer_of(axis, ahead)
            index = sem_of(color, level, ahead, 1)
            copies.append(
                remote(
                    final_ref.at[color, pl.ds(mine, part)], final_ref.at[color, pl.ds(mine, part)],
                    ring_send.at[index], ring_recv.at[index], device,
                )
            )
        return copies

    def small_copies(axis):
        copies = []
        for ahead in range(1, digits[axis]):
            _, device = peer_of(axis, ahead)
            index = sum(digits[:axis]) - axis + ahead
            copies.append(
                remote(small_sum_ref, small_got_ref.at[index], small_send.at[index], small_recv.at[index], device)
            )
        return copies

    depth = len(digits)
    stage, flight = [0] * COLORS, [()] * COLORS

    def advance(color):
        now = stage[color]
        if now > 2 * depth + 1:
            return
        for copy in flight[color]:
            copy.wait()
        if now == 1:
            swapped(color)
        elif 1 < now <= depth + 1:
            scattered(color, now - 2)
        elif now == 2 * depth + 1:
            settled(color)
        if now == 0:
            flight[color] = swap(color)
        elif now <= depth:
            flight[color] = scatter(color, now - 1)
        elif now <= 2 * depth:
            flight[color] = gather(color, 2 * depth - now)
        else:
            flight[color] = ()
        for copy in flight[color]:
            copy.start()
        stage[color] = now + 1

    small_state = [0, ()]

    def advance_small():
        now, flying = small_state
        if now > depth + 1:
            return
        for copy in flying:
            copy.wait()
        if now == 1:
            small_sum_ref[...] = small_mine_ref[...] + small_got_ref[0]
        elif now > 1:
            value = small_sum_ref[...]
            for ahead in range(1, digits[now - 2]):
                value = value + small_got_ref[sum(digits[: now - 2]) - (now - 2) + ahead]
            small_sum_ref[...] = value
        if now == 0:
            flying = [
                remote(
                    small_mine_ref, small_got_ref.at[0], core_send.at[COLORS], core_recv.at[COLORS], other
                )
            ]
        elif now <= depth:
            flying = small_copies(now - 1)
        else:
            flying = ()
        for copy in flying:
            copy.start()
        small_state[:] = now + 1, flying

    return advance, advance_small


MESH = pl.DeviceIdType.MESH
GROUP = 4


def partner(me, step, owners, sign):
    groups = owners // GROUP
    outer = lax.rem(lax.div(me, GROUP) + sign * lax.div(step, GROUP) + groups, groups)
    inner = lax.rem(lax.rem(me, GROUP) + sign * lax.rem(step, GROUP) + GROUP, GROUP)
    return outer * GROUP + inner


def greet(me, core, owners):
    barrier = pltpu.get_barrier_semaphore()

    def signal(step, carry):
        pl.semaphore_signal(
            barrier, inc=1, device_id=(partner(me, step, owners, 1), core), device_id_type=MESH
        )
        return carry

    lax.fori_loop(1, owners, signal, 0)
    pl.semaphore_signal(barrier, inc=1, device_id=(me, 1 - core), device_id_type=MESH)
    pl.semaphore_wait(barrier, owners)


def remote(source, target, send, receive, device):
    return pltpu.make_async_remote_copy(
        src_ref=source, dst_ref=target, send_sem=send, recv_sem=receive,
        device_id=device, device_id_type=MESH,
    )


def whole(count):
    return [pl.BlockSpec(memory_space=pltpu.VMEM)] * count


def params(**extra):
    return pltpu.CompilerParams(vmem_limit_bytes=60 * 2**20, **extra)


def forward(x, cot, segments, route_rows, place_rows, in_half, out_half, small_part, owners, experts, buckets, heads):
    length, width = x.shape
    slots = 4 * length
    blocks, span = length // BLOCK, length // 2 + BLOCK
    any_, near = pl.BlockSpec(memory_space=pl.ANY), pl.BlockSpec(memory_space=pltpu.VMEM)
    shape, vmem, dma = jax.ShapeDtypeStruct, pltpu.VMEM, pltpu.SemaphoreType.DMA
    return pl.pallas_call(
        functools.partial(forward_kernel, owners, experts, buckets),
        out_shape=(
            shape((length, width), F32),
            shape((length, width), BF16),
            shape((length, 3 * width), BF16),
            shape((length, width), BF16),
            shape((heads // 2, blocks, 2 * BLOCK, span), BF16),
            shape((2, length), F32),
            shape((slots, width), BF16),
            shape((owners, 1, slots // owners), F32),
            shape((slots, width), BF16),
            shape((2 * in_half.shape[0], 3 * width), BF16),
            shape((2 * out_half.shape[0], width), BF16),
            shape(small_part.shape, BF16),
        ),
        in_specs=whole(8),
        out_specs=(any_, any_, any_, any_, any_, near, any_, near, any_, any_, any_, near),
        scratch_shapes=[
            vmem((length, width), F32),
            vmem((length, width), BF16),
            vmem((length, 3 * width), BF16),
            vmem((length, width), BF16),
            vmem((heads // 2, blocks, 2 * BLOCK, span), BF16),
            vmem((slots, width), BF16),
            vmem((2 * in_half.shape[0], 3 * width), BF16),
            vmem((2 * out_half.shape[0], width), BF16),
            dma((9,)),
            vmem((heads // 2, 2 * BLOCK, span), F32),
            vmem((blocks, BLOCK, span), F32),
            vmem((length, width), BF16),
            vmem((length, width), BF16),
            vmem((slots, width), BF16),
            vmem(small_part.shape, BF16),
            dma((3,)),
            dma((3,)),
            dma((owners,)),
            dma((owners,)),
        ],
        compiler_params=params(collective_id=0, has_side_effects=True),
        cost_estimate=pl.CostEstimate(
            flops=12 * 10**9, bytes_accessed=2 * 10**7, transcendentals=2 * 10**6
        ),
        name="attention_forward",
    )(x, cot, segments, route_rows, place_rows, in_half, out_half, small_part)


def backward(operands, y_rows, owners, experts, buckets, digits):
    x, probs, small = operands[0], operands[6], operands[14]
    length, width = x.shape
    pairs, blocks, _, span = probs.shape
    slots = operands[10].shape[0]
    share = width // 2
    columns = width // 2
    piece_rows = share * 2 // owners
    any_, near = pl.BlockSpec(memory_space=pl.ANY), pl.BlockSpec(memory_space=pltpu.VMEM)
    shape, vmem, dma = jax.ShapeDtypeStruct, pltpu.VMEM, pltpu.SemaphoreType.DMA
    pieces = (COLORS, owners, piece_rows, columns)
    return pl.pallas_call(
        functools.partial(backward_kernel, owners, experts, buckets, digits),
        out_shape=(
            shape((length, width), F32),
            shape((length, width), F32),
            shape((share, 3 * width), F32),
            shape((share, width), F32),
            shape(small.shape, F32),
        ),
        in_specs=[any_] * 7 + [near] * 3 + [any_, near, any_, any_, near, any_],
        out_specs=tuple(whole(5)),
        scratch_shapes=[
            vmem((slots, width), BF16),
            vmem((length, width), F32),
            vmem((length, width), F32),
            vmem((length, width), BF16),
            vmem((length, width), BF16),
            vmem((width, width), BF16),
            vmem((length, width), F32),
            vmem((length, 3 * width), BF16),
            vmem(probs.shape, BF16),
            vmem((width, 3 * width), BF16),
            dma((10,)),
            vmem((length, width), BF16),
            vmem((length, 3 * width), BF16),
            vmem((width, length), BF16),
            vmem((length, 2 * (width // (2 * pairs))), F32),
            vmem((length, 2 * (width // (2 * pairs))), F32),
            vmem((pairs, 2 * BLOCK, span), F32),
            vmem((2 * pairs, span + BLOCK), F32),
            vmem((width, 4 * width), F32),
            vmem(small.shape, F32),
            vmem((sum(digits) - len(digits) + 1,) + small.shape, F32),
            vmem((slots, width), BF16),
            vmem(pieces, BF16),
            vmem((2,) + pieces, BF16),
            vmem(pieces, BF16),
            dma((owners,)),
            dma((owners,)),
            dma,
            dma((COLORS + 1,)),
            dma((COLORS + 1,)),
            dma((COLORS * 24,)),
            dma((COLORS * 24,)),
            dma((12,)),
            dma((12,)),
        ],
        compiler_params=pltpu.CompilerParams(
            vmem_limit_bytes=67043328, collective_id=2, has_side_effects=True
        ),
        cost_estimate=pl.CostEstimate(
            flops=25 * 10**9, bytes_accessed=3 * 10**7, transcendentals=2 * 10**6
        ),
        name="attention_backward",
    )(*operands, y_rows)


def expert_kernel(
    owners,
    x_ref, gate_ref, cot_ref, up_hbm, down_hbm,
    y_ref, home_ref, dot_ref, up_grad_ref, down_grad_ref,
    up, down, rows, cots, act, pre, out_sum, back_sum, back_rows, y_rows, gates, dots,
    up_ring, down_ring, up_got, down_got, up_out, down_out,
    weight_sem, cot_sem, own_sem, y_sem,
    x_send, x_recv, gate_send, gate_recv, back_send, back_recv, dot_send, dot_recv,
    ring_send, up_recv, down_recv, out_sem,
):
    me, core = lax.axis_index("expert"), lax.axis_index("dp")
    slots, width = rows.shape
    hidden = up.shape[1]
    capacity = slots // owners
    chunk = min(slots, 512)
    per = chunk // capacity
    tile = 256

    def block(index):
        return pl.ds(pl.multiple_of(index * capacity, capacity), capacity)

    load_up = pltpu.make_async_copy(up_hbm, up, weight_sem.at[0])
    load_down = pltpu.make_async_copy(down_hbm, down, weight_sem.at[1])
    load_cots = pltpu.make_async_copy(cot_ref, cots, cot_sem)
    load_up.start()
    load_down.start()
    load_cots.start()
    own_rows = pltpu.make_async_copy(x_ref.at[block(me)], rows.at[block(0)], own_sem.at[0])
    own_rows.start()
    greet(me, core, owners)

    def send_rows(step):
        peer = partner(me, step, owners, 1)
        return (
            remote(x_ref.at[block(peer)], rows.at[block(step)], x_send.at[step], x_recv.at[step], (peer, core)),
            remote(gate_ref.at[peer], gates.at[step], gate_send.at[step], gate_recv.at[step], (peer, core)),
        )

    def start_rows(step, carry):
        for copy in send_rows(step):
            copy.start()
        return carry

    early = owners - per if slots > 2 * chunk else owners
    lax.fori_loop(1, early, start_rows, 0)
    gates[0] = gate_ref[me]

    def send_back(step):
        peer = partner(me, step, owners, -1)
        return (
            remote(back_rows.at[block(step)], home_ref.at[block(me)], back_send.at[step], back_recv.at[step], (peer, core)),
            remote(dots.at[step], dot_ref.at[me], dot_send.at[step], dot_recv.at[step], (peer, core)),
        )

    def get_back(step):
        peer = partner(me, step, owners, 1)
        return (
            remote(back_rows.at[block(step)], home_ref.at[block(peer)], back_send.at[step], back_recv.at[step], (peer, core)),
            remote(dots.at[step], dot_ref.at[peer], dot_send.at[step], dot_recv.at[step], (peer, core)),
        )

    home_own = pltpu.make_async_copy(back_rows.at[block(0)], home_ref.at[block(me)], own_sem.at[1])
    y_copies = []
    for index in range(slots // chunk):
        first = index * per
        part = slice(index * chunk, (index + 1) * chunk)
        if index == 0:
            own_rows.wait()
            load_cots.wait()
            load_up.wait()
            load_down.wait()

        def arrive(step, carry):
            for copy in send_rows(step):
                copy.wait_recv()
            return carry

        lax.fori_loop(max(first, 1), first + per, arrive, 0)
        column = jnp.concatenate(
            [
                jnp.transpose(jnp.broadcast_to(gates[first + b], (BLOCK, capacity)))[:, 0:1]
                for b in range(per)
            ],
            axis=0,
        )
        out_sum[...] = jnp.zeros_like(out_sum)
        back_sum[...] = jnp.zeros_like(back_sum)

        def through(step, carry):
            columns = pl.ds(pl.multiple_of(step * 512, 512), 512)
            before = dot(rows[part, :], up[:, columns])
            act_grad = dot(cots[part, :], down[columns, :], 1, 1)
            chance = normal_cdf(before)
            value = before * chance
            slope = chance + before * (
                jnp.exp(-0.5 * before * before) * (1.0 / math.sqrt(2.0 * math.pi))
            )
            out_sum[...] += dot(value.astype(BF16), down[columns, :])
            act[part, columns] = (value * column).astype(BF16)
            pre_grad = (act_grad * slope * column).astype(BF16)
            pre[part, columns] = pre_grad
            back_sum[...] += dot(pre_grad, up[:, columns], 1, 1)
            return carry

        lax.fori_loop(0, hidden // 512, through, 0)
        back_rows[part, :] = back_sum[...].astype(BF16)
        produced = out_sum[...]
        inner = jnp.sum(produced * cots[part, :].astype(F32), axis=1, keepdims=True)
        spread = jnp.broadcast_to(inner, (chunk, BLOCK))
        for b in range(per):
            turned = jnp.transpose(spread[b * capacity : (b + 1) * capacity, :])
            dots[first + b] = turned[0:1, :]
        if index >= 2:
            y_copies[index - 2].wait()
        y_rows[index % 2] = (produced * column).astype(BF16)
        y_copy = pltpu.make_async_copy(y_rows.at[index % 2], y_ref.at[part], y_sem.at[index % 2])
        y_copy.start()
        y_copies.append(y_copy)

        def start_back(step, carry):
            for copy in send_back(step):
                copy.start()
            return carry

        lax.fori_loop(max(first, 1), first + per, start_back, 0)
        if index == 0:
            home_own.start()
            dot_ref[me] = dots[0]
            lax.fori_loop(early, owners, start_rows, 0)
    for y_copy in y_copies[-2:]:
        y_copy.wait()

    half = hidden // 2
    count = half // tile

    def columns_of(side, step):
        return pl.ds(pl.multiple_of(side * half + step * tile, tile), tile)

    def up_tile(side, step):
        return dot(rows[...], pre[:, columns_of(side, step)], 0, 0)

    def down_tile(side, step):
        return dot(act[:, columns_of(side, step)], cots[...], 0, 0)

    def up_copy(step):
        slot = lax.rem(step, 2)
        return remote(
            up_ring.at[slot], up_got.at[:, columns_of(0, step)], ring_send.at[slot], up_recv.at[step], (me, 1 - core)
        )

    def down_copy(step):
        slot = lax.rem(step, 2)
        return remote(
            down_ring.at[slot], down_got.at[columns_of(0, step), :], ring_send.at[2 + slot], down_recv.at[step], (me, 1 - core)
        )

    def give(step, carry):
        slot = lax.rem(step, 2)

        @pl.when(step >= 2)
        def _():
            up_copy(step - 2).wait_send()
            down_copy(step - 2).wait_send()

        up_ring[slot] = up_tile(1 - core, step).astype(BF16)
        up_copy(step).start()
        down_ring[slot] = down_tile(1 - core, step).astype(BF16)
        down_copy(step).start()
        return carry

    lax.fori_loop(0, count, give, 0)

    def up_write(step):
        slot = lax.rem(step, 2)
        return pltpu.make_async_copy(up_out.at[slot], up_grad_ref.at[:, columns_of(0, step)], out_sem.at[slot])

    def down_write(step):
        slot = lax.rem(step, 2)
        return pltpu.make_async_copy(down_out.at[slot], down_grad_ref.at[columns_of(0, step), :], out_sem.at[2 + slot])

    def take(step, carry):
        slot = lax.rem(step, 2)

        @pl.when(step >= 2)
        def _():
            up_write(step - 2).wait()
            down_write(step - 2).wait()

        mine = up_tile(core, step)
        up_copy(step).wait_recv()
        up_out[slot] = mine + up_got[:, columns_of(0, step)].astype(F32)
        up_write(step).start()
        mine = down_tile(core, step)
        down_copy(step).wait_recv()
        down_out[slot] = mine + down_got[columns_of(0, step), :].astype(F32)
        down_write(step).start()
        return carry

    lax.fori_loop(0, count, take, 0)

    for step in range(max(count - 2, 0), count):
        up_copy(step).wait_send()
        down_copy(step).wait_send()
        up_write(step).wait()
        down_write(step).wait()
    home_own.wait()

    def finish(step, carry):
        for copy in send_rows(step):
            copy.wait_send()
        for copy in send_back(step):
            copy.wait_send()
        for copy in get_back(step):
            copy.wait_recv()
        return carry

    lax.fori_loop(1, owners, finish, 0)


def experts_of(x_rows, gate_rows, cot_rows, up_matrix, down_matrix, owners):
    slots, width = x_rows.shape
    hidden = up_matrix.shape[1]
    capacity = slots // owners
    chunk, tile, half = min(slots, 512), 256, hidden // 2
    count = half // tile
    shape, vmem, dma = jax.ShapeDtypeStruct, pltpu.VMEM, pltpu.SemaphoreType.DMA
    anywhere = pl.BlockSpec(memory_space=pl.ANY)
    near = pl.BlockSpec(memory_space=pltpu.VMEM)
    return pl.pallas_call(
        functools.partial(expert_kernel, owners),
        out_shape=(
            shape((slots, width), BF16),
            shape((slots, width), BF16),
            shape((owners, 1, capacity), F32),
            shape((width, half), F32),
            shape((half, width), F32),
        ),
        in_specs=[anywhere, near, anywhere, anywhere, anywhere],
        out_specs=(anywhere, anywhere, near, anywhere, anywhere),
        scratch_shapes=[
            vmem((width, hidden), BF16),
            vmem((hidden, width), BF16),
            vmem((slots, width), BF16),
            vmem((slots, width), BF16),
            vmem((slots, hidden), BF16),
            vmem((slots, hidden), BF16),
            vmem((chunk, width), F32),
            vmem((chunk, width), F32),
            vmem((slots, width), BF16),
            vmem((2, chunk, width), BF16),
            vmem((owners, 1, capacity), F32),
            vmem((owners, 1, capacity), F32),
            vmem((2, width, tile), BF16),
            vmem((2, tile, width), BF16),
            vmem((width, half), BF16),
            vmem((half, width), BF16),
            vmem((2, width, tile), F32),
            vmem((2, tile, width), F32),
            dma((2,)),
            dma,
            dma((2,)),
            dma((2,)),
        ]
        + [dma((owners,))] * 8
        + [dma((4,)), dma((count,)), dma((count,)), dma((4,))],
        compiler_params=pltpu.CompilerParams(
            vmem_limit_bytes=67043328, collective_id=1, has_side_effects=True
        ),
        cost_estimate=pl.CostEstimate(
            flops=58 * 10**9, bytes_accessed=4 * 10**7, transcendentals=2 * 10**7
        ),
        name="experts",
    )(x_rows, gate_rows, cot_rows, up_matrix, down_matrix)


def shards(
    block_input,
    cotangent,
    segment_ids,
    routes,
    slot_ids,
    attention_in,
    attention_out,
    router_weight,
    first_gain,
    second_gain,
    bias_table,
    expert_up,
    expert_down,
):
    length, width = block_input.shape
    owners = lax.axis_size("expert")
    capacity = 4 * length // owners
    experts = router_weight.shape[1]
    heads = bias_table.shape[1]
    member = lax.axis_index("dp")
    pair_size = lax.axis_size("dp")
    buckets = pair_size * bias_table.shape[0]
    share = width // pair_size
    inner = owners // 4
    side = math.isqrt(inner)
    digits = (side, inner // side, 4)

    rows = -(-(experts + 2 + heads) // 16) * 16
    wide_part = jnp.concatenate([router_weight.T, first_gain[None], second_gain[None]], axis=0)
    small_part = jnp.zeros((rows, width), BF16)
    small_part = lax.dynamic_update_slice(small_part, wide_part, (0, member * share))
    small_part = lax.dynamic_update_slice(
        small_part, bias_table.T, (experts + 2, member * bias_table.shape[0])
    )
    route_rows = routes.T
    place_rows = route_rows * capacity + slot_ids.T
    (
        hidden_state, normed_two, triple, context, probs, gates,
        x_rows, gate_rows, cot_rows, full_in, full_out, small,
    ) = forward(
        block_input, cotangent, segment_ids, route_rows, place_rows, attention_in, attention_out, small_part,
        owners, experts, buckets, heads,
    )
    y_rows, home_rows, gate_dots, up_share, down_share = experts_of(
        x_rows, gate_rows, cot_rows, expert_up[0], expert_down[0], owners
    )
    block_output, input_grad, in_share, out_share, small_sum = backward(
        (
            block_input, cotangent, hidden_state, normed_two, triple, context, probs, gates, route_rows, place_rows,
            home_rows, gate_dots, full_in, full_out, small,
        ),
        y_rows, owners, experts, buckets, digits,
    )
    mine = lax.dynamic_slice_in_dim(small_sum[: experts + 2], member * share, share, 1)
    bias_grad = lax.dynamic_slice(
        small_sum, (experts + 2, member * bias_table.shape[0]), (heads, bias_table.shape[0])
    )
    return (
        block_output,
        input_grad,
        in_share,
        out_share,
        mine[:experts].T,
        mine[experts],
        mine[experts + 1],
        bias_grad.T,
        up_share[None],
        down_share[None],
    )


def solution(mesh):
    rows = P(("expert", "dp"), None)
    return jax.shard_map(
        shards,
        mesh=mesh,
        in_specs=(
            rows,
            rows,
            rows,
            rows,
            rows,
            P("dp", None),
            P("dp", None),
            P("dp", None),
            P("dp"),
            P("dp"),
            P("dp", None),
            P("expert", None, None),
            P("expert", None, None),
        ),
        out_specs=(
            rows,
            rows,
            P("dp", None),
            P("dp", None),
            P("dp", None),
            P("dp"),
            P("dp"),
            P("dp", None),
            P("expert", None, "dp"),
            P("expert", "dp", None),
        ),
        check_vma=False,
    )
```

```python
import functools
import math

import jax
import jax.numpy as jnp
import numpy as np
from jax import lax
from jax.experimental import pallas as pl
from jax.experimental.pallas import tpu as pltpu
from jax.sharding import PartitionSpec as P

EPS = 1e-06
F32 = jnp.float32
BF16 = jnp.bfloat16
BLOCK = 128
MASKED = -1e30


def reach_marks(buckets, reach_len):
    half_count = buckets // 2
    step_ids = np.arange(1, half_count)
    thresholds = np.floor(half_count * (reach_len / half_count) ** (step_ids / half_count))
    thresholds = np.maximum(thresholds, half_count + step_ids)
    return [int(mark) for mark in thresholds.astype(np.int32)]


def normal_cdf(argument):
    return 0.5 * (1.0 + jax.scipy.special.erf(argument * (1.0 / math.sqrt(2.0))))


def gelu_slope(argument):
    return normal_cdf(argument) + argument * (
        jnp.exp(-0.5 * argument * argument) * (1.0 / math.sqrt(2.0 * math.pi))
    )


def dot(left, right, left_dim=1, right_dim=0):
    return lax.dot_general(
        left, right, (((left_dim,), (right_dim,)), ((), ())), preferred_element_type=F32
    )


def bucket_hot(buckets, length, width):
    column = lax.broadcasted_iota(jnp.int32, (1, width), 1)
    distance = jnp.maximum(length // 2 + BLOCK - 1 - column, 0)
    bucket = jnp.minimum(distance, buckets // 2)
    for mark in reach_marks(buckets, length):
        bucket = bucket + jnp.where(distance >= mark, 1, 0)
    rows = lax.broadcasted_iota(jnp.int32, (buckets, width), 0)
    return jnp.where(rows == bucket, 1.0, 0.0)


def spans(length):
    reach = length // 2
    for block in range(length // BLOCK):
        low = max(0, block * BLOCK - reach)
        high = (block + 1) * BLOCK
        yield block, low, high, reach + BLOCK - (high - low)


def halves(pair):
    lane = lax.broadcasted_iota(jnp.int32, (1, pair.shape[1]), 1)
    first = lane < pair.shape[1] // 2
    zero = jnp.zeros_like(pair)
    return jnp.where(first, pair, zero), jnp.where(first, zero, pair)


def hot_rows(place_ref, first, count):
    ids = first + lax.broadcasted_iota(jnp.int32, (count, place_ref.shape[1]), 0)
    return ids == place_ref[0:1, :], ids == place_ref[1:2, :]


def bf16_of(flags):
    return jnp.where(flags, 1.0, 0.0).astype(BF16)


def pieces_of(row):
    parts = []
    for _ in range(3):
        piece = row.astype(BF16).astype(F32)
        parts.append(piece)
        row = row - piece
    parts.append(jnp.zeros((5, row.shape[1]), F32))
    return jnp.concatenate(parts, axis=0).astype(BF16)


def forward_kernel(
    owners, experts, buckets,
    x_ref, cot_ref, segment_ref, route_ref, place_ref, in_half_ref, out_half_ref, small_part_ref,
    hidden_hbm, normed_hbm, triple_hbm, context_hbm, prob_hbm, gate_ref,
    x_rows_hbm, gate_rows_ref, cot_rows_ref, in_hbm, out_hbm, small_ref,
    hidden_ref, normed_ref, triple_ref, context_ref, prob_ref, x_rows_ref, in_ref, out_ref, store_sem,
    table_ref, mask_ref, one_ref, half_ref, cot_send_ref, small_got_ref,
    weight_send, weight_recv, cot_send, cot_recv,
):
    me, core = lax.axis_index("expert"), lax.axis_index("dp")
    length, width = x_ref.shape
    heads = 2 * prob_ref.shape[0]
    pair = 2 * (width // heads)
    pairs = heads // 2
    reach = length // 2
    span = reach + BLOCK
    scale = 1.0 / math.sqrt(width // heads)
    slots = x_rows_ref.shape[0]
    capacity = slots // owners
    share = in_half_ref.shape[0]

    def block(index):
        return pl.ds(pl.multiple_of(index * capacity, capacity), capacity)

    stores = []

    def store(source, target):
        copy = pltpu.make_async_copy(source, target, store_sem.at[len(stores)])
        copy.start()
        stores.append(copy)

    mine = pl.ds(pl.multiple_of(core * share, share), share)
    half_ref[...] = cot_ref[...].astype(BF16)
    greet(me, core, owners)
    weights = [
        remote(in_half_ref, in_ref.at[mine], weight_send.at[0], weight_recv.at[0], (me, 1 - core)),
        remote(out_half_ref, out_ref.at[mine], weight_send.at[1], weight_recv.at[1], (me, 1 - core)),
        remote(small_part_ref, small_got_ref, weight_send.at[2], weight_recv.at[2], (me, 1 - core)),
    ]
    for copy in weights:
        copy.start()
    in_ref[mine, :] = in_half_ref[...]
    out_ref[mine, :] = out_half_ref[...]

    def cot_copy(step):
        peer = partner(me, step, owners, 1)
        return remote(
            cot_send_ref.at[block(step)], cot_rows_ref.at[block(step)], cot_send.at[step], cot_recv.at[step], (peer, core)
        )

    def dispatch(step, carry):
        peer = partner(me, step, owners, 1)
        first, second = hot_rows(place_ref, peer * capacity, capacity)
        cot_send_ref[block(step), :] = dot(bf16_of(first | second), half_ref[...]).astype(BF16)

        @pl.when(step >= 2)
        def _():
            cot_copy(step - 1).start()

        return carry

    lax.fori_loop(0, owners, dispatch, 0)
    cot_copy(owners - 1).start()
    store(cot_send_ref.at[block(0)], cot_rows_ref.at[block(0)])

    x = x_ref[...]
    rms = lax.rsqrt(jnp.mean(x * x, axis=1, keepdims=True) + EPS)
    for copy in weights:
        copy.wait_recv()
    small_ref[...] = small_part_ref[...] + small_got_ref[...]
    store(in_ref, in_hbm)
    store(out_ref, out_hbm)
    one_ref[...] = (x * rms * small_ref[experts : experts + 1, :].astype(F32)).astype(BF16)

    chunk = 3 * pair

    def project(step, carry):
        columns = pl.ds(pl.multiple_of(step * chunk, BLOCK), chunk)
        triple_ref[:, columns] = dot(one_ref[...], in_ref[:, columns]).astype(BF16)
        return carry

    lax.fori_loop(0, 3 * width // chunk, project, 0)

    store(triple_ref, triple_hbm)
    wide = span + BLOCK
    bias = small_ref[experts + 2 : experts + 2 + heads, 0:buckets]
    by_column = dot(bias, bucket_hot(buckets, length, wide).astype(BF16))
    for head in range(heads):
        spread = jnp.broadcast_to(by_column[head : head + 1, :], (BLOCK, wide))
        rolled = pltpu.roll(spread, wide - BLOCK + 1, 1, stride=1, stride_axis=0)
        table_ref[head // 2, (head % 2) * BLOCK : (head % 2 + 1) * BLOCK, :] = rolled[:, :span]

    segment_row = segment_ref[...].astype(F32)
    segment_column = jnp.transpose(jnp.broadcast_to(segment_row, (BLOCK, length)))
    for index, low, high, skip in spans(length):
        rows = index * BLOCK + lax.broadcasted_iota(jnp.int32, (BLOCK, high - low), 0)
        columns = low + lax.broadcasted_iota(jnp.int32, (BLOCK, high - low), 1)
        own = segment_column[index * BLOCK : (index + 1) * BLOCK, 0:1]
        allowed = (rows >= columns) & (own == segment_row[:, low:high])
        mask_ref[index, :, skip:] = jnp.where(allowed, 0.0, MASKED)

    def attend(step, carry):
        base = pl.multiple_of(step * pair, pair)
        query_columns = pl.ds(base, pair)
        key_columns = pl.ds(pl.multiple_of(width + base, pair), pair)
        value_columns = pl.ds(pl.multiple_of(2 * width + base, pair), pair)
        for index, low, high, skip in spans(length):
            rows = slice(index * BLOCK, (index + 1) * BLOCK)
            query = triple_ref[rows, query_columns] * jnp.asarray(scale, BF16)
            stacked = jnp.concatenate(halves(query), axis=0)
            scores = dot(stacked, triple_ref[low:high, key_columns], 1, 1)
            mask = mask_ref[index, :, skip:]
            scores = scores + table_ref[step, :, skip:] + jnp.concatenate([mask, mask], axis=0)
            top = jnp.max(scores, axis=1, keepdims=True)
            weight = jnp.exp(scores - top)
            prob = weight * (1.0 / jnp.sum(weight, axis=1, keepdims=True))
            half = prob.astype(BF16)
            prob_ref[step, index, :, skip:] = half
            first, second = halves(triple_ref[low:high, value_columns])
            context = dot(half[:BLOCK], first) + dot(half[BLOCK:], second)
            context_ref[rows, query_columns] = context.astype(BF16)
        return carry

    lax.fori_loop(0, pairs, attend, 0)
    store(prob_ref, prob_hbm)
    store(context_ref, context_hbm)

    hidden = x_ref[...] + dot(context_ref[...], out_ref[...])
    hidden_ref[...] = hidden
    store(hidden_ref, hidden_hbm)
    rms = lax.rsqrt(jnp.mean(hidden * hidden, axis=1, keepdims=True) + EPS)
    normed = (hidden * rms * small_ref[experts + 1 : experts + 2, :].astype(F32)).astype(BF16)
    normed_ref[...] = normed
    store(normed_ref, normed_hbm)
    logits = dot(small_ref[0:experts, :], normed, 1, 1)
    expert_ids = lax.broadcasted_iota(jnp.int32, logits.shape, 0)
    first = jnp.sum(jnp.where(expert_ids == route_ref[0:1, :], logits, 0.0), axis=0, keepdims=True)
    second = jnp.sum(jnp.where(expert_ids == route_ref[1:2, :], logits, 0.0), axis=0, keepdims=True)
    gate_first = 1.0 / (1.0 + jnp.exp(second - first))
    gate_second = 1.0 / (1.0 + jnp.exp(first - second))
    gate_ref[0:1, :] = gate_first
    gate_ref[1:2, :] = gate_second
    first_pieces, second_pieces = pieces_of(gate_first), pieces_of(gate_second)

    def outgoing(step, carry):
        first, second = hot_rows(place_ref, step * capacity, capacity)
        x_rows_ref[block(step), :] = dot(bf16_of(first | second), normed_ref[...]).astype(BF16)
        gates = dot(first_pieces, bf16_of(first), 1, 1) + dot(second_pieces, bf16_of(second), 1, 1)
        gate_rows_ref[step] = jnp.sum(gates, axis=0, keepdims=True)
        return carry

    lax.fori_loop(0, owners, outgoing, 0)
    store(x_rows_ref, x_rows_hbm)

    def finish(step, carry):
        cot_copy(step).wait()
        return carry

    lax.fori_loop(1, owners, finish, 0)
    for copy in weights:
        copy.wait_send()
    for copy in stores:
        copy.wait()


def backward_kernel(
    owners, experts, buckets, digits,
    x_hbm, cot_hbm, hidden_hbm, normed_hbm, triple_hbm, context_hbm, prob_hbm, gate_ref, route_ref, place_ref,
    home_hbm, dot_ref, in_hbm, out_hbm, small_ref, y_hbm,
    block_ref, input_grad_ref, in_share_ref, out_share_ref, small_sum_ref,
    home_ref, cot_ref, hidden_ref, normed_ref, context_ref, out_ref, x_ref, triple_ref, prob_ref, in_ref, load_sem,
    context_grad_ref, triple_grad_ref, turned_ref, key_ref, value_ref, diagonal_ref, sums_ref,
    grads_ref, small_mine_ref, small_got_ref, came_ref, work_ref, got_ref, final_ref,
    y_send, y_recv, own_sem, core_send, core_recv, ring_send, ring_recv, small_send, small_recv,
):
    me, core = lax.axis_index("expert"), lax.axis_index("dp")
    hidden_grad_ref = block_ref
    length, width = x_ref.shape
    pairs = prob_ref.shape[0]
    heads = 2 * pairs
    pair = 2 * (width // heads)
    reach = length // 2
    span = reach + BLOCK
    scale = 1.0 / math.sqrt(width // heads)
    slots = home_ref.shape[0]
    capacity = slots // owners

    def block(index):
        return pl.ds(pl.multiple_of(index * capacity, capacity), capacity)

    loads = [
        pltpu.make_async_copy(source, target, load_sem.at[index])
        for index, (source, target) in enumerate(
            (
                (home_hbm, home_ref),
                (cot_hbm, cot_ref),
                (hidden_hbm, hidden_ref),
                (normed_hbm, normed_ref),
                (context_hbm, context_ref),
                (out_hbm, out_ref),
                (x_hbm, x_ref),
                (triple_hbm, triple_ref),
                (prob_hbm, prob_ref),
                (in_hbm, in_ref),
            )
        )
    ]
    for copy in loads:
        copy.start()
    own_y = pltpu.make_async_copy(y_hbm.at[block(0)], came_ref.at[block(me)], own_sem)
    own_y.start()
    greet(me, core, owners)

    def y_copy(step, sign):
        peer = partner(me, step, owners, -1)
        target = me if sign < 0 else partner(me, step, owners, 1)
        return remote(
            y_hbm.at[block(step)], came_ref.at[block(target)], y_send.at[step], y_recv.at[step], (peer, core)
        )

    def start_y(step, carry):
        y_copy(step, -1).start()
        return carry

    lax.fori_loop(1, owners, start_y, 0)

    def column(row):
        return jnp.transpose(jnp.broadcast_to(row, (BLOCK, length)))

    place_first = column(place_ref[0:1, :].astype(F32))
    place_second = column(place_ref[1:2, :].astype(F32))
    lane = lax.broadcasted_iota(jnp.int32, (length, BLOCK), 1).astype(F32)
    wide_k = 2 * BLOCK

    def hot_columns(group):
        first = (group * BLOCK).astype(F32) if hasattr(group, "astype") else float(group * BLOCK)
        return place_first - first == lane, place_second - first == lane

    def gather_rows(rows_ref, base_ref):
        def add(group, carry):
            left = hot_columns(2 * group)
            right = hot_columns(2 * group + 1)
            hot = jnp.concatenate([bf16_of(left[0] | left[1]), bf16_of(right[0] | right[1])], axis=1)
            rows = pl.ds(pl.multiple_of(group * wide_k, wide_k), wide_k)
            base_ref[...] += dot(hot, rows_ref[rows, :])
            return carry

        lax.fori_loop(0, slots // wide_k, add, 0)

    per_row = BLOCK // capacity

    def dot_row(group):
        if per_row == 1:
            return dot_ref[group]
        return jnp.concatenate([dot_ref[group * per_row + b] for b in range(per_row)], axis=1)

    def pick(group, carry):
        first, second = hot_columns(group)
        row = dot_row(group)
        return carry + jnp.where(first, row, 0.0) - jnp.where(second, row, 0.0)

    picked = lax.fori_loop(0, slots // BLOCK, pick, jnp.zeros((length, BLOCK), F32))
    difference = jnp.sum(picked, axis=1, keepdims=True)
    gates = column(gate_ref[0:1, :]) * column(gate_ref[1:2, :])
    ids = lax.broadcasted_iota(jnp.int32, (length, BLOCK), 1)
    pick_first = jnp.where(column(route_ref[0:1, :].astype(F32)).astype(jnp.int32) == ids, 1.0, 0.0)
    pick_second = jnp.where(column(route_ref[1:2, :].astype(F32)).astype(jnp.int32) == ids, 1.0, 0.0)
    logit_grad = ((pick_first - pick_second) * gates * difference).astype(BF16)

    small_mine_ref[...] = jnp.zeros_like(small_mine_ref)
    for copy in loads[:6]:
        copy.wait()
    hidden_grad_ref[...] = dot(logit_grad[:, 0:experts], small_ref[0:experts, :])
    gather_rows(home_ref, hidden_grad_ref)
    small_mine_ref[0:experts, :] = dot(logit_grad, normed_ref[...], 0, 0)[0:experts, :]

    def settle(step, carry):
        rows = pl.ds(pl.multiple_of(step * BLOCK, BLOCK), BLOCK)
        normed_grad = hidden_grad_ref[rows, :]
        hidden = hidden_ref[rows, :]
        rms = lax.rsqrt(jnp.mean(hidden * hidden, axis=1, keepdims=True) + EPS)
        scaled = normed_grad * small_ref[experts + 1 : experts + 2, :].astype(F32)
        inner = jnp.mean(scaled * hidden, axis=1, keepdims=True)
        hidden_grad_ref[rows, :] = cot_ref[rows, :] + (rms * scaled - hidden * (rms * rms * rms) * inner)
        return carry + jnp.sum(normed_grad * (hidden * rms), axis=0, keepdims=True)

    small_mine_ref[experts + 1 : experts + 2, :] = lax.fori_loop(
        0, length // BLOCK, settle, jnp.zeros((1, width), F32)
    )

    residual = hidden_grad_ref[...].astype(BF16)
    grads_ref[:, 3 * width :] = dot(jnp.transpose(context_ref[...]), residual)
    advance, advance_small = reducer(
        me, core, digits, grads_ref, in_share_ref, out_share_ref, small_mine_ref, small_got_ref, small_sum_ref,
        work_ref, got_ref, final_ref, core_send, core_recv, ring_send, ring_recv, small_send, small_recv,
    )
    advance(3)
    context_grad_ref[...] = dot(residual, out_ref[...], 1, 1).astype(BF16)
    diagonal_ref[...] = jnp.zeros_like(diagonal_ref)
    for copy in loads[6:]:
        copy.wait()
    x = x_ref[...]
    rms = lax.rsqrt(jnp.mean(x * x, axis=1, keepdims=True) + EPS)
    gain = small_ref[experts : experts + 1, :].astype(F32)
    turned_ref[...] = jnp.transpose((x * rms * gain).astype(BF16))

    def attend(step, carry):
        base = pl.multiple_of(step * pair, pair)
        query_columns = pl.ds(base, pair)
        key_columns = pl.ds(pl.multiple_of(width + base, pair), pair)
        value_columns = pl.ds(pl.multiple_of(2 * width + base, pair), pair)
        key_ref[...] = jnp.zeros_like(key_ref)
        value_ref[...] = jnp.zeros_like(value_ref)
        for index, low, high, skip in spans(length):
            rows = slice(index * BLOCK, (index + 1) * BLOCK)
            query = triple_ref[rows, query_columns] * jnp.asarray(scale, BF16)
            query = jnp.concatenate(halves(query), axis=0)
            grad = jnp.concatenate(halves(context_grad_ref[rows, query_columns]), axis=0)
            half = prob_ref[step, index, :, skip:]
            prob = half.astype(F32)
            prob_grad = dot(grad, triple_ref[low:high, value_columns], 1, 1)
            norm = 1.0 / jnp.sum(prob, axis=1, keepdims=True)
            row_dot = norm * jnp.sum(prob * prob_grad, axis=1, keepdims=True)
            score_grad = (prob * norm) * (prob_grad - row_dot)
            diagonal_ref[step, :, skip:] += score_grad
            score_half = score_grad.astype(BF16)
            first, second = halves(triple_ref[low:high, key_columns])
            query_grad = dot(score_half[:BLOCK], first) + dot(score_half[BLOCK:], second)
            triple_grad_ref[rows, query_columns] = (query_grad * scale).astype(BF16)
            key_ref[low:high, :] += dot(score_half, query, 0, 0)
            value_ref[low:high, :] += dot(half, grad, 0, 0)
        triple_grad_ref[:, key_columns] = key_ref[...].astype(BF16)
        triple_grad_ref[:, value_columns] = value_ref[...].astype(BF16)
        return carry

    groups = COLORS - 1
    part = width // groups
    for group in range(groups):
        lax.fori_loop(group * pairs // groups, (group + 1) * pairs // groups, attend, 0)
        for color in [3, *range(group)]:
            advance(color)

        def weigh(section, carry):
            source = pl.ds(pl.multiple_of(section * width + group * part, BLOCK), part)
            target = pl.ds(pl.multiple_of(group * width + section * part, BLOCK), part)
            grads_ref[:, target] = dot(turned_ref[...], triple_grad_ref[:, source])
            return carry

        lax.fori_loop(0, 3, weigh, 0)
        advance(group)

    def finish(step, carry):
        rows = pl.ds(pl.multiple_of(step * BLOCK, BLOCK), BLOCK)
        normed_grad = dot(triple_grad_ref[rows, :], in_ref[...], 1, 1)
        part = x_ref[rows, :]
        scaling = lax.rsqrt(jnp.mean(part * part, axis=1, keepdims=True) + EPS)
        scaled = normed_grad * gain
        inner = jnp.mean(scaled * part, axis=1, keepdims=True)
        input_grad_ref[rows, :] = hidden_grad_ref[rows, :] + (
            scaling * scaled - part * (scaling * scaling * scaling) * inner
        )
        return carry + jnp.sum(normed_grad * (part * scaling), axis=0, keepdims=True)

    small_mine_ref[experts : experts + 1, :] = lax.fori_loop(
        0, length // BLOCK, finish, jnp.zeros((1, width), F32)
    )

    for color in (2, 1, 0, 3):
        advance(color)
    wide = span + BLOCK
    row_ids = lax.broadcasted_iota(jnp.int32, (BLOCK, wide), 0)
    for head in range(heads):
        sheet = diagonal_ref[head // 2, (head % 2) * BLOCK : (head % 2 + 1) * BLOCK, :]
        sheet = jnp.concatenate([sheet, jnp.zeros((BLOCK, BLOCK), F32)], axis=1)
        sheet = pltpu.roll(sheet, BLOCK - 1, 1)
        step = 1
        while step < BLOCK:
            sheet = jnp.where((row_ids & step) != 0, pltpu.roll(sheet, wide - step, 1), sheet)
            step *= 2
        sums_ref[head : head + 1, :] = jnp.sum(sheet, axis=0, keepdims=True)
    hot = bucket_hot(buckets, length, wide).astype(BF16)
    rest = sums_ref[...]
    total = jnp.zeros((heads, buckets), F32)
    for _ in range(3):
        piece = rest.astype(BF16)
        total = total + dot(piece, hot, 1, 1)
        rest = rest - piece.astype(F32)
    small_mine_ref[experts + 2 : experts + 2 + heads, 0:buckets] = total

    def finish_y(step, carry):
        y_copy(step, -1).wait_send()
        y_copy(step, 1).wait_recv()
        return carry

    for turn in range(2 * len(digits) + 2):
        for color in (2, 1, 0, 3):
            advance(color)
        advance_small()
        if turn == 3:
            own_y.wait()
            lax.fori_loop(1, owners, finish_y, 0)
            block_ref[...] = hidden_ref[...]
            gather_rows(came_ref, block_ref)


COLORS = 4


def reducer(
    me, core, digits, grads_ref, in_share_ref, out_share_ref, small_mine_ref, small_got_ref, small_sum_ref,
    work_ref, got_ref, final_ref, core_send, core_recv, ring_send, ring_recv, small_send, small_recv,
):
    _, many, rows, columns = work_ref.shape
    share, width = out_share_ref.shape
    groups = COLORS - 1
    section = width // groups
    down = share // rows
    strides = []
    stride = 1
    for size in digits:
        strides.append(stride)
        stride *= size
    place = [lax.rem(lax.div(me, strides[axis]), digits[axis]) for axis in range(len(digits))]
    orders = [[0, 1, 2], [1, 0, 2]]
    other = (me, 1 - core)

    def sheets(color, side):
        for across in range(width // columns):
            sheet = grads_ref[
                pl.ds(pl.multiple_of(side * share, share), share),
                color * width + across * columns : color * width + (across + 1) * columns,
            ]
            for step in range(down):
                yield across * down + step, sheet[step * rows : (step + 1) * rows, :]

    def swap(color):
        for index, value in sheets(color, 1 - core):
            work_ref[color, index] = value.astype(BF16)
        return [remote(work_ref.at[color], got_ref.at[0, color], core_send.at[color], core_recv.at[color], other)]

    def swapped(color):
        for index, value in sheets(color, core):
            work_ref[color, index] = (value + got_ref[0, color, index].astype(F32)).astype(BF16)

    def settled(color):
        for index in range(many):
            across, step = index // down, index % down
            low = step * rows
            value = final_ref[color, index].astype(F32)
            if color == groups:
                out_share_ref[low : low + rows, across * columns : (across + 1) * columns] = value
                continue
            for left in range(0, columns, BLOCK):
                start = across * columns + left
                target = start // section * width + color * section + start % section
                in_share_ref[low : low + rows, target : target + BLOCK] = value[:, left : left + BLOCK]

    def peer_of(axis, ahead):
        digit = lax.rem(place[axis] + ahead, digits[axis])
        return digit, (me + (digit - place[axis]) * strides[axis], core)

    levels = []
    for color in range(COLORS):
        order = orders[color % 2]
        base, extent, landing, seen = jnp.int32(0), many, 0, []
        for axis in order:
            part = extent // digits[axis]
            seen.append((axis, base, part, landing))
            base = base + place[axis] * part
            extent = part
            landing += part * (digits[axis] - 1)
        levels.append(seen)

    def sem_of(color, level, ahead, way):
        return ((color * 3 + level) * 4 + ahead) * 2 + way

    def scatter(color, level):
        axis, base, part, landing = levels[color][level]
        copies = []
        for ahead in range(1, digits[axis]):
            digit, device = peer_of(axis, ahead)
            index = sem_of(color, level, ahead, 0)
            copies.append(
                remote(
                    work_ref.at[color, pl.ds(base + digit * part, part)],
                    got_ref.at[1, color, pl.ds(landing + (ahead - 1) * part, part)],
                    ring_send.at[index], ring_recv.at[index], device,
                )
            )
        return copies

    def scattered(color, level):
        axis, base, part, landing = levels[color][level]
        mine = base + place[axis] * part
        target = final_ref if level == len(digits) - 1 else work_ref

        def add(step, carry):
            value = work_ref[color, mine + step].astype(F32)
            for ahead in range(1, digits[axis]):
                value = value + got_ref[1, color, landing + (ahead - 1) * part + step].astype(F32)
            target[color, mine + step] = value.astype(BF16)
            return carry

        lax.fori_loop(0, part, add, 0)

    def gather(color, level):
        axis, base, part, _ = levels[color][level]
        mine = base + place[axis] * part
        copies = []
        for ahead in range(1, digits[axis]):
            _, device = peer_of(axis, ahead)
            index = sem_of(color, level, ahead, 1)
            copies.append(
                remote(
                    final_ref.at[color, pl.ds(mine, part)], final_ref.at[color, pl.ds(mine, part)],
                    ring_send.at[index], ring_recv.at[index], device,
                )
            )
        return copies

    def small_copies(axis):
        copies = []
        for ahead in range(1, digits[axis]):
            _, device = peer_of(axis, ahead)
            index = sum(digits[:axis]) - axis + ahead
            copies.append(
                remote(small_sum_ref, small_got_ref.at[index], small_send.at[index], small_recv.at[index], device)
            )
        return copies

    depth = len(digits)
    stage, flight = [0] * COLORS, [()] * COLORS

    def advance(color):
        now = stage[color]
        if now > 2 * depth + 1:
            return
        for copy in flight[color]:
            copy.wait()
        if now == 1:
            swapped(color)
        elif 1 < now <= depth + 1:
            scattered(color, now - 2)
        elif now == 2 * depth + 1:
            settled(color)
        if now == 0:
            flight[color] = swap(color)
        elif now <= depth:
            flight[color] = scatter(color, now - 1)
        elif now <= 2 * depth:
            flight[color] = gather(color, 2 * depth - now)
        else:
            flight[color] = ()
        for copy in flight[color]:
            copy.start()
        stage[color] = now + 1

    small_state = [0, ()]

    def advance_small():
        now, flying = small_state
        if now > depth + 1:
            return
        for copy in flying:
            copy.wait()
        if now == 1:
            small_sum_ref[...] = small_mine_ref[...] + small_got_ref[0]
        elif now > 1:
            value = small_sum_ref[...]
            for ahead in range(1, digits[now - 2]):
                value = value + small_got_ref[sum(digits[: now - 2]) - (now - 2) + ahead]
            small_sum_ref[...] = value
        if now == 0:
            flying = [
                remote(
                    small_mine_ref, small_got_ref.at[0], core_send.at[COLORS], core_recv.at[COLORS], other
                )
            ]
        elif now <= depth:
            flying = small_copies(now - 1)
        else:
            flying = ()
        for copy in flying:
            copy.start()
        small_state[:] = now + 1, flying

    return advance, advance_small


MESH = pl.DeviceIdType.MESH
GROUP = 4


def partner(me, step, owners, sign):
    groups = owners // GROUP
    outer = lax.rem(lax.div(me, GROUP) + sign * lax.div(step, GROUP) + groups, groups)
    inner = lax.rem(lax.rem(me, GROUP) + sign * lax.rem(step, GROUP) + GROUP, GROUP)
    return outer * GROUP + inner


def greet(me, core, owners):
    barrier = pltpu.get_barrier_semaphore()

    def signal(step, carry):
        pl.semaphore_signal(
            barrier, inc=1, device_id=(partner(me, step, owners, 1), core), device_id_type=MESH
        )
        return carry

    lax.fori_loop(1, owners, signal, 0)
    pl.semaphore_signal(barrier, inc=1, device_id=(me, 1 - core), device_id_type=MESH)
    pl.semaphore_wait(barrier, owners)


def remote(source, target, send, receive, device):
    return pltpu.make_async_remote_copy(
        src_ref=source, dst_ref=target, send_sem=send, recv_sem=receive,
        device_id=device, device_id_type=MESH,
    )


def whole(count):
    return [pl.BlockSpec(memory_space=pltpu.VMEM)] * count


def params(**extra):
    return pltpu.CompilerParams(vmem_limit_bytes=60 * 2**20, **extra)


def forward(x, cot, segments, route_rows, place_rows, in_half, out_half, small_part, owners, experts, buckets, heads):
    length, width = x.shape
    slots = 4 * length
    blocks, span = length // BLOCK, length // 2 + BLOCK
    any_, near = pl.BlockSpec(memory_space=pl.ANY), pl.BlockSpec(memory_space=pltpu.VMEM)
    shape, vmem, dma = jax.ShapeDtypeStruct, pltpu.VMEM, pltpu.SemaphoreType.DMA
    return pl.pallas_call(
        functools.partial(forward_kernel, owners, experts, buckets),
        out_shape=(
            shape((length, width), F32),
            shape((length, width), BF16),
            shape((length, 3 * width), BF16),
            shape((length, width), BF16),
            shape((heads // 2, blocks, 2 * BLOCK, span), BF16),
            shape((2, length), F32),
            shape((slots, width), BF16),
            shape((owners, 1, slots // owners), F32),
            shape((slots, width), BF16),
            shape((2 * in_half.shape[0], 3 * width), BF16),
            shape((2 * out_half.shape[0], width), BF16),
            shape(small_part.shape, BF16),
        ),
        in_specs=whole(8),
        out_specs=(any_, any_, any_, any_, any_, near, any_, near, any_, any_, any_, near),
        scratch_shapes=[
            vmem((length, width), F32),
            vmem((length, width), BF16),
            vmem((length, 3 * width), BF16),
            vmem((length, width), BF16),
            vmem((heads // 2, blocks, 2 * BLOCK, span), BF16),
            vmem((slots, width), BF16),
            vmem((2 * in_half.shape[0], 3 * width), BF16),
            vmem((2 * out_half.shape[0], width), BF16),
            dma((9,)),
            vmem((heads // 2, 2 * BLOCK, span), F32),
            vmem((blocks, BLOCK, span), F32),
            vmem((length, width), BF16),
            vmem((length, width), BF16),
            vmem((slots, width), BF16),
            vmem(small_part.shape, BF16),
            dma((3,)),
            dma((3,)),
            dma((owners,)),
            dma((owners,)),
        ],
        compiler_params=params(collective_id=0, has_side_effects=True),
        cost_estimate=pl.CostEstimate(
            flops=12 * 10**9, bytes_accessed=2 * 10**7, transcendentals=2 * 10**6
        ),
        name="attention_forward",
    )(x, cot, segments, route_rows, place_rows, in_half, out_half, small_part)


def backward(operands, y_rows, owners, experts, buckets, digits):
    x, probs, small = operands[0], operands[6], operands[14]
    length, width = x.shape
    pairs, blocks, _, span = probs.shape
    slots = operands[10].shape[0]
    share = width // 2
    columns = width // 2
    piece_rows = share * 2 // owners
    any_, near = pl.BlockSpec(memory_space=pl.ANY), pl.BlockSpec(memory_space=pltpu.VMEM)
    shape, vmem, dma = jax.ShapeDtypeStruct, pltpu.VMEM, pltpu.SemaphoreType.DMA
    pieces = (COLORS, owners, piece_rows, columns)
    return pl.pallas_call(
        functools.partial(backward_kernel, owners, experts, buckets, digits),
        out_shape=(
            shape((length, width), F32),
            shape((length, width), F32),
            shape((share, 3 * width), F32),
            shape((share, width), F32),
            shape(small.shape, F32),
        ),
        in_specs=[any_] * 7 + [near] * 3 + [any_, near, any_, any_, near, any_],
        out_specs=tuple(whole(5)),
        scratch_shapes=[
            vmem((slots, width), BF16),
            vmem((length, width), F32),
            vmem((length, width), F32),
            vmem((length, width), BF16),
            vmem((length, width), BF16),
            vmem((width, width), BF16),
            vmem((length, width), F32),
            vmem((length, 3 * width), BF16),
            vmem(probs.shape, BF16),
            vmem((width, 3 * width), BF16),
            dma((10,)),
            vmem((length, width), BF16),
            vmem((length, 3 * width), BF16),
            vmem((width, length), BF16),
            vmem((length, 2 * (width // (2 * pairs))), F32),
            vmem((length, 2 * (width // (2 * pairs))), F32),
            vmem((pairs, 2 * BLOCK, span), F32),
            vmem((2 * pairs, span + BLOCK), F32),
            vmem((width, 4 * width), F32),
            vmem(small.shape, F32),
            vmem((sum(digits) - len(digits) + 1,) + small.shape, F32),
            vmem((slots, width), BF16),
            vmem(pieces, BF16),
            vmem((2,) + pieces, BF16),
            vmem(pieces, BF16),
            dma((owners,)),
            dma((owners,)),
            dma,
            dma((COLORS + 1,)),
            dma((COLORS + 1,)),
            dma((COLORS * 24,)),
            dma((COLORS * 24,)),
            dma((12,)),
            dma((12,)),
        ],
        compiler_params=pltpu.CompilerParams(
            vmem_limit_bytes=67043328, collective_id=2, has_side_effects=True
        ),
        cost_estimate=pl.CostEstimate(
            flops=25 * 10**9, bytes_accessed=3 * 10**7, transcendentals=2 * 10**6
        ),
        name="attention_backward",
    )(*operands, y_rows)


def expert_kernel(
    owners,
    x_ref, gate_ref, cot_ref, up_hbm, down_hbm,
    y_ref, home_ref, dot_ref, up_grad_ref, down_grad_ref,
    up, down, rows, cots, act, pre, out_sum, back_sum, back_rows, y_rows, gates, dots,
    up_ring, down_ring, up_got, down_got, up_out, down_out,
    weight_sem, cot_sem, own_sem, y_sem,
    x_send, x_recv, gate_send, gate_recv, back_send, back_recv, dot_send, dot_recv,
    ring_send, up_recv, down_recv, out_sem,
):
    me, core = lax.axis_index("expert"), lax.axis_index("dp")
    slots, width = rows.shape
    hidden = up.shape[1]
    capacity = slots // owners
    chunk = min(slots, 512)
    per = chunk // capacity
    tile = 256

    def block(index):
        return pl.ds(pl.multiple_of(index * capacity, capacity), capacity)

    load_up = pltpu.make_async_copy(up_hbm, up, weight_sem.at[0])
    load_down = pltpu.make_async_copy(down_hbm, down, weight_sem.at[1])
    load_cots = pltpu.make_async_copy(cot_ref, cots, cot_sem)
    load_up.start()
    load_down.start()
    load_cots.start()
    own_rows = pltpu.make_async_copy(x_ref.at[block(me)], rows.at[block(0)], own_sem.at[0])
    own_rows.start()
    greet(me, core, owners)

    def send_rows(step):
        peer = partner(me, step, owners, 1)
        return (
            remote(x_ref.at[block(peer)], rows.at[block(step)], x_send.at[step], x_recv.at[step], (peer, core)),
            remote(gate_ref.at[peer], gates.at[step], gate_send.at[step], gate_recv.at[step], (peer, core)),
        )

    def start_rows(step, carry):
        for copy in send_rows(step):
            copy.start()
        return carry

    early = owners - per if slots > 2 * chunk else owners
    lax.fori_loop(1, early, start_rows, 0)
    gates[0] = gate_ref[me]

    def send_back(step):
        peer = partner(me, step, owners, -1)
        return (
            remote(back_rows.at[block(step)], home_ref.at[block(me)], back_send.at[step], back_recv.at[step], (peer, core)),
            remote(dots.at[step], dot_ref.at[me], dot_send.at[step], dot_recv.at[step], (peer, core)),
        )

    def get_back(step):
        peer = partner(me, step, owners, 1)
        return (
            remote(back_rows.at[block(step)], home_ref.at[block(peer)], back_send.at[step], back_recv.at[step], (peer, core)),
            remote(dots.at[step], dot_ref.at[peer], dot_send.at[step], dot_recv.at[step], (peer, core)),
        )

    home_own = pltpu.make_async_copy(back_rows.at[block(0)], home_ref.at[block(me)], own_sem.at[1])
    chunks = slots // chunk

    def y_copy(index):
        slot = lax.rem(index, 2)
        part = pl.ds(pl.multiple_of(index * chunk, chunk), chunk)
        return pltpu.make_async_copy(y_rows.at[slot], y_ref.at[part], y_sem.at[slot])

    def arrive(step, carry):
        for copy in send_rows(step):
            copy.wait_recv()
        return carry

    def start_back(step, carry):
        for copy in send_back(step):
            copy.start()
        return carry

    def process(index):
        first = index * per
        part = pl.ds(pl.multiple_of(index * chunk, chunk), chunk)
        column = jnp.concatenate(
            [
                jnp.transpose(jnp.broadcast_to(gates[first + b], (BLOCK, capacity)))[:, 0:1]
                for b in range(per)
            ],
            axis=0,
        )
        out_sum[...] = jnp.zeros_like(out_sum)
        back_sum[...] = jnp.zeros_like(back_sum)
        stretch = min(hidden, 512)

        def through(step, carry):
            columns = pl.ds(pl.multiple_of(step * stretch, stretch), stretch)
            before = dot(rows[part, :], up[:, columns])
            act_grad = dot(cots[part, :], down[columns, :], 1, 1)
            chance = normal_cdf(before)
            value = before * chance
            slope = chance + before * (
                jnp.exp(-0.5 * before * before) * (1.0 / math.sqrt(2.0 * math.pi))
            )
            out_sum[...] += dot(value.astype(BF16), down[columns, :])
            act[part, columns] = (value * column).astype(BF16)
            pre_grad = (act_grad * slope * column).astype(BF16)
            pre[part, columns] = pre_grad
            back_sum[...] += dot(pre_grad, up[:, columns], 1, 1)
            return carry

        lax.fori_loop(0, hidden // stretch, through, 0)
        back_rows[part, :] = back_sum[...].astype(BF16)
        produced = out_sum[...]
        inner = jnp.sum(produced * cots[part, :].astype(F32), axis=1, keepdims=True)
        spread = jnp.broadcast_to(inner, (chunk, BLOCK))
        for b in range(per):
            turned = jnp.transpose(spread[b * capacity : (b + 1) * capacity, :])
            dots[first + b] = turned[0:1, :]
        return (produced * column).astype(BF16)

    own_rows.wait()
    load_cots.wait()
    load_up.wait()
    load_down.wait()
    lax.fori_loop(1, per, arrive, 0)
    y_rows[0] = process(jnp.int32(0))
    y_copy(jnp.int32(0)).start()
    lax.fori_loop(1, per, start_back, 0)
    home_own.start()
    dot_ref[me] = dots[0]
    lax.fori_loop(early, owners, start_rows, 0)

    def later(index, carry):
        def arrive_in(b, carry):
            return arrive(index * per + b, carry)

        def start_in(b, carry):
            return start_back(index * per + b, carry)

        lax.fori_loop(0, per, arrive_in, 0)
        result = process(index)

        @pl.when(index >= 2)
        def _():
            y_copy(index - 2).wait()

        y_rows[lax.rem(index, 2)] = result
        y_copy(index).start()
        lax.fori_loop(0, per, start_in, 0)
        return carry

    lax.fori_loop(1, chunks, later, 0)
    for index in range(max(chunks - 2, 0), chunks):
        y_copy(jnp.int32(index)).wait()

    half = hidden // 2
    count = half // tile

    def columns_of(side, step):
        return pl.ds(pl.multiple_of(side * half + step * tile, tile), tile)

    def up_tile(side, step):
        return dot(rows[...], pre[:, columns_of(side, step)], 0, 0)

    def down_tile(side, step):
        return dot(act[:, columns_of(side, step)], cots[...], 0, 0)

    def up_copy(step):
        slot = lax.rem(step, 2)
        return remote(
            up_ring.at[slot], up_got.at[:, columns_of(0, step)], ring_send.at[slot], up_recv.at[step], (me, 1 - core)
        )

    def down_copy(step):
        slot = lax.rem(step, 2)
        return remote(
            down_ring.at[slot], down_got.at[columns_of(0, step), :], ring_send.at[2 + slot], down_recv.at[step], (me, 1 - core)
        )

    def give(step, carry):
        slot = lax.rem(step, 2)

        @pl.when(step >= 2)
        def _():
            up_copy(step - 2).wait_send()
            down_copy(step - 2).wait_send()

        up_ring[slot] = up_tile(1 - core, step).astype(BF16)
        up_copy(step).start()
        down_ring[slot] = down_tile(1 - core, step).astype(BF16)
        down_copy(step).start()
        return carry

    lax.fori_loop(0, count, give, 0)

    def up_write(step):
        slot = lax.rem(step, 2)
        return pltpu.make_async_copy(up_out.at[slot], up_grad_ref.at[:, columns_of(0, step)], out_sem.at[slot])

    def down_write(step):
        slot = lax.rem(step, 2)
        return pltpu.make_async_copy(down_out.at[slot], down_grad_ref.at[columns_of(0, step), :], out_sem.at[2 + slot])

    def take(step, carry):
        slot = lax.rem(step, 2)

        @pl.when(step >= 2)
        def _():
            up_write(step - 2).wait()
            down_write(step - 2).wait()

        mine = up_tile(core, step)
        up_copy(step).wait_recv()
        up_out[slot] = mine + up_got[:, columns_of(0, step)].astype(F32)
        up_write(step).start()
        mine = down_tile(core, step)
        down_copy(step).wait_recv()
        down_out[slot] = mine + down_got[columns_of(0, step), :].astype(F32)
        down_write(step).start()
        return carry

    lax.fori_loop(0, count, take, 0)

    for step in range(max(count - 2, 0), count):
        up_copy(step).wait_send()
        down_copy(step).wait_send()
        up_write(step).wait()
        down_write(step).wait()
    home_own.wait()

    def finish(step, carry):
        for copy in send_rows(step):
            copy.wait_send()
        for copy in send_back(step):
            copy.wait_send()
        for copy in get_back(step):
            copy.wait_recv()
        return carry

    lax.fori_loop(1, owners, finish, 0)


def experts_of(x_rows, gate_rows, cot_rows, up_matrix, down_matrix, owners):
    slots, width = x_rows.shape
    hidden = up_matrix.shape[1]
    capacity = slots // owners
    chunk, tile, half = min(slots, 512), 256, hidden // 2
    count = half // tile
    shape, vmem, dma = jax.ShapeDtypeStruct, pltpu.VMEM, pltpu.SemaphoreType.DMA
    anywhere = pl.BlockSpec(memory_space=pl.ANY)
    near = pl.BlockSpec(memory_space=pltpu.VMEM)
    return pl.pallas_call(
        functools.partial(expert_kernel, owners),
        out_shape=(
            shape((slots, width), BF16),
            shape((slots, width), BF16),
            shape((owners, 1, capacity), F32),
            shape((width, half), F32),
            shape((half, width), F32),
        ),
        in_specs=[anywhere, near, anywhere, anywhere, anywhere],
        out_specs=(anywhere, anywhere, near, anywhere, anywhere),
        scratch_shapes=[
            vmem((width, hidden), BF16),
            vmem((hidden, width), BF16),
            vmem((slots, width), BF16),
            vmem((slots, width), BF16),
            vmem((slots, hidden), BF16),
            vmem((slots, hidden), BF16),
            vmem((chunk, width), F32),
            vmem((chunk, width), F32),
            vmem((slots, width), BF16),
            vmem((2, chunk, width), BF16),
            vmem((owners, 1, capacity), F32),
            vmem((owners, 1, capacity), F32),
            vmem((2, width, tile), BF16),
            vmem((2, tile, width), BF16),
            vmem((width, half), BF16),
            vmem((half, width), BF16),
            vmem((2, width, tile), F32),
            vmem((2, tile, width), F32),
            dma((2,)),
            dma,
            dma((2,)),
            dma((2,)),
        ]
        + [dma((owners,))] * 8
        + [dma((4,)), dma((count,)), dma((count,)), dma((4,))],
        compiler_params=pltpu.CompilerParams(
            vmem_limit_bytes=67043328, collective_id=1, has_side_effects=True
        ),
        cost_estimate=pl.CostEstimate(
            flops=58 * 10**9, bytes_accessed=4 * 10**7, transcendentals=2 * 10**7
        ),
        name="experts",
    )(x_rows, gate_rows, cot_rows, up_matrix, down_matrix)


def shards(
    block_input,
    cotangent,
    segment_ids,
    routes,
    slot_ids,
    attention_in,
    attention_out,
    router_weight,
    first_gain,
    second_gain,
    bias_table,
    expert_up,
    expert_down,
):
    length, width = block_input.shape
    owners = lax.axis_size("expert")
    capacity = 4 * length // owners
    experts = router_weight.shape[1]
    heads = bias_table.shape[1]
    member = lax.axis_index("dp")
    pair_size = lax.axis_size("dp")
    buckets = pair_size * bias_table.shape[0]
    share = width // pair_size
    inner = owners // 4
    side = math.isqrt(inner)
    digits = (side, inner // side, 4)

    rows = -(-(experts + 2 + heads) // 16) * 16
    wide_part = jnp.concatenate([router_weight.T, first_gain[None], second_gain[None]], axis=0)
    small_part = jnp.zeros((rows, width), BF16)
    small_part = lax.dynamic_update_slice(small_part, wide_part, (0, member * share))
    small_part = lax.dynamic_update_slice(
        small_part, bias_table.T, (experts + 2, member * bias_table.shape[0])
    )
    route_rows = routes.T
    place_rows = route_rows * capacity + slot_ids.T
    (
        hidden_state, normed_two, triple, context, probs, gates,
        x_rows, gate_rows, cot_rows, full_in, full_out, small,
    ) = forward(
        block_input, cotangent, segment_ids, route_rows, place_rows, attention_in, attention_out, small_part,
        owners, experts, buckets, heads,
    )
    y_rows, home_rows, gate_dots, up_share, down_share = experts_of(
        x_rows, gate_rows, cot_rows, expert_up[0], expert_down[0], owners
    )
    block_output, input_grad, in_share, out_share, small_sum = backward(
        (
            block_input, cotangent, hidden_state, normed_two, triple, context, probs, gates, route_rows, place_rows,
            home_rows, gate_dots, full_in, full_out, small,
        ),
        y_rows, owners, experts, buckets, digits,
    )
    mine = lax.dynamic_slice_in_dim(small_sum[: experts + 2], member * share, share, 1)
    bias_grad = lax.dynamic_slice(
        small_sum, (experts + 2, member * bias_table.shape[0]), (heads, bias_table.shape[0])
    )
    return (
        block_output,
        input_grad,
        in_share,
        out_share,
        mine[:experts].T,
        mine[experts],
        mine[experts + 1],
        bias_grad.T,
        up_share[None],
        down_share[None],
    )


def solution(mesh):
    rows = P(("expert", "dp"), None)
    return jax.shard_map(
        shards,
        mesh=mesh,
        in_specs=(
            rows,
            rows,
            rows,
            rows,
            rows,
            P("dp", None),
            P("dp", None),
            P("dp", None),
            P("dp"),
            P("dp"),
            P("dp", None),
            P("expert", None, None),
            P("expert", None, None),
        ),
        out_specs=(
            rows,
            rows,
            P("dp", None),
            P("dp", None),
            P("dp", None),
            P("dp"),
            P("dp"),
            P("dp", None),
            P("expert", None, "dp"),
            P("expert", "dp", None),
        ),
        check_vma=False,
    )
```

```python
import functools
import math

import jax
import jax.numpy as jnp
import numpy as np
from jax import lax
from jax.experimental import pallas as pl
from jax.experimental.pallas import tpu as pltpu
from jax.sharding import PartitionSpec as P

EPS = 1e-06
F32 = jnp.float32
BF16 = jnp.bfloat16
BLOCK = 128
MASKED = -1e30


def reach_marks(buckets, reach_len):
    half_count = buckets // 2
    step_ids = np.arange(1, half_count)
    thresholds = np.floor(half_count * (reach_len / half_count) ** (step_ids / half_count))
    thresholds = np.maximum(thresholds, half_count + step_ids)
    return [int(mark) for mark in thresholds.astype(np.int32)]


def normal_cdf(argument):
    return 0.5 * (1.0 + jax.scipy.special.erf(argument * (1.0 / math.sqrt(2.0))))


def gelu_slope(argument):
    return normal_cdf(argument) + argument * (
        jnp.exp(-0.5 * argument * argument) * (1.0 / math.sqrt(2.0 * math.pi))
    )


def dot(left, right, left_dim=1, right_dim=0):
    return lax.dot_general(
        left, right, (((left_dim,), (right_dim,)), ((), ())), preferred_element_type=F32
    )


def bucket_hot(buckets, length, width):
    column = lax.broadcasted_iota(jnp.int32, (1, width), 1)
    distance = jnp.maximum(length // 2 + BLOCK - 1 - column, 0)
    bucket = jnp.minimum(distance, buckets // 2)
    for mark in reach_marks(buckets, length):
        bucket = bucket + jnp.where(distance >= mark, 1, 0)
    rows = lax.broadcasted_iota(jnp.int32, (buckets, width), 0)
    return jnp.where(rows == bucket, 1.0, 0.0)


def spans(length):
    reach = length // 2
    for block in range(length // BLOCK):
        low = max(0, block * BLOCK - reach)
        high = (block + 1) * BLOCK
        yield block, low, high, reach + BLOCK - (high - low)


def halves(pair):
    lane = lax.broadcasted_iota(jnp.int32, (1, pair.shape[1]), 1)
    first = lane < pair.shape[1] // 2
    zero = jnp.zeros_like(pair)
    return jnp.where(first, pair, zero), jnp.where(first, zero, pair)


def hot_rows(place_ref, first, count):
    ids = first + lax.broadcasted_iota(jnp.int32, (count, place_ref.shape[1]), 0)
    return ids == place_ref[0:1, :], ids == place_ref[1:2, :]


def bf16_of(flags):
    return jnp.where(flags, 1.0, 0.0).astype(BF16)


def pieces_of(row):
    parts = []
    for _ in range(3):
        piece = row.astype(BF16).astype(F32)
        parts.append(piece)
        row = row - piece
    parts.append(jnp.zeros((5, row.shape[1]), F32))
    return jnp.concatenate(parts, axis=0).astype(BF16)


def forward_kernel(
    owners, experts, buckets,
    x_ref, cot_ref, segment_ref, route_ref, place_ref, in_half_ref, out_half_ref, small_part_ref,
    hidden_hbm, normed_hbm, triple_hbm, context_hbm, prob_hbm, gate_ref,
    x_rows_hbm, gate_rows_ref, cot_rows_ref, in_hbm, out_hbm, small_ref,
    hidden_ref, normed_ref, triple_ref, context_ref, prob_ref, x_rows_ref, in_ref, out_ref, store_sem,
    table_ref, mask_ref, one_ref, half_ref, cot_send_ref, small_got_ref,
    weight_send, weight_recv, cot_send, cot_recv,
):
    me, core = lax.axis_index("expert"), lax.axis_index("dp")
    length, width = x_ref.shape
    heads = 2 * prob_ref.shape[0]
    pair = 2 * (width // heads)
    pairs = heads // 2
    reach = length // 2
    span = reach + BLOCK
    scale = 1.0 / math.sqrt(width // heads)
    slots = x_rows_ref.shape[0]
    capacity = slots // owners
    share = in_half_ref.shape[0]

    def block(index):
        return pl.ds(pl.multiple_of(index * capacity, capacity), capacity)

    stores = []

    def store(source, target):
        copy = pltpu.make_async_copy(source, target, store_sem.at[len(stores)])
        copy.start()
        stores.append(copy)

    mine = pl.ds(pl.multiple_of(core * share, share), share)
    half_ref[...] = cot_ref[...].astype(BF16)
    greet(me, core, owners)
    weights = [
        remote(in_half_ref, in_ref.at[mine], weight_send.at[0], weight_recv.at[0], (me, 1 - core)),
        remote(out_half_ref, out_ref.at[mine], weight_send.at[1], weight_recv.at[1], (me, 1 - core)),
        remote(small_part_ref, small_got_ref, weight_send.at[2], weight_recv.at[2], (me, 1 - core)),
    ]
    for copy in weights:
        copy.start()
    in_ref[mine, :] = in_half_ref[...]
    out_ref[mine, :] = out_half_ref[...]

    def cot_copy(step):
        peer = partner(me, step, owners, 1)
        return remote(
            cot_send_ref.at[block(step)], cot_rows_ref.at[block(step)], cot_send.at[step], cot_recv.at[step], (peer, core)
        )

    def dispatch(step, carry):
        peer = partner(me, step, owners, 1)
        first, second = hot_rows(place_ref, peer * capacity, capacity)
        cot_send_ref[block(step), :] = dot(bf16_of(first | second), half_ref[...]).astype(BF16)

        @pl.when(step >= 2)
        def _():
            cot_copy(step - 1).start()

        return carry

    lax.fori_loop(0, owners, dispatch, 0)
    cot_copy(owners - 1).start()
    store(cot_send_ref.at[block(0)], cot_rows_ref.at[block(0)])

    x = x_ref[...]
    rms = lax.rsqrt(jnp.mean(x * x, axis=1, keepdims=True) + EPS)
    for copy in weights:
        copy.wait_recv()
    small_ref[...] = small_part_ref[...] + small_got_ref[...]
    store(in_ref, in_hbm)
    store(out_ref, out_hbm)
    one_ref[...] = (x * rms * small_ref[experts : experts + 1, :].astype(F32)).astype(BF16)

    chunk = 3 * pair

    def project(step, carry):
        columns = pl.ds(pl.multiple_of(step * chunk, BLOCK), chunk)
        triple_ref[:, columns] = dot(one_ref[...], in_ref[:, columns]).astype(BF16)
        return carry

    lax.fori_loop(0, 3 * width // chunk, project, 0)

    store(triple_ref, triple_hbm)
    wide = span + BLOCK
    bias = small_ref[experts + 2 : experts + 2 + heads, 0:buckets]
    by_column = dot(bias, bucket_hot(buckets, length, wide).astype(BF16))
    for head in range(heads):
        spread = jnp.broadcast_to(by_column[head : head + 1, :], (BLOCK, wide))
        rolled = pltpu.roll(spread, wide - BLOCK + 1, 1, stride=1, stride_axis=0)
        table_ref[head // 2, (head % 2) * BLOCK : (head % 2 + 1) * BLOCK, :] = rolled[:, :span]

    segment_row = segment_ref[...].astype(F32)
    segment_column = jnp.transpose(jnp.broadcast_to(segment_row, (BLOCK, length)))
    for index, low, high, skip in spans(length):
        rows = index * BLOCK + lax.broadcasted_iota(jnp.int32, (BLOCK, high - low), 0)
        columns = low + lax.broadcasted_iota(jnp.int32, (BLOCK, high - low), 1)
        own = segment_column[index * BLOCK : (index + 1) * BLOCK, 0:1]
        allowed = (rows >= columns) & (own == segment_row[:, low:high])
        mask_ref[index, :, skip:] = jnp.where(allowed, 0.0, MASKED)

    def attend(step, carry):
        base = pl.multiple_of(step * pair, pair)
        query_columns = pl.ds(base, pair)
        key_columns = pl.ds(pl.multiple_of(width + base, pair), pair)
        value_columns = pl.ds(pl.multiple_of(2 * width + base, pair), pair)
        for index, low, high, skip in spans(length):
            rows = slice(index * BLOCK, (index + 1) * BLOCK)
            query = triple_ref[rows, query_columns] * jnp.asarray(scale, BF16)
            stacked = jnp.concatenate(halves(query), axis=0)
            scores = dot(stacked, triple_ref[low:high, key_columns], 1, 1)
            mask = mask_ref[index, :, skip:]
            scores = scores + table_ref[step, :, skip:] + jnp.concatenate([mask, mask], axis=0)
            top = jnp.max(scores, axis=1, keepdims=True)
            weight = jnp.exp(scores - top)
            prob = weight * (1.0 / jnp.sum(weight, axis=1, keepdims=True))
            half = prob.astype(BF16)
            prob_ref[step, index, :, skip:] = half
            first, second = halves(triple_ref[low:high, value_columns])
            context = dot(half[:BLOCK], first) + dot(half[BLOCK:], second)
            context_ref[rows, query_columns] = context.astype(BF16)
        return carry

    lax.fori_loop(0, pairs, attend, 0)
    store(prob_ref, prob_hbm)
    store(context_ref, context_hbm)

    hidden = x_ref[...] + dot(context_ref[...], out_ref[...])
    hidden_ref[...] = hidden
    store(hidden_ref, hidden_hbm)
    rms = lax.rsqrt(jnp.mean(hidden * hidden, axis=1, keepdims=True) + EPS)
    normed = (hidden * rms * small_ref[experts + 1 : experts + 2, :].astype(F32)).astype(BF16)
    normed_ref[...] = normed
    store(normed_ref, normed_hbm)
    logits = dot(small_ref[0:experts, :], normed, 1, 1)
    expert_ids = lax.broadcasted_iota(jnp.int32, logits.shape, 0)
    first = jnp.sum(jnp.where(expert_ids == route_ref[0:1, :], logits, 0.0), axis=0, keepdims=True)
    second = jnp.sum(jnp.where(expert_ids == route_ref[1:2, :], logits, 0.0), axis=0, keepdims=True)
    gate_first = 1.0 / (1.0 + jnp.exp(second - first))
    gate_second = 1.0 / (1.0 + jnp.exp(first - second))
    gate_ref[0:1, :] = gate_first
    gate_ref[1:2, :] = gate_second
    first_pieces, second_pieces = pieces_of(gate_first), pieces_of(gate_second)

    def outgoing(step, carry):
        first, second = hot_rows(place_ref, step * capacity, capacity)
        x_rows_ref[block(step), :] = dot(bf16_of(first | second), normed_ref[...]).astype(BF16)
        gates = dot(first_pieces, bf16_of(first), 1, 1) + dot(second_pieces, bf16_of(second), 1, 1)
        gate_rows_ref[step] = jnp.sum(gates, axis=0, keepdims=True)
        return carry

    lax.fori_loop(0, owners, outgoing, 0)
    store(x_rows_ref, x_rows_hbm)

    def finish(step, carry):
        cot_copy(step).wait()
        return carry

    lax.fori_loop(1, owners, finish, 0)
    for copy in weights:
        copy.wait_send()
    for copy in stores:
        copy.wait()


def backward_kernel(
    owners, experts, buckets, digits,
    x_hbm, cot_hbm, hidden_hbm, normed_hbm, triple_hbm, context_hbm, prob_hbm, gate_ref, route_ref, place_ref,
    home_hbm, dot_ref, in_hbm, out_hbm, small_ref, y_hbm,
    block_ref, input_grad_ref, in_share_ref, out_share_ref, small_sum_ref,
    home_ref, cot_ref, hidden_ref, normed_ref, context_ref, out_ref, x_ref, triple_ref, prob_ref, in_ref, load_sem,
    context_grad_ref, triple_grad_ref, turned_ref, key_ref, value_ref, diagonal_ref, sums_ref,
    grads_ref, small_mine_ref, small_got_ref, came_ref, work_ref, got_ref, final_ref,
    y_send, y_recv, own_sem, core_send, core_recv, ring_send, ring_recv, small_send, small_recv,
):
    me, core = lax.axis_index("expert"), lax.axis_index("dp")
    hidden_grad_ref = block_ref
    length, width = x_ref.shape
    pairs = prob_ref.shape[0]
    heads = 2 * pairs
    pair = 2 * (width // heads)
    reach = length // 2
    span = reach + BLOCK
    scale = 1.0 / math.sqrt(width // heads)
    slots = home_ref.shape[0]
    capacity = slots // owners

    def block(index):
        return pl.ds(pl.multiple_of(index * capacity, capacity), capacity)

    loads = [
        pltpu.make_async_copy(source, target, load_sem.at[index])
        for index, (source, target) in enumerate(
            (
                (home_hbm, home_ref),
                (cot_hbm, cot_ref),
                (hidden_hbm, hidden_ref),
                (normed_hbm, normed_ref),
                (context_hbm, context_ref),
                (out_hbm, out_ref),
                (x_hbm, x_ref),
                (triple_hbm, triple_ref),
                (prob_hbm, prob_ref),
                (in_hbm, in_ref),
            )
        )
    ]
    for copy in loads:
        copy.start()
    own_y = pltpu.make_async_copy(y_hbm.at[block(0)], came_ref.at[block(me)], own_sem)
    own_y.start()
    greet(me, core, owners)

    def y_copy(step, sign):
        peer = partner(me, step, owners, -1)
        target = me if sign < 0 else partner(me, step, owners, 1)
        return remote(
            y_hbm.at[block(step)], came_ref.at[block(target)], y_send.at[step], y_recv.at[step], (peer, core)
        )

    def start_y(step, carry):
        y_copy(step, -1).start()
        return carry

    lax.fori_loop(1, owners, start_y, 0)

    def column(row):
        return jnp.transpose(jnp.broadcast_to(row, (BLOCK, length)))

    place_first = column(place_ref[0:1, :].astype(F32))
    place_second = column(place_ref[1:2, :].astype(F32))
    lane = lax.broadcasted_iota(jnp.int32, (length, BLOCK), 1).astype(F32)
    wide_k = 2 * BLOCK

    def hot_columns(group):
        first = (group * BLOCK).astype(F32) if hasattr(group, "astype") else float(group * BLOCK)
        return place_first - first == lane, place_second - first == lane

    def gather_rows(rows_ref, base_ref):
        def add(group, carry):
            left = hot_columns(2 * group)
            right = hot_columns(2 * group + 1)
            hot = jnp.concatenate([bf16_of(left[0] | left[1]), bf16_of(right[0] | right[1])], axis=1)
            rows = pl.ds(pl.multiple_of(group * wide_k, wide_k), wide_k)
            base_ref[...] += dot(hot, rows_ref[rows, :])
            return carry

        lax.fori_loop(0, slots // wide_k, add, 0)

    per_row = BLOCK // capacity

    def dot_row(group):
        if per_row == 1:
            return dot_ref[group]
        return jnp.concatenate([dot_ref[group * per_row + b] for b in range(per_row)], axis=1)

    def pick(group, carry):
        first, second = hot_columns(group)
        row = dot_row(group)
        return carry + jnp.where(first, row, 0.0) - jnp.where(second, row, 0.0)

    picked = lax.fori_loop(0, slots // BLOCK, pick, jnp.zeros((length, BLOCK), F32))
    difference = jnp.sum(picked, axis=1, keepdims=True)
    gates = column(gate_ref[0:1, :]) * column(gate_ref[1:2, :])
    ids = lax.broadcasted_iota(jnp.int32, (length, BLOCK), 1)
    pick_first = jnp.where(column(route_ref[0:1, :].astype(F32)).astype(jnp.int32) == ids, 1.0, 0.0)
    pick_second = jnp.where(column(route_ref[1:2, :].astype(F32)).astype(jnp.int32) == ids, 1.0, 0.0)
    logit_grad = ((pick_first - pick_second) * gates * difference).astype(BF16)

    small_mine_ref[...] = jnp.zeros_like(small_mine_ref)
    for copy in loads[:6]:
        copy.wait()
    hidden_grad_ref[...] = dot(logit_grad[:, 0:experts], small_ref[0:experts, :])
    gather_rows(home_ref, hidden_grad_ref)
    small_mine_ref[0:experts, :] = dot(logit_grad, normed_ref[...], 0, 0)[0:experts, :]

    def settle(step, carry):
        rows = pl.ds(pl.multiple_of(step * BLOCK, BLOCK), BLOCK)
        normed_grad = hidden_grad_ref[rows, :]
        hidden = hidden_ref[rows, :]
        rms = lax.rsqrt(jnp.mean(hidden * hidden, axis=1, keepdims=True) + EPS)
        scaled = normed_grad * small_ref[experts + 1 : experts + 2, :].astype(F32)
        inner = jnp.mean(scaled * hidden, axis=1, keepdims=True)
        hidden_grad_ref[rows, :] = cot_ref[rows, :] + (rms * scaled - hidden * (rms * rms * rms) * inner)
        return carry + jnp.sum(normed_grad * (hidden * rms), axis=0, keepdims=True)

    small_mine_ref[experts + 1 : experts + 2, :] = lax.fori_loop(
        0, length // BLOCK, settle, jnp.zeros((1, width), F32)
    )

    residual = hidden_grad_ref[...].astype(BF16)
    grads_ref[:, 3 * width :] = dot(jnp.transpose(context_ref[...]), residual)
    advance, advance_small = reducer(
        me, core, digits, grads_ref, in_share_ref, out_share_ref, small_mine_ref, small_got_ref, small_sum_ref,
        work_ref, got_ref, final_ref, core_send, core_recv, ring_send, ring_recv, small_send, small_recv,
    )
    advance(3)
    context_grad_ref[...] = dot(residual, out_ref[...], 1, 1).astype(BF16)
    diagonal_ref[...] = jnp.zeros_like(diagonal_ref)
    for copy in loads[6:]:
        copy.wait()
    x = x_ref[...]
    rms = lax.rsqrt(jnp.mean(x * x, axis=1, keepdims=True) + EPS)
    gain = small_ref[experts : experts + 1, :].astype(F32)
    turned_ref[...] = jnp.transpose((x * rms * gain).astype(BF16))

    def attend(step, carry):
        base = pl.multiple_of(step * pair, pair)
        query_columns = pl.ds(base, pair)
        key_columns = pl.ds(pl.multiple_of(width + base, pair), pair)
        value_columns = pl.ds(pl.multiple_of(2 * width + base, pair), pair)
        key_ref[...] = jnp.zeros_like(key_ref)
        value_ref[...] = jnp.zeros_like(value_ref)
        for index, low, high, skip in spans(length):
            rows = slice(index * BLOCK, (index + 1) * BLOCK)
            query = triple_ref[rows, query_columns] * jnp.asarray(scale, BF16)
            query = jnp.concatenate(halves(query), axis=0)
            grad = jnp.concatenate(halves(context_grad_ref[rows, query_columns]), axis=0)
            half = prob_ref[step, index, :, skip:]
            prob = half.astype(F32)
            prob_grad = dot(grad, triple_ref[low:high, value_columns], 1, 1)
            norm = 1.0 / jnp.sum(prob, axis=1, keepdims=True)
            row_dot = norm * jnp.sum(prob * prob_grad, axis=1, keepdims=True)
            score_grad = (prob * norm) * (prob_grad - row_dot)
            diagonal_ref[step, :, skip:] += score_grad
            score_half = score_grad.astype(BF16)
            first, second = halves(triple_ref[low:high, key_columns])
            query_grad = dot(score_half[:BLOCK], first) + dot(score_half[BLOCK:], second)
            triple_grad_ref[rows, query_columns] = (query_grad * scale).astype(BF16)
            key_ref[low:high, :] += dot(score_half, query, 0, 0)
            value_ref[low:high, :] += dot(half, grad, 0, 0)
        triple_grad_ref[:, key_columns] = key_ref[...].astype(BF16)
        triple_grad_ref[:, value_columns] = value_ref[...].astype(BF16)
        return carry

    groups = COLORS - 1
    part = width // groups
    for group in range(groups):
        lax.fori_loop(group * pairs // groups, (group + 1) * pairs // groups, attend, 0)
        for color in [3, *range(group)]:
            advance(color)

        def weigh(section, carry):
            source = pl.ds(pl.multiple_of(section * width + group * part, BLOCK), part)
            target = pl.ds(pl.multiple_of(group * width + section * part, BLOCK), part)
            grads_ref[:, target] = dot(turned_ref[...], triple_grad_ref[:, source])
            return carry

        lax.fori_loop(0, 3, weigh, 0)
        advance(group)

    def finish(step, carry):
        rows = pl.ds(pl.multiple_of(step * BLOCK, BLOCK), BLOCK)
        normed_grad = dot(triple_grad_ref[rows, :], in_ref[...], 1, 1)
        part = x_ref[rows, :]
        scaling = lax.rsqrt(jnp.mean(part * part, axis=1, keepdims=True) + EPS)
        scaled = normed_grad * gain
        inner = jnp.mean(scaled * part, axis=1, keepdims=True)
        input_grad_ref[rows, :] = hidden_grad_ref[rows, :] + (
            scaling * scaled - part * (scaling * scaling * scaling) * inner
        )
        return carry + jnp.sum(normed_grad * (part * scaling), axis=0, keepdims=True)

    small_mine_ref[experts : experts + 1, :] = lax.fori_loop(
        0, length // BLOCK, finish, jnp.zeros((1, width), F32)
    )

    for color in (2, 1, 0, 3):
        advance(color)
    wide = span + BLOCK
    row_ids = lax.broadcasted_iota(jnp.int32, (BLOCK, wide), 0)
    for head in range(heads):
        sheet = diagonal_ref[head // 2, (head % 2) * BLOCK : (head % 2 + 1) * BLOCK, :]
        sheet = jnp.concatenate([sheet, jnp.zeros((BLOCK, BLOCK), F32)], axis=1)
        sheet = pltpu.roll(sheet, BLOCK - 1, 1)
        step = 1
        while step < BLOCK:
            sheet = jnp.where((row_ids & step) != 0, pltpu.roll(sheet, wide - step, 1), sheet)
            step *= 2
        sums_ref[head : head + 1, :] = jnp.sum(sheet, axis=0, keepdims=True)
    hot = bucket_hot(buckets, length, wide).astype(BF16)
    rest = sums_ref[...]
    total = jnp.zeros((heads, buckets), F32)
    for _ in range(3):
        piece = rest.astype(BF16)
        total = total + dot(piece, hot, 1, 1)
        rest = rest - piece.astype(F32)
    small_mine_ref[experts + 2 : experts + 2 + heads, 0:buckets] = total

    def finish_y(step, carry):
        y_copy(step, -1).wait_send()
        y_copy(step, 1).wait_recv()
        return carry

    for turn in range(2 * len(digits) + 2):
        for color in (2, 1, 0, 3):
            advance(color)
        advance_small()
        if turn == 3:
            own_y.wait()
            lax.fori_loop(1, owners, finish_y, 0)
            block_ref[...] = hidden_ref[...]
            gather_rows(came_ref, block_ref)


COLORS = 4


def reducer(
    me, core, digits, grads_ref, in_share_ref, out_share_ref, small_mine_ref, small_got_ref, small_sum_ref,
    work_ref, got_ref, final_ref, core_send, core_recv, ring_send, ring_recv, small_send, small_recv,
):
    _, many, rows, columns = work_ref.shape
    share, width = out_share_ref.shape
    groups = COLORS - 1
    section = width // groups
    down = share // rows
    strides = []
    stride = 1
    for size in digits:
        strides.append(stride)
        stride *= size
    place = [lax.rem(lax.div(me, strides[axis]), digits[axis]) for axis in range(len(digits))]
    orders = [[0, 1, 2], [1, 0, 2]]
    other = (me, 1 - core)

    def sheets(color, side):
        for across in range(width // columns):
            sheet = grads_ref[
                pl.ds(pl.multiple_of(side * share, share), share),
                color * width + across * columns : color * width + (across + 1) * columns,
            ]
            for step in range(down):
                yield across * down + step, sheet[step * rows : (step + 1) * rows, :]

    def swap(color):
        for index, value in sheets(color, 1 - core):
            work_ref[color, index] = value.astype(BF16)
        return [remote(work_ref.at[color], got_ref.at[0, color], core_send.at[color], core_recv.at[color], other)]

    def swapped(color):
        for index, value in sheets(color, core):
            work_ref[color, index] = (value + got_ref[0, color, index].astype(F32)).astype(BF16)

    def settled(color):
        for index in range(many):
            across, step = index // down, index % down
            low = step * rows
            value = final_ref[color, index].astype(F32)
            if color == groups:
                out_share_ref[low : low + rows, across * columns : (across + 1) * columns] = value
                continue
            for left in range(0, columns, BLOCK):
                start = across * columns + left
                target = start // section * width + color * section + start % section
                in_share_ref[low : low + rows, target : target + BLOCK] = value[:, left : left + BLOCK]

    def peer_of(axis, ahead):
        digit = lax.rem(place[axis] + ahead, digits[axis])
        return digit, (me + (digit - place[axis]) * strides[axis], core)

    levels = []
    for color in range(COLORS):
        order = orders[color % 2]
        base, extent, landing, seen = jnp.int32(0), many, 0, []
        for axis in order:
            part = extent // digits[axis]
            seen.append((axis, base, part, landing))
            base = base + place[axis] * part
            extent = part
            landing += part * (digits[axis] - 1)
        levels.append(seen)

    def sem_of(color, level, ahead, way):
        return ((color * 3 + level) * 4 + ahead) * 2 + way

    def scatter(color, level):
        axis, base, part, landing = levels[color][level]
        copies = []
        for ahead in range(1, digits[axis]):
            digit, device = peer_of(axis, ahead)
            index = sem_of(color, level, ahead, 0)
            copies.append(
                remote(
                    work_ref.at[color, pl.ds(base + digit * part, part)],
                    got_ref.at[1, color, pl.ds(landing + (ahead - 1) * part, part)],
                    ring_send.at[index], ring_recv.at[index], device,
                )
            )
        return copies

    def scattered(color, level):
        axis, base, part, landing = levels[color][level]
        mine = base + place[axis] * part
        target = final_ref if level == len(digits) - 1 else work_ref

        def add(step, carry):
            value = work_ref[color, mine + step].astype(F32)
            for ahead in range(1, digits[axis]):
                value = value + got_ref[1, color, landing + (ahead - 1) * part + step].astype(F32)
            target[color, mine + step] = value.astype(BF16)
            return carry

        lax.fori_loop(0, part, add, 0)

    def gather(color, level):
        axis, base, part, _ = levels[color][level]
        mine = base + place[axis] * part
        copies = []
        for ahead in range(1, digits[axis]):
            _, device = peer_of(axis, ahead)
            index = sem_of(color, level, ahead, 1)
            copies.append(
                remote(
                    final_ref.at[color, pl.ds(mine, part)], final_ref.at[color, pl.ds(mine, part)],
                    ring_send.at[index], ring_recv.at[index], device,
                )
            )
        return copies

    def small_copies(axis):
        copies = []
        for ahead in range(1, digits[axis]):
            _, device = peer_of(axis, ahead)
            index = sum(digits[:axis]) - axis + ahead
            copies.append(
                remote(small_sum_ref, small_got_ref.at[index], small_send.at[index], small_recv.at[index], device)
            )
        return copies

    depth = len(digits)
    stage, flight = [0] * COLORS, [()] * COLORS

    def advance(color):
        now = stage[color]
        if now > 2 * depth + 1:
            return
        for copy in flight[color]:
            copy.wait()
        if now == 1:
            swapped(color)
        elif 1 < now <= depth + 1:
            scattered(color, now - 2)
        elif now == 2 * depth + 1:
            settled(color)
        if now == 0:
            flight[color] = swap(color)
        elif now <= depth:
            flight[color] = scatter(color, now - 1)
        elif now <= 2 * depth:
            flight[color] = gather(color, 2 * depth - now)
        else:
            flight[color] = ()
        for copy in flight[color]:
            copy.start()
        stage[color] = now + 1

    small_state = [0, ()]

    def advance_small():
        now, flying = small_state
        if now > depth + 1:
            return
        for copy in flying:
            copy.wait()
        if now == 1:
            small_sum_ref[...] = small_mine_ref[...] + small_got_ref[0]
        elif now > 1:
            value = small_sum_ref[...]
            for ahead in range(1, digits[now - 2]):
                value = value + small_got_ref[sum(digits[: now - 2]) - (now - 2) + ahead]
            small_sum_ref[...] = value
        if now == 0:
            flying = [
                remote(
                    small_mine_ref, small_got_ref.at[0], core_send.at[COLORS], core_recv.at[COLORS], other
                )
            ]
        elif now <= depth:
            flying = small_copies(now - 1)
        else:
            flying = ()
        for copy in flying:
            copy.start()
        small_state[:] = now + 1, flying

    return advance, advance_small


MESH = pl.DeviceIdType.MESH
GROUP = 4


def partner(me, step, owners, sign):
    groups = owners // GROUP
    outer = lax.rem(lax.div(me, GROUP) + sign * lax.div(step, GROUP) + groups, groups)
    inner = lax.rem(lax.rem(me, GROUP) + sign * lax.rem(step, GROUP) + GROUP, GROUP)
    return outer * GROUP + inner


def greet(me, core, owners):
    barrier = pltpu.get_barrier_semaphore()

    def signal(step, carry):
        pl.semaphore_signal(
            barrier, inc=1, device_id=(partner(me, step, owners, 1), core), device_id_type=MESH
        )
        return carry

    lax.fori_loop(1, owners, signal, 0)
    pl.semaphore_signal(barrier, inc=1, device_id=(me, 1 - core), device_id_type=MESH)
    pl.semaphore_wait(barrier, owners)


def remote(source, target, send, receive, device):
    return pltpu.make_async_remote_copy(
        src_ref=source, dst_ref=target, send_sem=send, recv_sem=receive,
        device_id=device, device_id_type=MESH,
    )


def whole(count):
    return [pl.BlockSpec(memory_space=pltpu.VMEM)] * count


def params(**extra):
    return pltpu.CompilerParams(vmem_limit_bytes=60 * 2**20, **extra)


def forward(x, cot, segments, route_rows, place_rows, in_half, out_half, small_part, owners, experts, buckets, heads):
    length, width = x.shape
    slots = 4 * length
    blocks, span = length // BLOCK, length // 2 + BLOCK
    any_, near = pl.BlockSpec(memory_space=pl.ANY), pl.BlockSpec(memory_space=pltpu.VMEM)
    shape, vmem, dma = jax.ShapeDtypeStruct, pltpu.VMEM, pltpu.SemaphoreType.DMA
    return pl.pallas_call(
        functools.partial(forward_kernel, owners, experts, buckets),
        out_shape=(
            shape((length, width), F32),
            shape((length, width), BF16),
            shape((length, 3 * width), BF16),
            shape((length, width), BF16),
            shape((heads // 2, blocks, 2 * BLOCK, span), BF16),
            shape((2, length), F32),
            shape((slots, width), BF16),
            shape((owners, 1, slots // owners), F32),
            shape((slots, width), BF16),
            shape((2 * in_half.shape[0], 3 * width), BF16),
            shape((2 * out_half.shape[0], width), BF16),
            shape(small_part.shape, BF16),
        ),
        in_specs=whole(8),
        out_specs=(any_, any_, any_, any_, any_, near, any_, near, any_, any_, any_, near),
        scratch_shapes=[
            vmem((length, width), F32),
            vmem((length, width), BF16),
            vmem((length, 3 * width), BF16),
            vmem((length, width), BF16),
            vmem((heads // 2, blocks, 2 * BLOCK, span), BF16),
            vmem((slots, width), BF16),
            vmem((2 * in_half.shape[0], 3 * width), BF16),
            vmem((2 * out_half.shape[0], width), BF16),
            dma((9,)),
            vmem((heads // 2, 2 * BLOCK, span), F32),
            vmem((blocks, BLOCK, span), F32),
            vmem((length, width), BF16),
            vmem((length, width), BF16),
            vmem((slots, width), BF16),
            vmem(small_part.shape, BF16),
            dma((3,)),
            dma((3,)),
            dma((owners,)),
            dma((owners,)),
        ],
        compiler_params=params(collective_id=0, has_side_effects=True),
        cost_estimate=pl.CostEstimate(
            flops=12 * 10**9, bytes_accessed=2 * 10**7, transcendentals=2 * 10**6
        ),
        name="attention_forward",
    )(x, cot, segments, route_rows, place_rows, in_half, out_half, small_part)


def backward(operands, y_rows, owners, experts, buckets, digits):
    x, probs, small = operands[0], operands[6], operands[14]
    length, width = x.shape
    pairs, blocks, _, span = probs.shape
    slots = operands[10].shape[0]
    share = width // 2
    columns = width // 2
    piece_rows = share * 2 // owners
    any_, near = pl.BlockSpec(memory_space=pl.ANY), pl.BlockSpec(memory_space=pltpu.VMEM)
    shape, vmem, dma = jax.ShapeDtypeStruct, pltpu.VMEM, pltpu.SemaphoreType.DMA
    pieces = (COLORS, owners, piece_rows, columns)
    return pl.pallas_call(
        functools.partial(backward_kernel, owners, experts, buckets, digits),
        out_shape=(
            shape((length, width), F32),
            shape((length, width), F32),
            shape((share, 3 * width), F32),
            shape((share, width), F32),
            shape(small.shape, F32),
        ),
        in_specs=[any_] * 7 + [near] * 3 + [any_, near, any_, any_, near, any_],
        out_specs=tuple(whole(5)),
        scratch_shapes=[
            vmem((slots, width), BF16),
            vmem((length, width), F32),
            vmem((length, width), F32),
            vmem((length, width), BF16),
            vmem((length, width), BF16),
            vmem((width, width), BF16),
            vmem((length, width), F32),
            vmem((length, 3 * width), BF16),
            vmem(probs.shape, BF16),
            vmem((width, 3 * width), BF16),
            dma((10,)),
            vmem((length, width), BF16),
            vmem((length, 3 * width), BF16),
            vmem((width, length), BF16),
            vmem((length, 2 * (width // (2 * pairs))), F32),
            vmem((length, 2 * (width // (2 * pairs))), F32),
            vmem((pairs, 2 * BLOCK, span), F32),
            vmem((2 * pairs, span + BLOCK), F32),
            vmem((width, 4 * width), F32),
            vmem(small.shape, F32),
            vmem((sum(digits) - len(digits) + 1,) + small.shape, F32),
            vmem((slots, width), BF16),
            vmem(pieces, BF16),
            vmem((2,) + pieces, BF16),
            vmem(pieces, BF16),
            dma((owners,)),
            dma((owners,)),
            dma,
            dma((COLORS + 1,)),
            dma((COLORS + 1,)),
            dma((COLORS * 24,)),
            dma((COLORS * 24,)),
            dma((12,)),
            dma((12,)),
        ],
        compiler_params=pltpu.CompilerParams(
            vmem_limit_bytes=67043328, collective_id=2, has_side_effects=True
        ),
        cost_estimate=pl.CostEstimate(
            flops=25 * 10**9, bytes_accessed=3 * 10**7, transcendentals=2 * 10**6
        ),
        name="attention_backward",
    )(*operands, y_rows)


def expert_kernel(
    owners,
    x_ref, gate_ref, cot_ref, up_hbm, down_hbm,
    y_ref, home_ref, dot_ref, up_grad_ref, down_grad_ref,
    up, down, rows, cots, act, pre, out_sum, back_sum, back_rows, y_rows, gates, dots,
    up_ring, down_ring, up_got, down_got, up_out, down_out,
    weight_sem, cot_sem, own_sem, y_sem,
    x_send, x_recv, gate_send, gate_recv, back_send, back_recv, dot_send, dot_recv,
    ring_send, up_recv, down_recv, out_sem,
):
    me, core = lax.axis_index("expert"), lax.axis_index("dp")
    slots, width = rows.shape
    hidden = up.shape[1]
    capacity = slots // owners
    chunk = min(slots, 512)
    per = chunk // capacity
    tile = 256

    def block(index):
        return pl.ds(pl.multiple_of(index * capacity, capacity), capacity)

    load_up = pltpu.make_async_copy(up_hbm, up, weight_sem.at[0])
    load_down = pltpu.make_async_copy(down_hbm, down, weight_sem.at[1])
    load_cots = pltpu.make_async_copy(cot_ref, cots, cot_sem)
    load_up.start()
    load_down.start()
    load_cots.start()
    own_rows = pltpu.make_async_copy(x_ref.at[block(me)], rows.at[block(0)], own_sem.at[0])
    own_rows.start()
    greet(me, core, owners)

    def send_rows(step):
        peer = partner(me, step, owners, 1)
        return (
            remote(x_ref.at[block(peer)], rows.at[block(step)], x_send.at[step], x_recv.at[step], (peer, core)),
            remote(gate_ref.at[peer], gates.at[step], gate_send.at[step], gate_recv.at[step], (peer, core)),
        )

    def start_rows(step, carry):
        for copy in send_rows(step):
            copy.start()
        return carry

    lax.fori_loop(1, owners, start_rows, 0)
    gates[0] = gate_ref[me]

    def send_back(step):
        peer = partner(me, step, owners, -1)
        return (
            remote(back_rows.at[block(step)], home_ref.at[block(me)], back_send.at[step], back_recv.at[step], (peer, core)),
            remote(dots.at[step], dot_ref.at[me], dot_send.at[step], dot_recv.at[step], (peer, core)),
        )

    def get_back(step):
        peer = partner(me, step, owners, 1)
        return (
            remote(back_rows.at[block(step)], home_ref.at[block(peer)], back_send.at[step], back_recv.at[step], (peer, core)),
            remote(dots.at[step], dot_ref.at[peer], dot_send.at[step], dot_recv.at[step], (peer, core)),
        )

    home_own = pltpu.make_async_copy(back_rows.at[block(0)], home_ref.at[block(me)], own_sem.at[1])
    chunks = slots // chunk

    def y_copy(index):
        slot = lax.rem(index, 2)
        part = pl.ds(pl.multiple_of(index * chunk, chunk), chunk)
        return pltpu.make_async_copy(y_rows.at[slot], y_ref.at[part], y_sem.at[slot])

    def arrive(step, carry):
        for copy in send_rows(step):
            copy.wait_recv()
        return carry

    def start_back(step, carry):
        for copy in send_back(step):
            copy.start()
        return carry

    def process(index):
        first = index * per
        part = pl.ds(pl.multiple_of(index * chunk, chunk), chunk)
        column = jnp.concatenate(
            [
                jnp.transpose(jnp.broadcast_to(gates[first + b], (BLOCK, capacity)))[:, 0:1]
                for b in range(per)
            ],
            axis=0,
        )
        out_sum[...] = jnp.zeros_like(out_sum)
        back_sum[...] = jnp.zeros_like(back_sum)
        stretch = hidden // 4

        def through(step, carry):
            columns = pl.ds(pl.multiple_of(step * stretch, stretch), stretch)
            before = dot(rows[part, :], up[:, columns])
            act_grad = dot(cots[part, :], down[columns, :], 1, 1)
            chance = normal_cdf(before)
            value = before * chance
            slope = chance + before * (
                jnp.exp(-0.5 * before * before) * (1.0 / math.sqrt(2.0 * math.pi))
            )
            out_sum[...] += dot(value.astype(BF16), down[columns, :])
            act[part, columns] = (value * column).astype(BF16)
            pre_grad = (act_grad * slope * column).astype(BF16)
            pre[part, columns] = pre_grad
            back_sum[...] += dot(pre_grad, up[:, columns], 1, 1)
            return carry

        lax.fori_loop(0, hidden // stretch, through, 0)
        back_rows[part, :] = back_sum[...].astype(BF16)
        produced = out_sum[...]
        inner = jnp.sum(produced * cots[part, :].astype(F32), axis=1, keepdims=True)
        spread = jnp.broadcast_to(inner, (chunk, BLOCK))
        for b in range(per):
            turned = jnp.transpose(spread[b * capacity : (b + 1) * capacity, :])
            dots[first + b] = turned[0:1, :]
        return (produced * column).astype(BF16)

    own_rows.wait()
    load_cots.wait()
    load_up.wait()
    load_down.wait()
    lax.fori_loop(1, per, arrive, 0)
    y_rows[0] = process(jnp.int32(0))
    y_copy(jnp.int32(0)).start()
    lax.fori_loop(1, per, start_back, 0)
    home_own.start()
    dot_ref[me] = dots[0]

    def later(index, carry):
        def arrive_in(b, carry):
            return arrive(index * per + b, carry)

        def start_in(b, carry):
            return start_back(index * per + b, carry)

        lax.fori_loop(0, per, arrive_in, 0)
        result = process(index)

        @pl.when(index >= 2)
        def _():
            y_copy(index - 2).wait()

        y_rows[lax.rem(index, 2)] = result
        y_copy(index).start()
        lax.fori_loop(0, per, start_in, 0)
        return carry

    lax.fori_loop(1, chunks, later, 0)
    for index in range(max(chunks - 2, 0), chunks):
        y_copy(jnp.int32(index)).wait()

    half = hidden // 2
    count = half // tile

    def columns_of(side, step):
        return pl.ds(pl.multiple_of(side * half + step * tile, tile), tile)

    def up_tile(side, step):
        return dot(rows[...], pre[:, columns_of(side, step)], 0, 0)

    def down_tile(side, step):
        return dot(act[:, columns_of(side, step)], cots[...], 0, 0)

    def up_copy(step):
        slot = lax.rem(step, 2)
        return remote(
            up_ring.at[slot], up_got.at[:, columns_of(0, step)], ring_send.at[slot], up_recv.at[step], (me, 1 - core)
        )

    def down_copy(step):
        slot = lax.rem(step, 2)
        return remote(
            down_ring.at[slot], down_got.at[columns_of(0, step), :], ring_send.at[2 + slot], down_recv.at[step], (me, 1 - core)
        )

    def give(step, carry):
        slot = lax.rem(step, 2)

        @pl.when(step >= 2)
        def _():
            up_copy(step - 2).wait_send()
            down_copy(step - 2).wait_send()

        up_ring[slot] = up_tile(1 - core, step).astype(BF16)
        up_copy(step).start()
        down_ring[slot] = down_tile(1 - core, step).astype(BF16)
        down_copy(step).start()
        return carry

    lax.fori_loop(0, count, give, 0)

    def up_write(step):
        slot = lax.rem(step, 2)
        return pltpu.make_async_copy(up_out.at[slot], up_grad_ref.at[:, columns_of(0, step)], out_sem.at[slot])

    def down_write(step):
        slot = lax.rem(step, 2)
        return pltpu.make_async_copy(down_out.at[slot], down_grad_ref.at[columns_of(0, step), :], out_sem.at[2 + slot])

    def take(step, carry):
        slot = lax.rem(step, 2)

        @pl.when(step >= 2)
        def _():
            up_write(step - 2).wait()
            down_write(step - 2).wait()

        mine = up_tile(core, step)
        up_copy(step).wait_recv()
        up_out[slot] = mine + up_got[:, columns_of(0, step)].astype(F32)
        up_write(step).start()
        mine = down_tile(core, step)
        down_copy(step).wait_recv()
        down_out[slot] = mine + down_got[columns_of(0, step), :].astype(F32)
        down_write(step).start()
        return carry

    lax.fori_loop(0, count, take, 0)

    for step in range(max(count - 2, 0), count):
        up_copy(step).wait_send()
        down_copy(step).wait_send()
        up_write(step).wait()
        down_write(step).wait()
    home_own.wait()

    def finish(step, carry):
        for copy in send_rows(step):
            copy.wait_send()
        for copy in send_back(step):
            copy.wait_send()
        for copy in get_back(step):
            copy.wait_recv()
        return carry

    lax.fori_loop(1, owners, finish, 0)


def experts_of(x_rows, gate_rows, cot_rows, up_matrix, down_matrix, owners):
    slots, width = x_rows.shape
    hidden = up_matrix.shape[1]
    capacity = slots // owners
    chunk, tile, half = min(slots, 512), 256, hidden // 2
    count = half // tile
    shape, vmem, dma = jax.ShapeDtypeStruct, pltpu.VMEM, pltpu.SemaphoreType.DMA
    anywhere = pl.BlockSpec(memory_space=pl.ANY)
    near = pl.BlockSpec(memory_space=pltpu.VMEM)
    return pl.pallas_call(
        functools.partial(expert_kernel, owners),
        out_shape=(
            shape((slots, width), BF16),
            shape((slots, width), BF16),
            shape((owners, 1, capacity), F32),
            shape((width, half), F32),
            shape((half, width), F32),
        ),
        in_specs=[anywhere, near, anywhere, anywhere, anywhere],
        out_specs=(anywhere, anywhere, near, anywhere, anywhere),
        scratch_shapes=[
            vmem((width, hidden), BF16),
            vmem((hidden, width), BF16),
            vmem((slots, width), BF16),
            vmem((slots, width), BF16),
            vmem((slots, hidden), BF16),
            vmem((slots, hidden), BF16),
            vmem((chunk, width), F32),
            vmem((chunk, width), F32),
            vmem((slots, width), BF16),
            vmem((2, chunk, width), BF16),
            vmem((owners, 1, capacity), F32),
            vmem((owners, 1, capacity), F32),
            vmem((2, width, tile), BF16),
            vmem((2, tile, width), BF16),
            vmem((width, half), BF16),
            vmem((half, width), BF16),
            vmem((2, width, tile), F32),
            vmem((2, tile, width), F32),
            dma((2,)),
            dma,
            dma((2,)),
            dma((2,)),
        ]
        + [dma((owners,))] * 8
        + [dma((4,)), dma((count,)), dma((count,)), dma((4,))],
        compiler_params=pltpu.CompilerParams(
            vmem_limit_bytes=67043328, collective_id=1, has_side_effects=True
        ),
        cost_estimate=pl.CostEstimate(
            flops=58 * 10**9, bytes_accessed=4 * 10**7, transcendentals=2 * 10**7
        ),
        name="experts",
    )(x_rows, gate_rows, cot_rows, up_matrix, down_matrix)


def shards(
    block_input,
    cotangent,
    segment_ids,
    routes,
    slot_ids,
    attention_in,
    attention_out,
    router_weight,
    first_gain,
    second_gain,
    bias_table,
    expert_up,
    expert_down,
):
    length, width = block_input.shape
    owners = lax.axis_size("expert")
    capacity = 4 * length // owners
    experts = router_weight.shape[1]
    heads = bias_table.shape[1]
    member = lax.axis_index("dp")
    pair_size = lax.axis_size("dp")
    buckets = pair_size * bias_table.shape[0]
    share = width // pair_size
    inner = owners // 4
    side = math.isqrt(inner)
    digits = (side, inner // side, 4)

    rows = -(-(experts + 2 + heads) // 16) * 16
    wide_part = jnp.concatenate([router_weight.T, first_gain[None], second_gain[None]], axis=0)
    small_part = jnp.zeros((rows, width), BF16)
    small_part = lax.dynamic_update_slice(small_part, wide_part, (0, member * share))
    small_part = lax.dynamic_update_slice(
        small_part, bias_table.T, (experts + 2, member * bias_table.shape[0])
    )
    route_rows = routes.T
    place_rows = route_rows * capacity + slot_ids.T
    (
        hidden_state, normed_two, triple, context, probs, gates,
        x_rows, gate_rows, cot_rows, full_in, full_out, small,
    ) = forward(
        block_input, cotangent, segment_ids, route_rows, place_rows, attention_in, attention_out, small_part,
        owners, experts, buckets, heads,
    )
    y_rows, home_rows, gate_dots, up_share, down_share = experts_of(
        x_rows, gate_rows, cot_rows, expert_up[0], expert_down[0], owners
    )
    block_output, input_grad, in_share, out_share, small_sum = backward(
        (
            block_input, cotangent, hidden_state, normed_two, triple, context, probs, gates, route_rows, place_rows,
            home_rows, gate_dots, full_in, full_out, small,
        ),
        y_rows, owners, experts, buckets, digits,
    )
    mine = lax.dynamic_slice_in_dim(small_sum[: experts + 2], member * share, share, 1)
    bias_grad = lax.dynamic_slice(
        small_sum, (experts + 2, member * bias_table.shape[0]), (heads, bias_table.shape[0])
    )
    return (
        block_output,
        input_grad,
        in_share,
        out_share,
        mine[:experts].T,
        mine[experts],
        mine[experts + 1],
        bias_grad.T,
        up_share[None],
        down_share[None],
    )


def solution(mesh):
    rows = P(("expert", "dp"), None)
    return jax.shard_map(
        shards,
        mesh=mesh,
        in_specs=(
            rows,
            rows,
            rows,
            rows,
            rows,
            P("dp", None),
            P("dp", None),
            P("dp", None),
            P("dp"),
            P("dp"),
            P("dp", None),
            P("expert", None, None),
            P("expert", None, None),
        ),
        out_specs=(
            rows,
            rows,
            P("dp", None),
            P("dp", None),
            P("dp", None),
            P("dp"),
            P("dp"),
            P("dp", None),
            P("expert", None, "dp"),
            P("expert", "dp", None),
        ),
        check_vma=False,
    )
```
